128 devices in a mesh: view: 4 (over x_lo, core), vol: 32 (over x_hi, z, y).
Axes of the slice: x: 4 (x_hi: 2, x_lo: 2; x = x_hi * 2 + x_lo), y: 4, z: 4, core: 2. Of those that a mesh axis runs over, the one named last changes fastest.
Arguments:
- raw_views: bfloat16 [12, 256, 256, 128], P('view', 'vol'), may hold values from 0.18 to 5.41, as said below
- weights: float32 [12, 256, 8], P('view'), may hold values from 0.05 to 1
- offsets: int32 [12, 256], P('view'), may hold values from 0 to 248, as said below
- psf_taps: float32 [12, 3, 9], P('view'), may hold values from 0.01 to 1
Outputs:
- joined_volume: float32 [256, 256, 128], P(None, 'vol')
The draws below stay inside these ranges and needn't reach their ends.
Inputs may be any that keep to these rules, and one draw needn't show every extreme that they name: offsets[v, x] - x + 4 lies in -3 to 4 except where clipped to 0 or 248. `raw_views`: positive intensities.
All inputs are finite; a program needn't handle non-finite values.
Results may differ from the reference program's by a relative error of at most 0.0003.
The reference program's roundings to bfloat16 on the way (of `resampled`) count: a program that leaves them out, or rounds other values in their place, can miss the bound.
Values may be sent and summed in bfloat16 or wider, within the bound.
A program may use at most 64 MiB of HBM per device.

```python
import math
import jax
import jax.numpy as jnp
from jax import lax

VIEWS = 12
BAND = 8
TAPS = 9
ITERS = 2
NY = 128
NZ = 256
NX = 256


def draw_offsets(key, part):
    key_shift, key_jitter = jax.random.split(key)
    offset_shift = jax.random.randint(key_shift, (VIEWS, 1), -2, 4)
    jitter = jax.random.randint(key_jitter, (VIEWS, NX), -1, 2)
    position = jnp.arange(NX, dtype=jnp.int32)[None, :]
    return jnp.clip(position - BAND // 2 + offset_shift + jitter, 0, NX - BAND).astype(jnp.int32)


def draw_raw_views(key, part):
    key_object = jax.random.fold_in(key, 11)
    key_factor = jax.random.fold_in(key, 23)
    common = jnp.exp(jax.random.uniform(key_object, (1, NZ, NX, NY), jnp.float32, jnp.log(0.25), jnp.log(4.0)))
    factor = jnp.exp(jax.random.uniform(key_factor, (VIEWS, NZ, NX, NY), jnp.float32, -0.3, 0.3))
    return (common * factor).astype(jnp.bfloat16)


def levels(own_key, shape, cuts, smallest, top_value):
    def one(axis_at, shards_of):
        draws = jax.random.uniform(jax.random.fold_in(jax.random.fold_in(own_key, 6), axis_at), (shards_of,), jnp.float32, smallest / len(cuts), top_value / len(cuts))
        return jnp.repeat(jnp.exp(draws), shape[axis_at] // shards_of).reshape((-1,) + (1,) * (len(shape) - axis_at - 1))

    level = one(*cuts[0])
    for cut in cuts[1:]:
        level = level * one(*cut)
    return level


def setup_inputs(seed: int = 0) -> dict:
    keys = jax.random.split(jax.random.key(seed), 5)
    raw_views = draw_raw_views(jax.random.fold_in(keys[4], 71), 0)
    weights = jnp.clip(jnp.exp(math.log(1.0) - 2.9957323 * jax.random.uniform(keys[1], (VIEWS, NX, BAND), jnp.float32) ** levels(keys[1], (VIEWS, NX, BAND), ((0, 4),), -0.2, 0.2)), 0.05, 1.0)
    offsets = draw_offsets(jax.random.fold_in(keys[4], 71), 0)
    psf_taps = jnp.clip(jnp.exp(math.log(1.0) - 4.6051702 * jax.random.uniform(keys[3], (VIEWS, 3, TAPS), jnp.float32) ** levels(keys[3], (VIEWS, 3, TAPS), ((0, 4),), -0.2, 0.2)), 0.01, 1.0)
    return dict(raw_views=raw_views, weights=weights, offsets=offsets, psf_taps=psf_taps)


def pad_axis(field, axis, width):
    widths = [(0, 0)] * field.ndim
    widths[axis] = (width, width)
    return jnp.pad(field, widths)


def correlate(extended, taps, axis, length):
    result = taps[0] * lax.slice_in_dim(extended, 0, length, axis=axis)
    for offset in range(1, taps.shape[0]):
        result = result + taps[offset] * lax.slice_in_dim(extended, offset, offset + length, axis=axis)
    return result


def blur_forward(extended, taps, length):
    rim_width = (taps.shape[1] - 1) // 2
    along_x = correlate(extended, taps[1], 1, length)
    along_z = correlate(pad_axis(along_x, 0, rim_width), taps[0], 0, along_x.shape[0])
    return correlate(pad_axis(along_z, 2, rim_width), taps[2], 2, along_z.shape[2])


def blur_back_yz(field, taps):
    rim_width = (taps.shape[1] - 1) // 2
    along_y = correlate(pad_axis(field, 2, rim_width), taps[2][::-1], 2, field.shape[2])
    return correlate(pad_axis(along_y, 0, rim_width), taps[0][::-1], 0, field.shape[0])


def resample_view(planes, weight_rows, first_rows):
    result = jnp.zeros((planes.shape[0], first_rows.shape[0], planes.shape[2]), jnp.float32)
    for offset in range(weight_rows.shape[1]):
        gathered = jnp.take(planes, first_rows + offset, axis=1).astype(jnp.float32)
        result = result + weight_rows[None, :, offset, None] * gathered
    return result.astype(jnp.bfloat16)


def reference(raw_views, weights, offsets, psf_taps):
    weight_norm = weights / jnp.sum(weights, axis=-1, keepdims=True)
    taps_norm = psf_taps / jnp.sum(psf_taps, axis=-1, keepdims=True)
    resampled = lax.map(lambda items: resample_view(items[0], items[1], items[2]), (raw_views, weight_norm, offsets))
    rim_width = (TAPS - 1) // 2

    def add_view(total, view_data):
        return total + view_data.astype(jnp.float32), None

    start_sum, _ = lax.scan(add_view, jnp.zeros(resampled.shape[1:], jnp.float32), resampled)
    joined_volume = start_sum / VIEWS
    width = joined_volume.shape[1]
    for turn in range(ITERS):
        extended = pad_axis(joined_volume, 1, rim_width)

        def one_view(logs, items):
            view_data, taps = items
            blurred = blur_forward(extended, taps, width)
            ratio = view_data.astype(jnp.float32) / blurred
            partial_value = blur_back_yz(ratio, taps)
            back = correlate(pad_axis(partial_value, 1, rim_width), taps[1][::-1], 1, width)
            return logs + jnp.log(back), None

        logs, _ = lax.scan(one_view, jnp.zeros(joined_volume.shape, jnp.float32), (resampled, taps_norm))
        joined_volume = joined_volume * jnp.exp(logs / VIEWS)
    return joined_volume
```

```python
import functools

import jax
import jax.numpy as jnp
from jax import lax
from jax.experimental import pallas as pl
from jax.experimental.pallas import tpu as pltpu
from jax.sharding import PartitionSpec as P

ITERS = 2
CZ = 8


def extended_2(shard, sides, width):
    for axis, dim in sides:
        devices, length = (lax.axis_size(axis), shard.shape[dim])
        up = [(i, (i + 1) % devices) for i in range(devices - 1)]
        down = [(j, i) for i, j in up]
        last = lax.slice_in_dim(shard, length - width, length, axis=dim)
        first = lax.slice_in_dim(shard, 0, width, axis=dim)
        before = lax.ppermute(last, axis, up)
        after = lax.ppermute(first, axis, down)
        shard = jnp.concatenate([before, shard, after], axis=dim)
    return shard


def resample_views(raw_views, weight_norm, offsets):
    rows = raw_views.shape[2]
    band = weight_norm.shape[2]
    target = offsets[:, :, None] + jnp.arange(band, dtype=jnp.int32)[None, None, :]
    onehot = target[..., None] == jnp.arange(rows, dtype=jnp.int32)[None, None, None, :]
    matrix = jnp.sum(jnp.where(onehot, weight_norm[..., None], 0.0), axis=2)
    result = jnp.einsum(
        "vxr,vzry->vzxy",
        matrix,
        raw_views.astype(jnp.float32),
        precision=lax.Precision.HIGHEST,
        preferred_element_type=jnp.float32,
    )
    return result.astype(jnp.bfloat16)


def _lane_weights(taps, ny, reverse):
    lane = lax.broadcasted_iota(jnp.int32, (8, ny), 1)
    out = []
    for t in range(9):
        d = t - 4
        tap = taps[8 - t] if reverse else taps[t]
        valid = (lane + d >= 0) & (lane + d < ny)
        out.append(((-d) % ny, jnp.where(valid, tap, 0.0)))
    return out


def _lane_correlate(f, weights):
    acc = None
    for shift, w in weights:
        rolled = f if shift == 0 else pltpu.roll(f, shift, 2)
        term = rolled * w[None]
        acc = term if acc is None else acc + term
    return acc


def _forward_kernel(taps_ref, est_ref, brick_ref, out_ref, a_ref, c_ref):
    v = pl.program_id(0)
    nz, _, ny = out_ref.shape[1:]
    tx = [taps_ref[v * 27 + 9 + t] for t in range(9)]
    tz = [taps_ref[v * 27 + t] for t in range(9)]
    ty = [taps_ref[v * 27 + 18 + t] for t in range(9)]
    zeros = jnp.zeros((4,) + a_ref.shape[1:], jnp.float32)
    a_ref[0:4] = zeros
    a_ref[nz + 4 : nz + 8] = zeros
    c_ref[0:4] = zeros
    c_ref[nz + 4 : nz + 8] = zeros

    def along_x(c, carry):
        z0 = pl.multiple_of(c * CZ, CZ)
        acc = tx[0] * est_ref[pl.ds(z0, CZ), pl.ds(0, 8), :]
        for t in range(1, 9):
            acc = acc + tx[t] * est_ref[pl.ds(z0, CZ), pl.ds(t, 8), :]
        a_ref[pl.ds(z0 + 4, CZ)] = acc
        return carry

    lax.fori_loop(0, nz // CZ, along_x, 0)
    wy = _lane_weights(ty, ny, False)
    wy_rev = _lane_weights(ty, ny, True)

    def middle(c, carry):
        z0 = pl.multiple_of(c * CZ, CZ)
        acc = tz[0] * a_ref[pl.ds(z0, CZ)]
        for t in range(1, 9):
            acc = acc + tz[t] * a_ref[pl.ds(z0 + t, CZ)]
        blurred = _lane_correlate(acc, wy)
        ratio = brick_ref[0, pl.ds(z0, CZ)].astype(jnp.float32) / blurred
        c_ref[pl.ds(z0 + 4, CZ)] = _lane_correlate(ratio, wy_rev)
        return carry

    lax.fori_loop(0, nz // CZ, middle, 0)

    def along_z_back(c, carry):
        z0 = pl.multiple_of(c * CZ, CZ)
        acc = tz[8] * c_ref[pl.ds(z0, CZ)]
        for t in range(1, 9):
            acc = acc + tz[8 - t] * c_ref[pl.ds(z0 + t, CZ)]
        out_ref[0, pl.ds(z0, CZ)] = acc
        return carry

    lax.fori_loop(0, nz // CZ, along_z_back, 0)


def forward_partials(taps_flat, extended, bricks):
    count, nz, width, ny = bricks.shape
    return pl.pallas_call(
        _forward_kernel,
        grid=(count,),
        in_specs=[
            pl.BlockSpec(memory_space=pltpu.SMEM),
            pl.BlockSpec((nz, width + 8, ny), lambda v: (0, 0, 0)),
            pl.BlockSpec((1, nz, width, ny), lambda v: (v, 0, 0, 0)),
        ],
        out_specs=pl.BlockSpec((1, nz, width, ny), lambda v: (v, 0, 0, 0)),
        out_shape=jax.ShapeDtypeStruct((count, nz, width, ny), jnp.float32),
        scratch_shapes=[
            pltpu.VMEM((nz + 8, width, ny), jnp.float32),
            pltpu.VMEM((nz + 8, width, ny), jnp.float32),
        ],
    )(taps_flat, extended, bricks)


def _back_kernel(taps_ref, wide_ref, out_ref):
    count = wide_ref.shape[0]
    nz = out_ref.shape[0]
    tx = [[taps_ref[v * 27 + 9 + t] for t in range(9)] for v in range(count)]

    def body(c, carry):
        z0 = pl.multiple_of(c * CZ, CZ)
        total = None
        for v in range(count):
            acc = tx[v][8] * wide_ref[v, pl.ds(z0, CZ), pl.ds(0, 8), :]
            for t in range(1, 9):
                acc = acc + tx[v][8 - t] * wide_ref[v, pl.ds(z0, CZ), pl.ds(t, 8), :]
            term = jnp.log(acc)
            total = term if total is None else total + term
        out_ref[pl.ds(z0, CZ)] = total
        return carry

    lax.fori_loop(0, nz // CZ, body, 0)


def back_logs(taps_flat, wide):
    count, nz, width8, ny = wide.shape
    return pl.pallas_call(
        _back_kernel,
        in_specs=[
            pl.BlockSpec(memory_space=pltpu.SMEM),
            pl.BlockSpec(memory_space=pltpu.VMEM),
        ],
        out_specs=pl.BlockSpec(memory_space=pltpu.VMEM),
        out_shape=jax.ShapeDtypeStruct((nz, width8 - 8, ny), jnp.float32),
    )(taps_flat, wide)


def per_device(raw_views, weights, offsets, psf_taps):
    count = raw_views.shape[0]
    total_views = count * lax.axis_size("view")
    rim_width = (psf_taps.shape[2] - 1) // 2
    weight_norm = weights / jnp.sum(weights, axis=-1, keepdims=True)
    taps_norm = psf_taps / jnp.sum(psf_taps, axis=-1, keepdims=True)
    taps_flat = taps_norm.reshape(-1)
    local_views = resample_views(raw_views, weight_norm, offsets)
    bricks = lax.all_to_all(local_views, "vol", split_axis=2, concat_axis=1, tiled=True)
    local_sum = bricks[0].astype(jnp.float32)
    for index in range(1, count):
        local_sum = local_sum + bricks[index].astype(jnp.float32)
    joined_volume = lax.psum(local_sum, "view") / total_views
    for turn in range(ITERS):
        extended = extended_2(joined_volume, (("vol", 1),), rim_width)
        partials = forward_partials(taps_flat, extended, bricks)
        ratio_wide = extended_2(partials, (("vol", 2),), rim_width)
        logs = back_logs(taps_flat, ratio_wide)
        summed = lax.psum(logs, "view")
        joined_volume = joined_volume * jnp.exp(summed / total_views)
    return joined_volume


def solution(mesh):
    placed = (
        P("view", "vol", None, None),
        P("view", None, None),
        P("view", None),
        P("view", None, None),
    )
    return jax.shard_map(
        per_device, mesh=mesh, in_specs=placed, out_specs=P(None, "vol", None), check_vma=False
    )
```

```python
import functools

import jax
import jax.numpy as jnp
from jax import lax
from jax.experimental import pallas as pl
from jax.experimental.pallas import tpu as pltpu
from jax.sharding import PartitionSpec as P

ITERS = 2
CZ = 8


def extended_2(shard, sides, width):
    for axis, dim in sides:
        devices, length = (lax.axis_size(axis), shard.shape[dim])
        up = [(i, (i + 1) % devices) for i in range(devices - 1)]
        down = [(j, i) for i, j in up]
        last = lax.slice_in_dim(shard, length - width, length, axis=dim)
        first = lax.slice_in_dim(shard, 0, width, axis=dim)
        before = lax.ppermute(last, axis, up)
        after = lax.ppermute(first, axis, down)
        shard = jnp.concatenate([before, shard, after], axis=dim)
    return shard


def resample_views(raw_views, weight_norm, offsets):
    rows = raw_views.shape[2]
    band = weight_norm.shape[2]
    target = offsets[:, :, None] + jnp.arange(band, dtype=jnp.int32)[None, None, :]
    onehot = target[..., None] == jnp.arange(rows, dtype=jnp.int32)[None, None, None, :]
    matrix = jnp.sum(jnp.where(onehot, weight_norm[..., None], 0.0), axis=2)
    result = jnp.einsum(
        "vxr,vzry->vzxy",
        matrix,
        raw_views.astype(jnp.float32),
        precision=lax.Precision.HIGHEST,
        preferred_element_type=jnp.float32,
    )
    return result.astype(jnp.bfloat16)


def _lane_weights(taps, ny, reverse):
    lane = lax.broadcasted_iota(jnp.int32, (8, ny), 1)
    out = []
    for t in range(9):
        d = t - 4
        tap = taps[8 - t] if reverse else taps[t]
        valid = (lane + d >= 0) & (lane + d < ny)
        out.append(((-d) % ny, jnp.where(valid, tap, 0.0)))
    return out


def _lane_correlate(f, weights):
    acc = None
    for shift, w in weights:
        rolled = f if shift == 0 else pltpu.roll(f, shift, 2)
        term = rolled * w[None]
        acc = term if acc is None else acc + term
    return acc


def _forward_kernel(v, taps_ref, est_ref, brick_ref, out_ref, a_ref, c_ref):
    nz, _, ny = out_ref.shape
    tx = [taps_ref[v * 27 + 9 + t] for t in range(9)]
    tz = [taps_ref[v * 27 + t] for t in range(9)]
    ty = [taps_ref[v * 27 + 18 + t] for t in range(9)]
    zeros = jnp.zeros((4,) + a_ref.shape[1:], jnp.float32)
    a_ref[0:4] = zeros
    a_ref[nz + 4 : nz + 8] = zeros
    c_ref[0:4] = zeros
    c_ref[nz + 4 : nz + 8] = zeros

    def along_x(c, carry):
        z0 = pl.multiple_of(c * CZ, CZ)
        acc = tx[0] * est_ref[pl.ds(z0, CZ), pl.ds(0, 8), :]
        for t in range(1, 9):
            acc = acc + tx[t] * est_ref[pl.ds(z0, CZ), pl.ds(t, 8), :]
        a_ref[pl.ds(z0 + 4, CZ)] = acc
        return carry

    lax.fori_loop(0, nz // CZ, along_x, 0)
    wy = _lane_weights(ty, ny, False)
    wy_rev = _lane_weights(ty, ny, True)

    def middle(c, carry):
        z0 = pl.multiple_of(c * CZ, CZ)
        acc = tz[0] * a_ref[pl.ds(z0, CZ)]
        for t in range(1, 9):
            acc = acc + tz[t] * a_ref[pl.ds(z0 + t, CZ)]
        blurred = _lane_correlate(acc, wy)
        ratio = brick_ref[pl.ds(z0, CZ)].astype(jnp.float32) / blurred
        c_ref[pl.ds(z0 + 4, CZ)] = _lane_correlate(ratio, wy_rev)
        return carry

    lax.fori_loop(0, nz // CZ, middle, 0)

    def along_z_back(c, carry):
        z0 = pl.multiple_of(c * CZ, CZ)
        acc = tz[8] * c_ref[pl.ds(z0, CZ)]
        for t in range(1, 9):
            acc = acc + tz[8 - t] * c_ref[pl.ds(z0 + t, CZ)]
        out_ref[pl.ds(z0, CZ)] = acc
        return carry

    lax.fori_loop(0, nz // CZ, along_z_back, 0)


def forward_partial(taps_flat, v, extended, brick):
    nz, width, ny = brick.shape
    return pl.pallas_call(
        functools.partial(_forward_kernel, v),
        in_specs=[
            pl.BlockSpec(memory_space=pltpu.SMEM),
            pl.BlockSpec(memory_space=pltpu.VMEM),
            pl.BlockSpec(memory_space=pltpu.VMEM),
        ],
        out_specs=pl.BlockSpec(memory_space=pltpu.VMEM),
        out_shape=jax.ShapeDtypeStruct((nz, width, ny), jnp.float32),
        scratch_shapes=[
            pltpu.VMEM((nz + 8, width, ny), jnp.float32),
            pltpu.VMEM((nz + 8, width, ny), jnp.float32),
        ],
    )(taps_flat, extended, brick)


def _back_kernel(taps_ref, *refs):
    wide_refs, out_ref = refs[:-1], refs[-1]
    count = len(wide_refs)
    nz = out_ref.shape[0]
    tx = [[taps_ref[v * 27 + 9 + t] for t in range(9)] for v in range(count)]

    def body(c, carry):
        z0 = pl.multiple_of(c * CZ, CZ)
        total = None
        for v in range(count):
            acc = tx[v][8] * wide_refs[v][pl.ds(z0, CZ), pl.ds(0, 8), :]
            for t in range(1, 9):
                acc = acc + tx[v][8 - t] * wide_refs[v][pl.ds(z0, CZ), pl.ds(t, 8), :]
            term = jnp.log(acc)
            total = term if total is None else total + term
        out_ref[pl.ds(z0, CZ)] = total
        return carry

    lax.fori_loop(0, nz // CZ, body, 0)


def back_logs(taps_flat, wides):
    nz, width8, ny = wides[0].shape
    return pl.pallas_call(
        _back_kernel,
        in_specs=[pl.BlockSpec(memory_space=pltpu.SMEM)]
        + [pl.BlockSpec(memory_space=pltpu.VMEM)] * len(wides),
        out_specs=pl.BlockSpec(memory_space=pltpu.VMEM),
        out_shape=jax.ShapeDtypeStruct((nz, width8 - 8, ny), jnp.float32),
    )(taps_flat, *wides)


def view_sum(part):
    count = lax.axis_size("view")
    core_swap = [(i, i ^ 1) for i in range(count)]
    chip_swap = [(i, i ^ 2) for i in range(count)]
    half = part.shape[0] // 2
    core = lax.axis_index("view") % 2
    own = lax.dynamic_slice_in_dim(part, core * half, half, axis=0)
    give = lax.dynamic_slice_in_dim(part, (1 - core) * half, half, axis=0)
    own = own + lax.ppermute(give, "view", core_swap)
    own = own + lax.ppermute(own, "view", chip_swap)
    other = lax.ppermute(own, "view", core_swap)
    low = jnp.where(core == 0, own, other)
    high = jnp.where(core == 0, other, own)
    return jnp.concatenate([low, high], axis=0)


def per_device(raw_views, weights, offsets, psf_taps):
    count = raw_views.shape[0]
    total_views = count * lax.axis_size("view")
    rim_width = (psf_taps.shape[2] - 1) // 2
    weight_norm = weights / jnp.sum(weights, axis=-1, keepdims=True)
    taps_norm = psf_taps / jnp.sum(psf_taps, axis=-1, keepdims=True)
    taps_flat = taps_norm.reshape(-1)
    local_views = resample_views(raw_views, weight_norm, offsets)
    bricks = lax.all_to_all(local_views, "vol", split_axis=2, concat_axis=1, tiled=True)
    local_sum = bricks[0].astype(jnp.float32)
    for index in range(1, count):
        local_sum = local_sum + bricks[index].astype(jnp.float32)
    joined_volume = view_sum(local_sum) / total_views
    for turn in range(ITERS):
        extended = extended_2(joined_volume, (("vol", 1),), rim_width)
        wides = []
        for index in range(count):
            partial_value = forward_partial(taps_flat, index, extended, bricks[index])
            wides.append(extended_2(partial_value, (("vol", 1),), rim_width))
        logs = back_logs(taps_flat, wides)
        summed = view_sum(logs)
        joined_volume = joined_volume * jnp.exp(summed / total_views)
    return joined_volume


def solution(mesh):
    placed = (
        P("view", "vol", None, None),
        P("view", None, None),
        P("view", None),
        P("view", None, None),
    )
    return jax.shard_map(
        per_device, mesh=mesh, in_specs=placed, out_specs=P(None, "vol", None), check_vma=False
    )
```

```python
import functools

import jax
import jax.numpy as jnp
from jax import lax
from jax.experimental import pallas as pl
from jax.experimental.pallas import tpu as pltpu
from jax.sharding import PartitionSpec as P

ITERS = 2
CZ = 8


def halos(shard, axis, dim, width):
    devices, length = (lax.axis_size(axis), shard.shape[dim])
    up = [(i, (i + 1) % devices) for i in range(devices - 1)]
    down = [(j, i) for i, j in up]
    last = lax.slice_in_dim(shard, length - width, length, axis=dim)
    first = lax.slice_in_dim(shard, 0, width, axis=dim)
    before = lax.ppermute(last, axis, up)
    after = lax.ppermute(first, axis, down)
    return before, after


def _fill_wide(wide_ref, before_ref, mid_ref, after_ref, z0):
    rim = before_ref.shape[1]
    width = mid_ref.shape[1]
    wide_ref[:, 0:rim, :] = before_ref[pl.ds(z0, CZ)]
    wide_ref[:, rim : rim + width, :] = mid_ref[pl.ds(z0, CZ)]
    wide_ref[:, rim + width :, :] = after_ref[pl.ds(z0, CZ)]


def resample_views(raw_views, weight_norm, offsets):
    rows = raw_views.shape[2]
    band = weight_norm.shape[2]
    target = offsets[:, :, None] + jnp.arange(band, dtype=jnp.int32)[None, None, :]
    onehot = target[..., None] == jnp.arange(rows, dtype=jnp.int32)[None, None, None, :]
    matrix = jnp.sum(jnp.where(onehot, weight_norm[..., None], 0.0), axis=2)
    result = jnp.einsum(
        "vxr,vzry->vzxy",
        matrix,
        raw_views.astype(jnp.float32),
        precision=lax.Precision.HIGHEST,
        preferred_element_type=jnp.float32,
    )
    return result.astype(jnp.bfloat16)


def _lane_weights(taps, ny, reverse):
    lane = lax.broadcasted_iota(jnp.int32, (8, ny), 1)
    out = []
    for t in range(9):
        d = t - 4
        tap = taps[8 - t] if reverse else taps[t]
        valid = (lane + d >= 0) & (lane + d < ny)
        out.append(((-d) % ny, jnp.where(valid, tap, 0.0)))
    return out


def _lane_correlate(f, weights):
    acc = None
    for shift, w in weights:
        rolled = f if shift == 0 else pltpu.roll(f, shift, 2)
        term = rolled * w[None]
        acc = term if acc is None else acc + term
    return acc


def _forward_kernel(v, taps_ref, before_ref, mid_ref, after_ref, brick_ref, out_ref, a_ref, c_ref, est_ref):
    nz, _, ny = out_ref.shape
    tx = [taps_ref[v * 27 + 9 + t] for t in range(9)]
    tz = [taps_ref[v * 27 + t] for t in range(9)]
    ty = [taps_ref[v * 27 + 18 + t] for t in range(9)]
    zeros = jnp.zeros((4,) + a_ref.shape[1:], jnp.float32)
    a_ref[0:4] = zeros
    a_ref[nz + 4 : nz + 8] = zeros
    c_ref[0:4] = zeros
    c_ref[nz + 4 : nz + 8] = zeros

    def along_x(c, carry):
        z0 = pl.multiple_of(c * CZ, CZ)
        _fill_wide(est_ref, before_ref, mid_ref, after_ref, z0)
        acc = tx[0] * est_ref[:, pl.ds(0, 8), :]
        for t in range(1, 9):
            acc = acc + tx[t] * est_ref[:, pl.ds(t, 8), :]
        a_ref[pl.ds(z0 + 4, CZ)] = acc
        return carry

    lax.fori_loop(0, nz // CZ, along_x, 0)
    wy = _lane_weights(ty, ny, False)
    wy_rev = _lane_weights(ty, ny, True)

    def middle(c, carry):
        z0 = pl.multiple_of(c * CZ, CZ)
        acc = tz[0] * a_ref[pl.ds(z0, CZ)]
        for t in range(1, 9):
            acc = acc + tz[t] * a_ref[pl.ds(z0 + t, CZ)]
        blurred = _lane_correlate(acc, wy)
        ratio = brick_ref[pl.ds(z0, CZ)].astype(jnp.float32) / blurred
        c_ref[pl.ds(z0 + 4, CZ)] = _lane_correlate(ratio, wy_rev)
        return carry

    lax.fori_loop(0, nz // CZ, middle, 0)

    def along_z_back(c, carry):
        z0 = pl.multiple_of(c * CZ, CZ)
        acc = tz[8] * c_ref[pl.ds(z0, CZ)]
        for t in range(1, 9):
            acc = acc + tz[8 - t] * c_ref[pl.ds(z0 + t, CZ)]
        out_ref[pl.ds(z0, CZ)] = acc
        return carry

    lax.fori_loop(0, nz // CZ, along_z_back, 0)


def forward_partial(taps_flat, v, before, mid, after, brick):
    nz, width, ny = brick.shape
    return pl.pallas_call(
        functools.partial(_forward_kernel, v),
        in_specs=[pl.BlockSpec(memory_space=pltpu.SMEM)] + [pl.BlockSpec(memory_space=pltpu.VMEM)] * 4,
        out_specs=pl.BlockSpec(memory_space=pltpu.VMEM),
        out_shape=jax.ShapeDtypeStruct((nz, width, ny), jnp.float32),
        scratch_shapes=[
            pltpu.VMEM((nz + 8, width, ny), jnp.float32),
            pltpu.VMEM((nz + 8, width, ny), jnp.float32),
            pltpu.VMEM((CZ, width + 8, ny), jnp.float32),
        ],
    )(taps_flat, before, mid, after, brick)


def _back_kernel(taps_ref, *refs):
    parts, out_ref, wide_ref = refs[:-2], refs[-2], refs[-1]
    count = len(parts) // 3
    nz = out_ref.shape[0]
    tx = [[taps_ref[v * 27 + 9 + t] for t in range(9)] for v in range(count)]

    def body(c, carry):
        z0 = pl.multiple_of(c * CZ, CZ)
        total = None
        for v in range(count):
            _fill_wide(wide_ref, *parts[3 * v : 3 * v + 3], z0)
            acc = tx[v][8] * wide_ref[:, pl.ds(0, 8), :]
            for t in range(1, 9):
                acc = acc + tx[v][8 - t] * wide_ref[:, pl.ds(t, 8), :]
            term = jnp.log(acc)
            total = term if total is None else total + term
        out_ref[pl.ds(z0, CZ)] = total
        return carry

    lax.fori_loop(0, nz // CZ, body, 0)


def back_logs(taps_flat, parts):
    nz, width, ny = parts[1].shape
    return pl.pallas_call(
        _back_kernel,
        in_specs=[pl.BlockSpec(memory_space=pltpu.SMEM)]
        + [pl.BlockSpec(memory_space=pltpu.VMEM)] * len(parts),
        out_specs=pl.BlockSpec(memory_space=pltpu.VMEM),
        out_shape=jax.ShapeDtypeStruct((nz, width, ny), jnp.float32),
        scratch_shapes=[pltpu.VMEM((CZ, width + 8, ny), jnp.float32)],
    )(taps_flat, *parts)


def view_sum(part):
    count = lax.axis_size("view")
    core_swap = [(i, i ^ 1) for i in range(count)]
    chip_swap = [(i, i ^ 2) for i in range(count)]
    half = part.shape[0] // 2
    core = lax.axis_index("view") % 2
    own = lax.dynamic_slice_in_dim(part, core * half, half, axis=0)
    give = lax.dynamic_slice_in_dim(part, (1 - core) * half, half, axis=0)
    own = own + lax.ppermute(give, "view", core_swap)
    own = own + lax.ppermute(own, "view", chip_swap)
    other = lax.ppermute(own, "view", core_swap)
    low = jnp.where(core == 0, own, other)
    high = jnp.where(core == 0, other, own)
    return jnp.concatenate([low, high], axis=0)


def per_device(raw_views, weights, offsets, psf_taps):
    count = raw_views.shape[0]
    total_views = count * lax.axis_size("view")
    rim_width = (psf_taps.shape[2] - 1) // 2
    weight_norm = weights / jnp.sum(weights, axis=-1, keepdims=True)
    taps_norm = psf_taps / jnp.sum(psf_taps, axis=-1, keepdims=True)
    taps_flat = taps_norm.reshape(-1)
    local_views = resample_views(raw_views, weight_norm, offsets)
    bricks = lax.all_to_all(local_views, "vol", split_axis=2, concat_axis=1, tiled=True)
    local_sum = bricks[0].astype(jnp.float32)
    for index in range(1, count):
        local_sum = local_sum + bricks[index].astype(jnp.float32)
    joined_volume = view_sum(local_sum) / total_views
    for turn in range(ITERS):
        before, after = halos(joined_volume, "vol", 1, rim_width)
        parts = []
        for index in range(count):
            partial_value = forward_partial(
                taps_flat, index, before, joined_volume, after, bricks[index]
            )
            low, high = halos(partial_value, "vol", 1, rim_width)
            parts += [low, partial_value, high]
        logs = back_logs(taps_flat, parts)
        summed = view_sum(logs)
        joined_volume = joined_volume * jnp.exp(summed / total_views)
    return joined_volume


def solution(mesh):
    placed = (
        P("view", "vol", None, None),
        P("view", None, None),
        P("view", None),
        P("view", None, None),
    )
    return jax.shard_map(
        per_device, mesh=mesh, in_specs=placed, out_specs=P(None, "vol", None), check_vma=False
    )
```

```python
import functools

import jax
import jax.numpy as jnp
from jax import lax
from jax.experimental import pallas as pl
from jax.experimental.pallas import tpu as pltpu
from jax.sharding import PartitionSpec as P

ITERS = 2
CZ = 8


def halos(shard, axis, dim, width):
    devices, length = (lax.axis_size(axis), shard.shape[dim])
    up = [(i, (i + 1) % devices) for i in range(devices - 1)]
    down = [(j, i) for i, j in up]
    last = lax.slice_in_dim(shard, length - width, length, axis=dim)
    first = lax.slice_in_dim(shard, 0, width, axis=dim)
    before = lax.ppermute(last, axis, up)
    after = lax.ppermute(first, axis, down)
    return before, after


def _fill_wide(wide_ref, before_ref, mid_ref, after_ref, z0):
    rim = before_ref.shape[1]
    width = mid_ref.shape[1]
    wide_ref[:, 0:rim, :] = before_ref[pl.ds(z0, CZ)]
    wide_ref[:, rim : rim + width, :] = mid_ref[pl.ds(z0, CZ)]
    wide_ref[:, rim + width :, :] = after_ref[pl.ds(z0, CZ)]


def resample_views(raw_views, weight_norm, offsets):
    rows = raw_views.shape[2]
    band = weight_norm.shape[2]
    target = offsets[:, :, None] + jnp.arange(band, dtype=jnp.int32)[None, None, :]
    onehot = target[..., None] == jnp.arange(rows, dtype=jnp.int32)[None, None, None, :]
    matrix = jnp.sum(jnp.where(onehot, weight_norm[..., None], 0.0), axis=2)
    result = jnp.einsum(
        "vxr,vzry->vzxy",
        matrix,
        raw_views.astype(jnp.float32),
        precision=lax.Precision.HIGHEST,
        preferred_element_type=jnp.float32,
    )
    return result.astype(jnp.bfloat16)


def _lane_weights(taps, ny, reverse):
    lane = lax.broadcasted_iota(jnp.int32, (8, ny), 1)
    out = []
    for t in range(9):
        d = t - 4
        tap = taps[8 - t] if reverse else taps[t]
        valid = (lane + d >= 0) & (lane + d < ny)
        out.append(((-d) % ny, jnp.where(valid, tap, 0.0)))
    return out


def _lane_correlate(f, weights):
    acc = None
    for shift, w in weights:
        rolled = f if shift == 0 else pltpu.roll(f, shift, 2)
        term = rolled * w[None]
        acc = term if acc is None else acc + term
    return acc


def _forward_kernel(
    v, taps_ref, toeplitz_ref, before_ref, mid_ref, after_ref, brick_ref, out_ref, a_ref, c_ref, est_ref
):
    nz, _, ny = out_ref.shape
    tx = [taps_ref[v * 27 + 9 + t] for t in range(9)]
    tz = [taps_ref[v * 27 + t] for t in range(9)]
    ty = [taps_ref[v * 27 + 18 + t] for t in range(9)]
    zeros = jnp.zeros((4,) + a_ref.shape[1:], jnp.float32)
    a_ref[0:4] = zeros
    a_ref[nz + 4 : nz + 8] = zeros
    c_ref[0:4] = zeros
    c_ref[nz + 4 : nz + 8] = zeros

    def along_x(c, carry):
        z0 = pl.multiple_of(c * CZ, CZ)
        _fill_wide(est_ref, before_ref, mid_ref, after_ref, z0)
        acc = tx[0] * est_ref[:, pl.ds(0, 8), :]
        for t in range(1, 9):
            acc = acc + tx[t] * est_ref[:, pl.ds(t, 8), :]
        a_ref[pl.ds(z0 + 4, CZ)] = acc
        return carry

    lax.fori_loop(0, nz // CZ, along_x, 0)
    forward_y = toeplitz_ref[0]
    back_y = toeplitz_ref[1]

    def along_y(f, matrix):
        flat = f.reshape(CZ * f.shape[1], ny)
        out = jnp.dot(flat, matrix, precision=lax.Precision.HIGHEST, preferred_element_type=jnp.float32)
        return out.reshape(f.shape)

    def middle(c, carry):
        z0 = pl.multiple_of(c * CZ, CZ)
        acc = tz[0] * a_ref[pl.ds(z0, CZ)]
        for t in range(1, 9):
            acc = acc + tz[t] * a_ref[pl.ds(z0 + t, CZ)]
        blurred = along_y(acc, forward_y)
        ratio = brick_ref[pl.ds(z0, CZ)].astype(jnp.float32) / blurred
        c_ref[pl.ds(z0 + 4, CZ)] = along_y(ratio, back_y)
        return carry

    lax.fori_loop(0, nz // CZ, middle, 0)

    def along_z_back(c, carry):
        z0 = pl.multiple_of(c * CZ, CZ)
        acc = tz[8] * c_ref[pl.ds(z0, CZ)]
        for t in range(1, 9):
            acc = acc + tz[8 - t] * c_ref[pl.ds(z0 + t, CZ)]
        out_ref[pl.ds(z0, CZ)] = acc
        return carry

    lax.fori_loop(0, nz // CZ, along_z_back, 0)


def toeplitz_pair(taps_y, ny):
    rows = jnp.arange(ny, dtype=jnp.int32)
    lag = rows[:, None] - rows[None, :] + 4
    inside = (lag >= 0) & (lag <= 8)
    matrix = jnp.where(inside, taps_y[jnp.clip(lag, 0, 8)], 0.0)
    return jnp.stack([matrix, matrix.T])


def forward_partial(taps_flat, v, before, mid, after, brick):
    nz, width, ny = brick.shape
    toeplitz = toeplitz_pair(taps_flat[v * 27 + 18 : v * 27 + 27], ny)
    return pl.pallas_call(
        functools.partial(_forward_kernel, v),
        in_specs=[pl.BlockSpec(memory_space=pltpu.SMEM)] + [pl.BlockSpec(memory_space=pltpu.VMEM)] * 5,
        out_specs=pl.BlockSpec(memory_space=pltpu.VMEM),
        out_shape=jax.ShapeDtypeStruct((nz, width, ny), jnp.float32),
        scratch_shapes=[
            pltpu.VMEM((nz + 8, width, ny), jnp.float32),
            pltpu.VMEM((nz + 8, width, ny), jnp.float32),
            pltpu.VMEM((CZ, width + 8, ny), jnp.float32),
        ],
    )(taps_flat, toeplitz, before, mid, after, brick)


def _back_kernel(taps_ref, *refs):
    parts, out_ref, wide_ref = refs[:-2], refs[-2], refs[-1]
    count = len(parts) // 3
    nz = out_ref.shape[0]
    tx = [[taps_ref[v * 27 + 9 + t] for t in range(9)] for v in range(count)]

    def body(c, carry):
        z0 = pl.multiple_of(c * CZ, CZ)
        total = None
        for v in range(count):
            _fill_wide(wide_ref, *parts[3 * v : 3 * v + 3], z0)
            acc = tx[v][8] * wide_ref[:, pl.ds(0, 8), :]
            for t in range(1, 9):
                acc = acc + tx[v][8 - t] * wide_ref[:, pl.ds(t, 8), :]
            term = jnp.log(acc)
            total = term if total is None else total + term
        out_ref[pl.ds(z0, CZ)] = total
        return carry

    lax.fori_loop(0, nz // CZ, body, 0)


def back_logs(taps_flat, parts):
    nz, width, ny = parts[1].shape
    return pl.pallas_call(
        _back_kernel,
        in_specs=[pl.BlockSpec(memory_space=pltpu.SMEM)]
        + [pl.BlockSpec(memory_space=pltpu.VMEM)] * len(parts),
        out_specs=pl.BlockSpec(memory_space=pltpu.VMEM),
        out_shape=jax.ShapeDtypeStruct((nz, width, ny), jnp.float32),
        scratch_shapes=[pltpu.VMEM((CZ, width + 8, ny), jnp.float32)],
    )(taps_flat, *parts)


def view_sum(part):
    count = lax.axis_size("view")
    core_swap = [(i, i ^ 1) for i in range(count)]
    chip_swap = [(i, i ^ 2) for i in range(count)]
    half = part.shape[0] // 2
    core = lax.axis_index("view") % 2
    own = lax.dynamic_slice_in_dim(part, core * half, half, axis=0)
    give = lax.dynamic_slice_in_dim(part, (1 - core) * half, half, axis=0)
    own = own + lax.ppermute(give, "view", core_swap)
    own = own + lax.ppermute(own, "view", chip_swap)
    other = lax.ppermute(own, "view", core_swap)
    low = jnp.where(core == 0, own, other)
    high = jnp.where(core == 0, other, own)
    return jnp.concatenate([low, high], axis=0)


def per_device(raw_views, weights, offsets, psf_taps):
    count = raw_views.shape[0]
    total_views = count * lax.axis_size("view")
    rim_width = (psf_taps.shape[2] - 1) // 2
    weight_norm = weights / jnp.sum(weights, axis=-1, keepdims=True)
    taps_norm = psf_taps / jnp.sum(psf_taps, axis=-1, keepdims=True)
    taps_flat = taps_norm.reshape(-1)
    local_views = resample_views(raw_views, weight_norm, offsets)
    bricks = lax.all_to_all(local_views, "vol", split_axis=2, concat_axis=1, tiled=True)
    local_sum = bricks[0].astype(jnp.float32)
    for index in range(1, count):
        local_sum = local_sum + bricks[index].astype(jnp.float32)
    joined_volume = view_sum(local_sum) / total_views
    for turn in range(ITERS):
        before, after = halos(joined_volume, "vol", 1, rim_width)
        parts = []
        for index in range(count):
            partial_value = forward_partial(
                taps_flat, index, before, joined_volume, after, bricks[index]
            )
            low, high = halos(partial_value, "vol", 1, rim_width)
            parts += [low, partial_value, high]
        logs = back_logs(taps_flat, parts)
        summed = view_sum(logs)
        joined_volume = joined_volume * jnp.exp(summed / total_views)
    return joined_volume


def solution(mesh):
    placed = (
        P("view", "vol", None, None),
        P("view", None, None),
        P("view", None),
        P("view", None, None),
    )
    return jax.shard_map(
        per_device, mesh=mesh, in_specs=placed, out_specs=P(None, "vol", None), check_vma=False
    )
```

```python
import functools

import jax
import jax.numpy as jnp
from jax import lax
from jax.experimental import pallas as pl
from jax.experimental.pallas import tpu as pltpu
from jax.sharding import PartitionSpec as P

ITERS = 2
CZ = 32


def halos(shard, axis, dim, width):
    length = shard.shape[dim]
    last = lax.slice_in_dim(shard, length - width, length, axis=dim)
    first = lax.slice_in_dim(shard, 0, width, axis=dim)
    return swap_rims(first, last, axis)


def swap_rims(first, last, axis):
    devices = lax.axis_size(axis)
    up = [(i, (i + 1) % devices) for i in range(devices - 1)]
    down = [(j, i) for i, j in up]
    before = lax.ppermute(last, axis, up)
    after = lax.ppermute(first, axis, down)
    return before, after


def _fill_wide(wide_ref, before_ref, mid_ref, after_ref, z0):
    rim = before_ref.shape[1]
    width = mid_ref.shape[1]
    wide_ref[:, 0:rim, :] = before_ref[pl.ds(z0, CZ)]
    wide_ref[:, rim : rim + width, :] = mid_ref[pl.ds(z0, CZ)]
    wide_ref[:, rim + width :, :] = after_ref[pl.ds(z0, CZ)]


def resample_views(raw_views, weight_norm, offsets):
    rows = raw_views.shape[2]
    band = weight_norm.shape[2]
    lag = jnp.arange(rows, dtype=jnp.int32)[None, None, :] - offsets[:, :, None]
    matrix = jnp.zeros(lag.shape, jnp.float32)
    for k in range(band):
        matrix = matrix + jnp.where(lag == k, weight_norm[:, :, k : k + 1], 0.0)
    result = jnp.einsum(
        "vxr,vzry->vzxy",
        matrix,
        raw_views.astype(jnp.float32),
        precision=lax.Precision.HIGHEST,
        preferred_element_type=jnp.float32,
    )
    return result.astype(jnp.bfloat16)


def _lane_weights(taps, ny, reverse):
    lane = lax.broadcasted_iota(jnp.int32, (8, ny), 1)
    out = []
    for t in range(9):
        d = t - 4
        tap = taps[8 - t] if reverse else taps[t]
        valid = (lane + d >= 0) & (lane + d < ny)
        out.append(((-d) % ny, jnp.where(valid, tap, 0.0)))
    return out


def _lane_correlate(f, weights):
    acc = None
    for shift, w in weights:
        rolled = f if shift == 0 else pltpu.roll(f, shift, 2)
        term = rolled * w[None]
        acc = term if acc is None else acc + term
    return acc


def _forward_kernel(
    v, taps_ref, before_ref, mid_ref, after_ref, brick_ref, out_ref, first_ref, last_ref, a_ref, c_ref, est_ref
):
    nz, width, ny = out_ref.shape
    rim = first_ref.shape[1]
    tx = [taps_ref[v * 27 + 9 + t] for t in range(9)]
    tz = [taps_ref[v * 27 + t] for t in range(9)]
    ty = [taps_ref[v * 27 + 18 + t] for t in range(9)]
    zeros = jnp.zeros((4,) + a_ref.shape[1:], jnp.float32)
    a_ref[0:4] = zeros
    a_ref[nz + 4 : nz + 8] = zeros
    c_ref[0:4] = zeros
    c_ref[nz + 4 : nz + 8] = zeros

    def along_x(c, carry):
        z0 = pl.multiple_of(c * CZ, CZ)
        _fill_wide(est_ref, before_ref, mid_ref, after_ref, z0)
        acc = tx[0] * est_ref[:, pl.ds(0, 8), :]
        for t in range(1, 9):
            acc = acc + tx[t] * est_ref[:, pl.ds(t, 8), :]
        a_ref[pl.ds(z0 + 4, CZ)] = acc
        return carry

    lax.fori_loop(0, nz // CZ, along_x, 0)
    wy = _lane_weights(ty, ny, False)
    wy_rev = _lane_weights(ty, ny, True)

    def middle(c, carry):
        z0 = pl.multiple_of(c * CZ, CZ)
        acc = tz[0] * a_ref[pl.ds(z0, CZ)]
        for t in range(1, 9):
            acc = acc + tz[t] * a_ref[pl.ds(z0 + t, CZ)]
        blurred = _lane_correlate(acc, wy)
        ratio = brick_ref[pl.ds(z0, CZ)].astype(jnp.float32) / blurred
        c_ref[pl.ds(z0 + 4, CZ)] = _lane_correlate(ratio, wy_rev)
        return carry

    lax.fori_loop(0, nz // CZ, middle, 0)

    def along_z_back(c, carry):
        z0 = pl.multiple_of(c * CZ, CZ)
        acc = tz[8] * c_ref[pl.ds(z0, CZ)]
        for t in range(1, 9):
            acc = acc + tz[8 - t] * c_ref[pl.ds(z0 + t, CZ)]
        out_ref[pl.ds(z0, CZ)] = acc
        first_ref[pl.ds(z0, CZ)] = acc[:, :rim, :]
        last_ref[pl.ds(z0, CZ)] = acc[:, width - rim :, :]
        return carry

    lax.fori_loop(0, nz // CZ, along_z_back, 0)


def forward_partial(taps_flat, v, before, mid, after, brick):
    nz, width, ny = brick.shape
    return pl.pallas_call(
        functools.partial(_forward_kernel, v),
        in_specs=[pl.BlockSpec(memory_space=pltpu.SMEM)] + [pl.BlockSpec(memory_space=pltpu.VMEM)] * 4,
        out_specs=[pl.BlockSpec(memory_space=pltpu.VMEM)] * 3,
        out_shape=[
            jax.ShapeDtypeStruct((nz, width, ny), jnp.float32),
            jax.ShapeDtypeStruct((nz, 4, ny), jnp.float32),
            jax.ShapeDtypeStruct((nz, 4, ny), jnp.float32),
        ],
        scratch_shapes=[
            pltpu.VMEM((nz + 8, width, ny), jnp.float32),
            pltpu.VMEM((nz + 8, width, ny), jnp.float32),
            pltpu.VMEM((CZ, width + 8, ny), jnp.float32),
        ],
    )(taps_flat, before, mid, after, brick)


def _back_kernel(taps_ref, *refs):
    parts, out_ref, wide_ref = refs[:-2], refs[-2], refs[-1]
    count = len(parts) // 3
    nz = out_ref.shape[0]
    tx = [[taps_ref[v * 27 + 9 + t] for t in range(9)] for v in range(count)]

    def body(c, carry):
        z0 = pl.multiple_of(c * CZ, CZ)
        total = None
        for v in range(count):
            _fill_wide(wide_ref, *parts[3 * v : 3 * v + 3], z0)
            acc = tx[v][8] * wide_ref[:, pl.ds(0, 8), :]
            for t in range(1, 9):
                acc = acc + tx[v][8 - t] * wide_ref[:, pl.ds(t, 8), :]
            term = jnp.log(acc)
            total = term if total is None else total + term
        out_ref[pl.ds(z0, CZ)] = total
        return carry

    lax.fori_loop(0, nz // CZ, body, 0)


def back_logs(taps_flat, parts):
    nz, width, ny = parts[1].shape
    return pl.pallas_call(
        _back_kernel,
        in_specs=[pl.BlockSpec(memory_space=pltpu.SMEM)]
        + [pl.BlockSpec(memory_space=pltpu.VMEM)] * len(parts),
        out_specs=pl.BlockSpec(memory_space=pltpu.VMEM),
        out_shape=jax.ShapeDtypeStruct((nz, width, ny), jnp.float32),
        scratch_shapes=[pltpu.VMEM((CZ, width + 8, ny), jnp.float32)],
    )(taps_flat, *parts)


def view_sum(part):
    count = lax.axis_size("view")
    core_swap = [(i, i ^ 1) for i in range(count)]
    chip_swap = [(i, i ^ 2) for i in range(count)]
    half = part.shape[0] // 2
    core = lax.axis_index("view") % 2
    own = lax.dynamic_slice_in_dim(part, core * half, half, axis=0)
    give = lax.dynamic_slice_in_dim(part, (1 - core) * half, half, axis=0)
    own = own + lax.ppermute(give, "view", core_swap)
    own = own + lax.ppermute(own, "view", chip_swap)
    other = lax.ppermute(own, "view", core_swap)
    low = jnp.where(core == 0, own, other)
    high = jnp.where(core == 0, other, own)
    return jnp.concatenate([low, high], axis=0)


def per_device(raw_views, weights, offsets, psf_taps):
    count = raw_views.shape[0]
    total_views = count * lax.axis_size("view")
    rim_width = (psf_taps.shape[2] - 1) // 2
    weight_norm = weights / jnp.sum(weights, axis=-1, keepdims=True)
    taps_norm = psf_taps / jnp.sum(psf_taps, axis=-1, keepdims=True)
    taps_flat = taps_norm.reshape(-1)
    local_views = resample_views(raw_views, weight_norm, offsets)
    bricks = lax.all_to_all(local_views, "vol", split_axis=2, concat_axis=1, tiled=True)
    local_sum = bricks[0].astype(jnp.float32)
    for index in range(1, count):
        local_sum = local_sum + bricks[index].astype(jnp.float32)
    joined_volume = view_sum(local_sum) / total_views
    for turn in range(ITERS):
        before, after = halos(joined_volume, "vol", 1, rim_width)
        parts = []
        for index in range(count):
            partial_value, first, last = forward_partial(
                taps_flat, index, before, joined_volume, after, bricks[index]
            )
            low, high = swap_rims(first, last, "vol")
            parts += [low, partial_value, high]
        logs = back_logs(taps_flat, parts)
        summed = view_sum(logs)
        joined_volume = joined_volume * jnp.exp(summed / total_views)
    return joined_volume


def solution(mesh):
    placed = (
        P("view", "vol", None, None),
        P("view", None, None),
        P("view", None),
        P("view", None, None),
    )
    return jax.shard_map(
        per_device, mesh=mesh, in_specs=placed, out_specs=P(None, "vol", None), check_vma=False
    )
```

```python
import functools

import jax
import jax.numpy as jnp
from jax import lax
from jax.experimental import pallas as pl
from jax.experimental.pallas import tpu as pltpu
from jax.sharding import PartitionSpec as P

ITERS = 2
CZ = 32


def halos(shard, axis, dim, width):
    length = shard.shape[dim]
    last = lax.slice_in_dim(shard, length - width, length, axis=dim)
    first = lax.slice_in_dim(shard, 0, width, axis=dim)
    return swap_rims(first, last, axis)


def swap_rims(first, last, axis):
    devices = lax.axis_size(axis)
    up = [(i, (i + 1) % devices) for i in range(devices - 1)]
    down = [(j, i) for i, j in up]
    before = lax.ppermute(last, axis, up)
    after = lax.ppermute(first, axis, down)
    return before, after


def _fill_wide(wide_ref, before_ref, mid_ref, after_ref, z0):
    rim = before_ref.shape[1]
    width = mid_ref.shape[1]
    wide_ref[:, 0:rim, :] = before_ref[pl.ds(z0, CZ)]
    wide_ref[:, rim : rim + width, :] = mid_ref[pl.ds(z0, CZ)]
    wide_ref[:, rim + width :, :] = after_ref[pl.ds(z0, CZ)]


def resample_views(raw_views, weight_norm, offsets):
    rows = raw_views.shape[2]
    band = weight_norm.shape[2]
    lag = jnp.arange(rows, dtype=jnp.int32)[None, None, :] - offsets[:, :, None]
    matrix = jnp.zeros(lag.shape, jnp.float32)
    for k in range(band):
        matrix = matrix + jnp.where(lag == k, weight_norm[:, :, k : k + 1], 0.0)
    result = jnp.einsum(
        "vxr,vzry->vzxy",
        matrix,
        raw_views.astype(jnp.float32),
        precision=lax.Precision.HIGHEST,
        preferred_element_type=jnp.float32,
    )
    return result.astype(jnp.bfloat16)


def _lane_weights(taps, ny, reverse):
    lane = lax.broadcasted_iota(jnp.int32, (8, ny), 1)
    out = []
    for t in range(9):
        d = t - 4
        tap = taps[8 - t] if reverse else taps[t]
        valid = (lane + d >= 0) & (lane + d < ny)
        out.append(((-d) % ny, jnp.where(valid, tap, 0.0)))
    return out


def _lane_correlate(f, weights):
    acc = None
    for shift, w in weights:
        rolled = f if shift == 0 else pltpu.roll(f, shift, 2)
        term = rolled * w[None]
        acc = term if acc is None else acc + term
    return acc


def _forward_kernel(
    v, taps_ref, before_ref, mid_ref, after_ref, brick_ref, out_ref, first_ref, last_ref, a_ref, c_ref, est_ref
):
    nz, width, ny = out_ref.shape
    rim = first_ref.shape[1]
    tx = [taps_ref[v * 27 + 9 + t] for t in range(9)]
    tz = [taps_ref[v * 27 + t] for t in range(9)]
    ty = [taps_ref[v * 27 + 18 + t] for t in range(9)]
    zeros = jnp.zeros((4,) + a_ref.shape[1:], jnp.float32)
    a_ref[0:4] = zeros
    a_ref[nz + 4 : nz + 8] = zeros
    c_ref[0:4] = zeros
    c_ref[nz + 4 : nz + 8] = zeros

    def along_x(c, carry):
        z0 = pl.multiple_of(c * CZ, CZ)
        _fill_wide(est_ref, before_ref, mid_ref, after_ref, z0)
        acc = tx[0] * est_ref[:, pl.ds(0, 8), :]
        for t in range(1, 9):
            acc = acc + tx[t] * est_ref[:, pl.ds(t, 8), :]
        a_ref[pl.ds(z0 + 4, CZ)] = acc
        return carry

    lax.fori_loop(0, nz // CZ, along_x, 0)
    wy = _lane_weights(ty, ny, False)
    wy_rev = _lane_weights(ty, ny, True)

    def middle(c, carry):
        z0 = pl.multiple_of(c * CZ, CZ)
        acc = tz[0] * a_ref[pl.ds(z0, CZ)]
        for t in range(1, 9):
            acc = acc + tz[t] * a_ref[pl.ds(z0 + t, CZ)]
        blurred = _lane_correlate(acc, wy)
        ratio = brick_ref[pl.ds(z0, CZ)].astype(jnp.float32) / blurred
        c_ref[pl.ds(z0 + 4, CZ)] = _lane_correlate(ratio, wy_rev)
        return carry

    lax.fori_loop(0, nz // CZ, middle, 0)

    def along_z_back(c, carry):
        z0 = pl.multiple_of(c * CZ, CZ)
        acc = tz[8] * c_ref[pl.ds(z0, CZ)]
        for t in range(1, 9):
            acc = acc + tz[8 - t] * c_ref[pl.ds(z0 + t, CZ)]
        out_ref[pl.ds(z0, CZ)] = acc
        first_ref[pl.ds(z0, CZ)] = acc[:, :rim, :]
        last_ref[pl.ds(z0, CZ)] = acc[:, width - rim :, :]
        return carry

    lax.fori_loop(0, nz // CZ, along_z_back, 0)


def forward_partial(taps_flat, v, before, mid, after, brick):
    nz, width, ny = brick.shape
    return pl.pallas_call(
        functools.partial(_forward_kernel, v),
        in_specs=[pl.BlockSpec(memory_space=pltpu.SMEM)] + [pl.BlockSpec(memory_space=pltpu.VMEM)] * 4,
        out_specs=[pl.BlockSpec(memory_space=pltpu.VMEM)] * 3,
        out_shape=[
            jax.ShapeDtypeStruct((nz, width, ny), jnp.float32),
            jax.ShapeDtypeStruct((nz, 4, ny), jnp.float32),
            jax.ShapeDtypeStruct((nz, 4, ny), jnp.float32),
        ],
        scratch_shapes=[
            pltpu.VMEM((nz + 8, width, ny), jnp.float32),
            pltpu.VMEM((nz + 8, width, ny), jnp.float32),
            pltpu.VMEM((CZ, width + 8, ny), jnp.float32),
        ],
    )(taps_flat, before, mid, after, brick)


def _back_kernel(taps_ref, *refs):
    parts, out_ref, wide_ref = refs[:-2], refs[-2], refs[-1]
    count = len(parts) // 3
    nz = out_ref.shape[0]
    tx = [[taps_ref[v * 27 + 9 + t] for t in range(9)] for v in range(count)]

    def body(c, carry):
        z0 = pl.multiple_of(c * CZ, CZ)
        total = None
        for v in range(count):
            _fill_wide(wide_ref, *parts[3 * v : 3 * v + 3], z0)
            acc = tx[v][8] * wide_ref[:, pl.ds(0, 8), :]
            for t in range(1, 9):
                acc = acc + tx[v][8 - t] * wide_ref[:, pl.ds(t, 8), :]
            term = jnp.log(acc)
            total = term if total is None else total + term
        out_ref[pl.ds(z0, CZ)] = total
        return carry

    lax.fori_loop(0, nz // CZ, body, 0)


def back_logs(taps_flat, parts):
    nz, width, ny = parts[1].shape
    return pl.pallas_call(
        _back_kernel,
        in_specs=[pl.BlockSpec(memory_space=pltpu.SMEM)]
        + [pl.BlockSpec(memory_space=pltpu.VMEM)] * len(parts),
        out_specs=pl.BlockSpec(memory_space=pltpu.VMEM),
        out_shape=jax.ShapeDtypeStruct((nz, width, ny), jnp.float32),
        scratch_shapes=[pltpu.VMEM((CZ, width + 8, ny), jnp.float32)],
    )(taps_flat, *parts)


def _pack(acc, first_ref, last_ref, p0):
    half = acc.shape[0] // 2
    upper, lower = acc[:half], acc[half:]
    row = lax.broadcasted_iota(jnp.int32, upper.shape, 1)
    first_ref[pl.ds(p0, half)] = jnp.where(row < 4, upper, pltpu.roll(lower, 4, 1))
    last_ref[pl.ds(p0, half)] = jnp.where(row < 4, pltpu.roll(upper, 4, 1), lower)


def _unpack(packed_ref, p0):
    packed = packed_ref[pl.ds(p0, CZ // 2)]
    return jnp.concatenate([packed, pltpu.roll(packed, 4, 1)], axis=0)


def _iteration_kernel(
    taps_ref, before_ref, mid_ref, after_ref, brick_ref, logs_ref,
    a_ref, c_ref, ext_ref, part_ref, send_ref, recv_ref, send_sem, recv_sem,
):
    count, nz, width, ny = part_ref.shape
    me = lax.axis_index("vol")
    view = lax.axis_index("view")
    has_lo = me > 0
    has_hi = me < lax.axis_size("vol") - 1
    barrier = pltpu.get_barrier_semaphore()

    @pl.when(has_lo)
    def _():
        pl.semaphore_signal(barrier, inc=1, device_id=(view, me - 1), device_id_type=pl.DeviceIdType.MESH)

    @pl.when(has_hi)
    def _():
        pl.semaphore_signal(barrier, inc=1, device_id=(view, me + 1), device_id_type=pl.DeviceIdType.MESH)

    pl.semaphore_wait(barrier, has_lo.astype(jnp.int32) + has_hi.astype(jnp.int32))

    @pl.when(jnp.logical_not(has_lo))
    def _():
        recv_ref[:, 0] = jnp.zeros(recv_ref.shape[:1] + recv_ref.shape[2:], jnp.float32)

    @pl.when(jnp.logical_not(has_hi))
    def _():
        recv_ref[:, 1] = jnp.zeros(recv_ref.shape[:1] + recv_ref.shape[2:], jnp.float32)

    def copies(v):
        up = pltpu.make_async_remote_copy(
            src_ref=send_ref.at[v, 1], dst_ref=recv_ref.at[v, 0],
            send_sem=send_sem.at[v, 1], recv_sem=recv_sem.at[v, 0],
            device_id=(view, me + 1), device_id_type=pl.DeviceIdType.MESH,
        )
        down = pltpu.make_async_remote_copy(
            src_ref=send_ref.at[v, 0], dst_ref=recv_ref.at[v, 1],
            send_sem=send_sem.at[v, 0], recv_sem=recv_sem.at[v, 1],
            device_id=(view, me - 1), device_id_type=pl.DeviceIdType.MESH,
        )
        return up, down

    zeros = jnp.zeros((4, width, ny), jnp.float32)
    a_ref[0:4] = zeros
    a_ref[nz + 4 : nz + 8] = zeros
    c_ref[0:4] = zeros
    c_ref[nz + 4 : nz + 8] = zeros
    for v in range(count):
        tx = [taps_ref[v * 27 + 9 + t] for t in range(9)]
        tz = [taps_ref[v * 27 + t] for t in range(9)]
        ty = [taps_ref[v * 27 + 18 + t] for t in range(9)]

        def along_x(c, carry):
            z0 = pl.multiple_of(c * CZ, CZ)
            _fill_wide(ext_ref, before_ref, mid_ref, after_ref, z0)
            acc = tx[0] * ext_ref[:, pl.ds(0, 8), :]
            for t in range(1, 9):
                acc = acc + tx[t] * ext_ref[:, pl.ds(t, 8), :]
            a_ref[pl.ds(z0 + 4, CZ)] = acc
            return carry

        lax.fori_loop(0, nz // CZ, along_x, 0)
        wy = _lane_weights(ty, ny, False)
        wy_rev = _lane_weights(ty, ny, True)

        def middle(c, carry):
            z0 = pl.multiple_of(c * CZ, CZ)
            acc = tz[0] * a_ref[pl.ds(z0, CZ)]
            for t in range(1, 9):
                acc = acc + tz[t] * a_ref[pl.ds(z0 + t, CZ)]
            blurred = _lane_correlate(acc, wy)
            ratio = brick_ref[v, pl.ds(z0, CZ)].astype(jnp.float32) / blurred
            c_ref[pl.ds(z0 + 4, CZ)] = _lane_correlate(ratio, wy_rev)
            return carry

        lax.fori_loop(0, nz // CZ, middle, 0)

        def along_z_back(c, carry):
            z0 = pl.multiple_of(c * CZ, CZ)
            acc = tz[8] * c_ref[pl.ds(z0, CZ)]
            for t in range(1, 9):
                acc = acc + tz[8 - t] * c_ref[pl.ds(z0 + t, CZ)]
            part_ref[v, pl.ds(z0, CZ)] = acc
            _pack(acc, send_ref.at[v, 0], send_ref.at[v, 1], pl.multiple_of(c * (CZ // 2), CZ // 2))
            return carry

        lax.fori_loop(0, nz // CZ, along_z_back, 0)
        up, down = copies(v)

        @pl.when(has_hi)
        def _():
            up.start()

        @pl.when(has_lo)
        def _():
            down.start()

    for v in range(count):
        up, down = copies(v)

        @pl.when(has_hi)
        def _():
            up.wait_send()
            down.wait_recv()

        @pl.when(has_lo)
        def _():
            down.wait_send()
            up.wait_recv()

    tb = [[taps_ref[v * 27 + 9 + t] for t in range(9)] for v in range(count)]

    def back(c, carry):
        z0 = pl.multiple_of(c * CZ, CZ)
        p0 = pl.multiple_of(c * (CZ // 2), CZ // 2)
        total = None
        for v in range(count):
            ext_ref[:, 0:4, :] = _unpack(recv_ref.at[v, 0], p0)[:, 0:4, :]
            ext_ref[:, 4 : 4 + width, :] = part_ref[v, pl.ds(z0, CZ)]
            ext_ref[:, 4 + width :, :] = _unpack(recv_ref.at[v, 1], p0)[:, 0:4, :]
            acc = tb[v][8] * ext_ref[:, pl.ds(0, 8), :]
            for t in range(1, 9):
                acc = acc + tb[v][8 - t] * ext_ref[:, pl.ds(t, 8), :]
            term = jnp.log(acc)
            total = term if total is None else total + term
        logs_ref[pl.ds(z0, CZ)] = total
        return carry

    lax.fori_loop(0, nz // CZ, back, 0)


def iteration_logs(taps_flat, before, mid, after, bricks):
    count, nz, width, ny = bricks.shape
    return pl.pallas_call(
        _iteration_kernel,
        in_specs=[pl.BlockSpec(memory_space=pltpu.SMEM)] + [pl.BlockSpec(memory_space=pltpu.VMEM)] * 4,
        out_specs=pl.BlockSpec(memory_space=pltpu.VMEM),
        out_shape=jax.ShapeDtypeStruct((nz, width, ny), jnp.float32),
        scratch_shapes=[
            pltpu.VMEM((nz + 8, width, ny), jnp.float32),
            pltpu.VMEM((nz + 8, width, ny), jnp.float32),
            pltpu.VMEM((CZ, width + 8, ny), jnp.float32),
            pltpu.VMEM((count, nz, width, ny), jnp.float32),
            pltpu.VMEM((count, 2, nz // 2, width, ny), jnp.float32),
            pltpu.VMEM((count, 2, nz // 2, width, ny), jnp.float32),
            pltpu.SemaphoreType.DMA((count, 2)),
            pltpu.SemaphoreType.DMA((count, 2)),
        ],
        compiler_params=pltpu.CompilerParams(
            collective_id=0, has_side_effects=True, vmem_limit_bytes=48 * 1024 * 1024
        ),
    )(taps_flat, before, mid, after, bricks)


def view_sum(part):
    count = lax.axis_size("view")
    core_swap = [(i, i ^ 1) for i in range(count)]
    chip_swap = [(i, i ^ 2) for i in range(count)]
    half = part.shape[0] // 2
    core = lax.axis_index("view") % 2
    own = lax.dynamic_slice_in_dim(part, core * half, half, axis=0)
    give = lax.dynamic_slice_in_dim(part, (1 - core) * half, half, axis=0)
    own = own + lax.ppermute(give, "view", core_swap)
    own = own + lax.ppermute(own, "view", chip_swap)
    other = lax.ppermute(own, "view", core_swap)
    low = jnp.where(core == 0, own, other)
    high = jnp.where(core == 0, other, own)
    return jnp.concatenate([low, high], axis=0)


def per_device(raw_views, weights, offsets, psf_taps):
    count = raw_views.shape[0]
    total_views = count * lax.axis_size("view")
    rim_width = (psf_taps.shape[2] - 1) // 2
    weight_norm = weights / jnp.sum(weights, axis=-1, keepdims=True)
    taps_norm = psf_taps / jnp.sum(psf_taps, axis=-1, keepdims=True)
    taps_flat = taps_norm.reshape(-1)
    local_views = resample_views(raw_views, weight_norm, offsets)
    bricks = lax.all_to_all(local_views, "vol", split_axis=2, concat_axis=1, tiled=True)
    local_sum = bricks[0].astype(jnp.float32)
    for index in range(1, count):
        local_sum = local_sum + bricks[index].astype(jnp.float32)
    joined_volume = view_sum(local_sum) / total_views
    for turn in range(ITERS):
        before, after = halos(joined_volume, "vol", 1, rim_width)
        logs = iteration_logs(taps_flat, before, joined_volume, after, bricks)
        summed = view_sum(logs)
        joined_volume = joined_volume * jnp.exp(summed / total_views)
    return joined_volume


def solution(mesh):
    placed = (
        P("view", "vol", None, None),
        P("view", None, None),
        P("view", None),
        P("view", None, None),
    )
    return jax.shard_map(
        per_device, mesh=mesh, in_specs=placed, out_specs=P(None, "vol", None), check_vma=False
    )
```

```python
import functools

import jax
import jax.numpy as jnp
from jax import lax
from jax.experimental import pallas as pl
from jax.experimental.pallas import tpu as pltpu
from jax.sharding import PartitionSpec as P

ITERS = 2
CZ = 32


def halos(shard, axis, dim, width):
    length = shard.shape[dim]
    last = lax.slice_in_dim(shard, length - width, length, axis=dim)
    first = lax.slice_in_dim(shard, 0, width, axis=dim)
    return swap_rims(first, last, axis)


def swap_rims(first, last, axis):
    devices = lax.axis_size(axis)
    up = [(i, (i + 1) % devices) for i in range(devices - 1)]
    down = [(j, i) for i, j in up]
    before = lax.ppermute(last, axis, up)
    after = lax.ppermute(first, axis, down)
    return before, after


def _fill_wide(wide_ref, before_ref, mid_ref, after_ref, z0):
    rim = before_ref.shape[1]
    width = mid_ref.shape[1]
    wide_ref[:, 0:rim, :] = before_ref[pl.ds(z0, CZ)]
    wide_ref[:, rim : rim + width, :] = mid_ref[pl.ds(z0, CZ)]
    wide_ref[:, rim + width :, :] = after_ref[pl.ds(z0, CZ)]


def resample_views(raw_views, weight_norm, offsets):
    rows = raw_views.shape[2]
    band = weight_norm.shape[2]
    lag = jnp.arange(rows, dtype=jnp.int32)[None, None, :] - offsets[:, :, None]
    matrix = jnp.zeros(lag.shape, jnp.float32)
    for k in range(band):
        matrix = matrix + jnp.where(lag == k, weight_norm[:, :, k : k + 1], 0.0)
    result = jnp.einsum(
        "vxr,vzry->vzxy",
        matrix,
        raw_views.astype(jnp.float32),
        precision=lax.Precision.HIGHEST,
        preferred_element_type=jnp.float32,
    )
    return result.astype(jnp.bfloat16)


def _lane_weights(taps, ny, reverse):
    lane = lax.broadcasted_iota(jnp.int32, (8, ny), 1)
    out = []
    for t in range(9):
        d = t - 4
        tap = taps[8 - t] if reverse else taps[t]
        valid = (lane + d >= 0) & (lane + d < ny)
        out.append(((-d) % ny, jnp.where(valid, tap, 0.0)))
    return out


def _lane_correlate(f, weights):
    acc = None
    for shift, w in weights:
        rolled = f if shift == 0 else pltpu.roll(f, shift, 2)
        term = rolled * w[None]
        acc = term if acc is None else acc + term
    return acc


def _forward_kernel(
    v, taps_ref, before_ref, mid_ref, after_ref, brick_ref, out_ref, first_ref, last_ref, a_ref, c_ref, est_ref
):
    nz, width, ny = out_ref.shape
    rim = first_ref.shape[1]
    tx = [taps_ref[v * 27 + 9 + t] for t in range(9)]
    tz = [taps_ref[v * 27 + t] for t in range(9)]
    ty = [taps_ref[v * 27 + 18 + t] for t in range(9)]
    zeros = jnp.zeros((4,) + a_ref.shape[1:], jnp.float32)
    a_ref[0:4] = zeros
    a_ref[nz + 4 : nz + 8] = zeros
    c_ref[0:4] = zeros
    c_ref[nz + 4 : nz + 8] = zeros

    def along_x(c, carry):
        z0 = pl.multiple_of(c * CZ, CZ)
        _fill_wide(est_ref, before_ref, mid_ref, after_ref, z0)
        acc = tx[0] * est_ref[:, pl.ds(0, 8), :]
        for t in range(1, 9):
            acc = acc + tx[t] * est_ref[:, pl.ds(t, 8), :]
        a_ref[pl.ds(z0 + 4, CZ)] = acc
        return carry

    lax.fori_loop(0, nz // CZ, along_x, 0)
    wy = _lane_weights(ty, ny, False)
    wy_rev = _lane_weights(ty, ny, True)

    def middle(c, carry):
        z0 = pl.multiple_of(c * CZ, CZ)
        acc = tz[0] * a_ref[pl.ds(z0, CZ)]
        for t in range(1, 9):
            acc = acc + tz[t] * a_ref[pl.ds(z0 + t, CZ)]
        blurred = _lane_correlate(acc, wy)
        ratio = brick_ref[pl.ds(z0, CZ)].astype(jnp.float32) / blurred
        c_ref[pl.ds(z0 + 4, CZ)] = _lane_correlate(ratio, wy_rev)
        return carry

    lax.fori_loop(0, nz // CZ, middle, 0)

    def along_z_back(c, carry):
        z0 = pl.multiple_of(c * CZ, CZ)
        acc = tz[8] * c_ref[pl.ds(z0, CZ)]
        for t in range(1, 9):
            acc = acc + tz[8 - t] * c_ref[pl.ds(z0 + t, CZ)]
        out_ref[pl.ds(z0, CZ)] = acc
        first_ref[pl.ds(z0, CZ)] = acc[:, :rim, :]
        last_ref[pl.ds(z0, CZ)] = acc[:, width - rim :, :]
        return carry

    lax.fori_loop(0, nz // CZ, along_z_back, 0)


def forward_partial(taps_flat, v, before, mid, after, brick):
    nz, width, ny = brick.shape
    return pl.pallas_call(
        functools.partial(_forward_kernel, v),
        in_specs=[pl.BlockSpec(memory_space=pltpu.SMEM)] + [pl.BlockSpec(memory_space=pltpu.VMEM)] * 4,
        out_specs=[pl.BlockSpec(memory_space=pltpu.VMEM)] * 3,
        out_shape=[
            jax.ShapeDtypeStruct((nz, width, ny), jnp.float32),
            jax.ShapeDtypeStruct((nz, 4, ny), jnp.float32),
            jax.ShapeDtypeStruct((nz, 4, ny), jnp.float32),
        ],
        scratch_shapes=[
            pltpu.VMEM((nz + 8, width, ny), jnp.float32),
            pltpu.VMEM((nz + 8, width, ny), jnp.float32),
            pltpu.VMEM((CZ, width + 8, ny), jnp.float32),
        ],
    )(taps_flat, before, mid, after, brick)


def _back_kernel(taps_ref, *refs):
    parts, out_ref, wide_ref = refs[:-2], refs[-2], refs[-1]
    count = len(parts) // 3
    nz = out_ref.shape[0]
    tx = [[taps_ref[v * 27 + 9 + t] for t in range(9)] for v in range(count)]

    def body(c, carry):
        z0 = pl.multiple_of(c * CZ, CZ)
        total = None
        for v in range(count):
            _fill_wide(wide_ref, *parts[3 * v : 3 * v + 3], z0)
            acc = tx[v][8] * wide_ref[:, pl.ds(0, 8), :]
            for t in range(1, 9):
                acc = acc + tx[v][8 - t] * wide_ref[:, pl.ds(t, 8), :]
            term = jnp.log(acc)
            total = term if total is None else total + term
        out_ref[pl.ds(z0, CZ)] = total
        return carry

    lax.fori_loop(0, nz // CZ, body, 0)


def back_logs(taps_flat, parts):
    nz, width, ny = parts[1].shape
    return pl.pallas_call(
        _back_kernel,
        in_specs=[pl.BlockSpec(memory_space=pltpu.SMEM)]
        + [pl.BlockSpec(memory_space=pltpu.VMEM)] * len(parts),
        out_specs=pl.BlockSpec(memory_space=pltpu.VMEM),
        out_shape=jax.ShapeDtypeStruct((nz, width, ny), jnp.float32),
        scratch_shapes=[pltpu.VMEM((CZ, width + 8, ny), jnp.float32)],
    )(taps_flat, *parts)


def _pack(acc, first_ref, last_ref, p0):
    half = acc.shape[0] // 2
    upper, lower = acc[:half], acc[half:]
    row = lax.broadcasted_iota(jnp.int32, upper.shape, 1)
    first_ref[pl.ds(p0, half)] = jnp.where(row < 4, upper, pltpu.roll(lower, 4, 1))
    last_ref[pl.ds(p0, half)] = jnp.where(row < 4, pltpu.roll(upper, 4, 1), lower)


def _unpack(packed_ref, p0):
    packed = packed_ref[pl.ds(p0, CZ // 2)]
    return jnp.concatenate([packed, pltpu.roll(packed, 4, 1)], axis=0)


def _iteration_kernel(
    taps_ref, before_ref, mid_ref, after_ref, brick_ref, logs_ref,
    a_ref, c_ref, ext_ref, part_ref, send_ref, recv_ref, send_sem, recv_sem,
):
    count, nz, width, ny = part_ref.shape
    me = lax.axis_index("vol")
    view = lax.axis_index("view")
    has_lo = me > 0
    has_hi = me < lax.axis_size("vol") - 1
    barrier = pltpu.get_barrier_semaphore()

    @pl.when(has_lo)
    def _():
        pl.semaphore_signal(barrier, inc=1, device_id=(view, me - 1), device_id_type=pl.DeviceIdType.MESH)

    @pl.when(has_hi)
    def _():
        pl.semaphore_signal(barrier, inc=1, device_id=(view, me + 1), device_id_type=pl.DeviceIdType.MESH)

    pl.semaphore_wait(barrier, has_lo.astype(jnp.int32) + has_hi.astype(jnp.int32))

    @pl.when(jnp.logical_not(has_lo))
    def _():
        recv_ref[:, 0] = jnp.zeros(recv_ref.shape[:1] + recv_ref.shape[2:], jnp.float32)

    @pl.when(jnp.logical_not(has_hi))
    def _():
        recv_ref[:, 1] = jnp.zeros(recv_ref.shape[:1] + recv_ref.shape[2:], jnp.float32)

    def copies(v):
        up = pltpu.make_async_remote_copy(
            src_ref=send_ref.at[v, 1], dst_ref=recv_ref.at[v, 0],
            send_sem=send_sem.at[v, 1], recv_sem=recv_sem.at[v, 0],
            device_id=(view, me + 1), device_id_type=pl.DeviceIdType.MESH,
        )
        down = pltpu.make_async_remote_copy(
            src_ref=send_ref.at[v, 0], dst_ref=recv_ref.at[v, 1],
            send_sem=send_sem.at[v, 0], recv_sem=recv_sem.at[v, 1],
            device_id=(view, me - 1), device_id_type=pl.DeviceIdType.MESH,
        )
        return up, down

    tb = [[taps_ref[v * 27 + 9 + t] for t in range(9)] for v in range(count)]

    def finish(v):
        up, down = copies(v)

        @pl.when(has_hi)
        def _():
            up.wait_send()
            down.wait_recv()

        @pl.when(has_lo)
        def _():
            down.wait_send()
            up.wait_recv()

        def back(c, carry):
            z0 = pl.multiple_of(c * CZ, CZ)
            p0 = pl.multiple_of(c * (CZ // 2), CZ // 2)
            ext_ref[:, 0:4, :] = _unpack(recv_ref.at[v, 0], p0)[:, 0:4, :]
            ext_ref[:, 4 : 4 + width, :] = part_ref[v, pl.ds(z0, CZ)]
            ext_ref[:, 4 + width :, :] = _unpack(recv_ref.at[v, 1], p0)[:, 0:4, :]
            acc = tb[v][8] * ext_ref[:, pl.ds(0, 8), :]
            for t in range(1, 9):
                acc = acc + tb[v][8 - t] * ext_ref[:, pl.ds(t, 8), :]
            term = jnp.log(acc)
            if v == 0:
                logs_ref[pl.ds(z0, CZ)] = term
            else:
                logs_ref[pl.ds(z0, CZ)] = logs_ref[pl.ds(z0, CZ)] + term
            return carry

        lax.fori_loop(0, nz // CZ, back, 0)

    zeros = jnp.zeros((4, width, ny), jnp.float32)
    a_ref[0:4] = zeros
    a_ref[nz + 4 : nz + 8] = zeros
    c_ref[0:4] = zeros
    c_ref[nz + 4 : nz + 8] = zeros
    for v in range(count):
        tx = [taps_ref[v * 27 + 9 + t] for t in range(9)]
        tz = [taps_ref[v * 27 + t] for t in range(9)]
        ty = [taps_ref[v * 27 + 18 + t] for t in range(9)]

        def along_x(c, carry):
            z0 = pl.multiple_of(c * CZ, CZ)
            _fill_wide(ext_ref, before_ref, mid_ref, after_ref, z0)
            acc = tx[0] * ext_ref[:, pl.ds(0, 8), :]
            for t in range(1, 9):
                acc = acc + tx[t] * ext_ref[:, pl.ds(t, 8), :]
            a_ref[pl.ds(z0 + 4, CZ)] = acc
            return carry

        lax.fori_loop(0, nz // CZ, along_x, 0)
        wy = _lane_weights(ty, ny, False)
        wy_rev = _lane_weights(ty, ny, True)

        def middle(c, carry):
            z0 = pl.multiple_of(c * CZ, CZ)
            acc = tz[0] * a_ref[pl.ds(z0, CZ)]
            for t in range(1, 9):
                acc = acc + tz[t] * a_ref[pl.ds(z0 + t, CZ)]
            blurred = _lane_correlate(acc, wy)
            ratio = brick_ref[v, pl.ds(z0, CZ)].astype(jnp.float32) / blurred
            c_ref[pl.ds(z0 + 4, CZ)] = _lane_correlate(ratio, wy_rev)
            return carry

        lax.fori_loop(0, nz // CZ, middle, 0)

        def along_z_back(c, carry):
            z0 = pl.multiple_of(c * CZ, CZ)
            acc = tz[8] * c_ref[pl.ds(z0, CZ)]
            for t in range(1, 9):
                acc = acc + tz[8 - t] * c_ref[pl.ds(z0 + t, CZ)]
            part_ref[v, pl.ds(z0, CZ)] = acc
            _pack(acc, send_ref.at[v, 0], send_ref.at[v, 1], pl.multiple_of(c * (CZ // 2), CZ // 2))
            return carry

        lax.fori_loop(0, nz // CZ, along_z_back, 0)
        up, down = copies(v)

        @pl.when(has_hi)
        def _():
            up.start()

        @pl.when(has_lo)
        def _():
            down.start()

        if v >= 1:
            finish(v - 1)
    finish(count - 1)


def iteration_logs(taps_flat, before, mid, after, bricks):
    count, nz, width, ny = bricks.shape
    return pl.pallas_call(
        _iteration_kernel,
        in_specs=[pl.BlockSpec(memory_space=pltpu.SMEM)] + [pl.BlockSpec(memory_space=pltpu.VMEM)] * 4,
        out_specs=pl.BlockSpec(memory_space=pltpu.VMEM),
        out_shape=jax.ShapeDtypeStruct((nz, width, ny), jnp.float32),
        scratch_shapes=[
            pltpu.VMEM((nz + 8, width, ny), jnp.float32),
            pltpu.VMEM((nz + 8, width, ny), jnp.float32),
            pltpu.VMEM((CZ, width + 8, ny), jnp.float32),
            pltpu.VMEM((count, nz, width, ny), jnp.float32),
            pltpu.VMEM((count, 2, nz // 2, width, ny), jnp.float32),
            pltpu.VMEM((count, 2, nz // 2, width, ny), jnp.float32),
            pltpu.SemaphoreType.DMA((count, 2)),
            pltpu.SemaphoreType.DMA((count, 2)),
        ],
        compiler_params=pltpu.CompilerParams(
            collective_id=0, has_side_effects=True, vmem_limit_bytes=48 * 1024 * 1024
        ),
    )(taps_flat, before, mid, after, bricks)


def view_sum(part):
    count = lax.axis_size("view")
    core_swap = [(i, i ^ 1) for i in range(count)]
    chip_swap = [(i, i ^ 2) for i in range(count)]
    half = part.shape[0] // 2
    core = lax.axis_index("view") % 2
    own = lax.dynamic_slice_in_dim(part, core * half, half, axis=0)
    give = lax.dynamic_slice_in_dim(part, (1 - core) * half, half, axis=0)
    own = own + lax.ppermute(give, "view", core_swap)
    own = own + lax.ppermute(own, "view", chip_swap)
    other = lax.ppermute(own, "view", core_swap)
    low = jnp.where(core == 0, own, other)
    high = jnp.where(core == 0, other, own)
    return jnp.concatenate([low, high], axis=0)


def per_device(raw_views, weights, offsets, psf_taps):
    count = raw_views.shape[0]
    total_views = count * lax.axis_size("view")
    rim_width = (psf_taps.shape[2] - 1) // 2
    weight_norm = weights / jnp.sum(weights, axis=-1, keepdims=True)
    taps_norm = psf_taps / jnp.sum(psf_taps, axis=-1, keepdims=True)
    taps_flat = taps_norm.reshape(-1)
    local_views = resample_views(raw_views, weight_norm, offsets)
    bricks = lax.all_to_all(local_views, "vol", split_axis=2, concat_axis=1, tiled=True)
    local_sum = bricks[0].astype(jnp.float32)
    for index in range(1, count):
        local_sum = local_sum + bricks[index].astype(jnp.float32)
    joined_volume = view_sum(local_sum) / total_views
    for turn in range(ITERS):
        before, after = halos(joined_volume, "vol", 1, rim_width)
        logs = iteration_logs(taps_flat, before, joined_volume, after, bricks)
        summed = view_sum(logs)
        joined_volume = joined_volume * jnp.exp(summed / total_views)
    return joined_volume


def solution(mesh):
    placed = (
        P("view", "vol", None, None),
        P("view", None, None),
        P("view", None),
        P("view", None, None),
    )
    return jax.shard_map(
        per_device, mesh=mesh, in_specs=placed, out_specs=P(None, "vol", None), check_vma=False
    )
```

```python
import functools

import jax
import jax.numpy as jnp
from jax import lax
from jax.experimental import pallas as pl
from jax.experimental.pallas import tpu as pltpu
from jax.sharding import PartitionSpec as P

ITERS = 2
CZ = 32


def halos(shard, axis, dim, width):
    length = shard.shape[dim]
    last = lax.slice_in_dim(shard, length - width, length, axis=dim)
    first = lax.slice_in_dim(shard, 0, width, axis=dim)
    return swap_rims(first, last, axis)


def swap_rims(first, last, axis):
    devices = lax.axis_size(axis)
    up = [(i, (i + 1) % devices) for i in range(devices - 1)]
    down = [(j, i) for i, j in up]
    before = lax.ppermute(last, axis, up)
    after = lax.ppermute(first, axis, down)
    return before, after


def _fill_wide(wide_ref, before_ref, mid_ref, after_ref, z0):
    rim = before_ref.shape[1]
    width = mid_ref.shape[1]
    wide_ref[:, 0:rim, :] = before_ref[pl.ds(z0, CZ)]
    wide_ref[:, rim : rim + width, :] = mid_ref[pl.ds(z0, CZ)]
    wide_ref[:, rim + width :, :] = after_ref[pl.ds(z0, CZ)]


def resample_views(raw_views, weight_norm, offsets):
    rows = raw_views.shape[2]
    band = weight_norm.shape[2]
    lag = jnp.arange(rows, dtype=jnp.int32)[None, None, :] - offsets[:, :, None]
    matrix = jnp.zeros(lag.shape, jnp.float32)
    for k in range(band):
        matrix = matrix + jnp.where(lag == k, weight_norm[:, :, k : k + 1], 0.0)
    result = jnp.einsum(
        "vxr,vzry->vzxy",
        matrix,
        raw_views.astype(jnp.float32),
        precision=lax.Precision.HIGHEST,
        preferred_element_type=jnp.float32,
    )
    return result.astype(jnp.bfloat16)


def _lane_weights(taps, ny, reverse):
    lane = lax.broadcasted_iota(jnp.int32, (8, ny), 1)
    out = []
    for t in range(9):
        d = t - 4
        tap = taps[8 - t] if reverse else taps[t]
        valid = (lane + d >= 0) & (lane + d < ny)
        out.append(((-d) % ny, jnp.where(valid, tap, 0.0)))
    return out


def _lane_correlate(f, weights):
    acc = None
    for shift, w in weights:
        rolled = f if shift == 0 else pltpu.roll(f, shift, 2)
        term = rolled * w[None]
        acc = term if acc is None else acc + term
    return acc


def _forward_kernel(
    v, taps_ref, before_ref, mid_ref, after_ref, brick_ref, out_ref, first_ref, last_ref, a_ref, c_ref, est_ref
):
    nz, width, ny = out_ref.shape
    rim = first_ref.shape[1]
    tx = [taps_ref[v * 27 + 9 + t] for t in range(9)]
    tz = [taps_ref[v * 27 + t] for t in range(9)]
    ty = [taps_ref[v * 27 + 18 + t] for t in range(9)]
    zeros = jnp.zeros((4,) + a_ref.shape[1:], jnp.float32)
    a_ref[0:4] = zeros
    a_ref[nz + 4 : nz + 8] = zeros
    c_ref[0:4] = zeros
    c_ref[nz + 4 : nz + 8] = zeros

    def along_x(c, carry):
        z0 = pl.multiple_of(c * CZ, CZ)
        _fill_wide(est_ref, before_ref, mid_ref, after_ref, z0)
        acc = tx[0] * est_ref[:, pl.ds(0, 8), :]
        for t in range(1, 9):
            acc = acc + tx[t] * est_ref[:, pl.ds(t, 8), :]
        a_ref[pl.ds(z0 + 4, CZ)] = acc
        return carry

    lax.fori_loop(0, nz // CZ, along_x, 0)
    wy = _lane_weights(ty, ny, False)
    wy_rev = _lane_weights(ty, ny, True)

    def middle(c, carry):
        z0 = pl.multiple_of(c * CZ, CZ)
        acc = tz[0] * a_ref[pl.ds(z0, CZ)]
        for t in range(1, 9):
            acc = acc + tz[t] * a_ref[pl.ds(z0 + t, CZ)]
        blurred = _lane_correlate(acc, wy)
        ratio = brick_ref[pl.ds(z0, CZ)].astype(jnp.float32) / blurred
        c_ref[pl.ds(z0 + 4, CZ)] = _lane_correlate(ratio, wy_rev)
        return carry

    lax.fori_loop(0, nz // CZ, middle, 0)

    def along_z_back(c, carry):
        z0 = pl.multiple_of(c * CZ, CZ)
        acc = tz[8] * c_ref[pl.ds(z0, CZ)]
        for t in range(1, 9):
            acc = acc + tz[8 - t] * c_ref[pl.ds(z0 + t, CZ)]
        out_ref[pl.ds(z0, CZ)] = acc
        first_ref[pl.ds(z0, CZ)] = acc[:, :rim, :]
        last_ref[pl.ds(z0, CZ)] = acc[:, width - rim :, :]
        return carry

    lax.fori_loop(0, nz // CZ, along_z_back, 0)


def forward_partial(taps_flat, v, before, mid, after, brick):
    nz, width, ny = brick.shape
    return pl.pallas_call(
        functools.partial(_forward_kernel, v),
        in_specs=[pl.BlockSpec(memory_space=pltpu.SMEM)] + [pl.BlockSpec(memory_space=pltpu.VMEM)] * 4,
        out_specs=[pl.BlockSpec(memory_space=pltpu.VMEM)] * 3,
        out_shape=[
            jax.ShapeDtypeStruct((nz, width, ny), jnp.float32),
            jax.ShapeDtypeStruct((nz, 4, ny), jnp.float32),
            jax.ShapeDtypeStruct((nz, 4, ny), jnp.float32),
        ],
        scratch_shapes=[
            pltpu.VMEM((nz + 8, width, ny), jnp.float32),
            pltpu.VMEM((nz + 8, width, ny), jnp.float32),
            pltpu.VMEM((CZ, width + 8, ny), jnp.float32),
        ],
    )(taps_flat, before, mid, after, brick)


def _back_kernel(taps_ref, *refs):
    parts, out_ref, wide_ref = refs[:-2], refs[-2], refs[-1]
    count = len(parts) // 3
    nz = out_ref.shape[0]
    tx = [[taps_ref[v * 27 + 9 + t] for t in range(9)] for v in range(count)]

    def body(c, carry):
        z0 = pl.multiple_of(c * CZ, CZ)
        total = None
        for v in range(count):
            _fill_wide(wide_ref, *parts[3 * v : 3 * v + 3], z0)
            acc = tx[v][8] * wide_ref[:, pl.ds(0, 8), :]
            for t in range(1, 9):
                acc = acc + tx[v][8 - t] * wide_ref[:, pl.ds(t, 8), :]
            term = jnp.log(acc)
            total = term if total is None else total + term
        out_ref[pl.ds(z0, CZ)] = total
        return carry

    lax.fori_loop(0, nz // CZ, body, 0)


def back_logs(taps_flat, parts):
    nz, width, ny = parts[1].shape
    return pl.pallas_call(
        _back_kernel,
        in_specs=[pl.BlockSpec(memory_space=pltpu.SMEM)]
        + [pl.BlockSpec(memory_space=pltpu.VMEM)] * len(parts),
        out_specs=pl.BlockSpec(memory_space=pltpu.VMEM),
        out_shape=jax.ShapeDtypeStruct((nz, width, ny), jnp.float32),
        scratch_shapes=[pltpu.VMEM((CZ, width + 8, ny), jnp.float32)],
    )(taps_flat, *parts)


def _pack(acc, first_ref, last_ref, p0):
    half = acc.shape[0] // 2
    upper, lower = acc[:half], acc[half:]
    row = lax.broadcasted_iota(jnp.int32, upper.shape, 1)
    first_ref[pl.ds(p0, half)] = jnp.where(row < 4, upper, pltpu.roll(lower, 4, 1))
    last_ref[pl.ds(p0, half)] = jnp.where(row < 4, pltpu.roll(upper, 4, 1), lower)


def _unpack(packed_ref, p0):
    packed = packed_ref[pl.ds(p0, CZ // 2)]
    return jnp.concatenate([packed, pltpu.roll(packed, 4, 1)], axis=0)


def _iteration_kernel(
    taps_ref, before_ref, mid_ref, after_ref, brick_ref, logs_ref,
    a_ref, c_ref, ext_ref, part_ref, send_ref, recv_ref, send_sem, recv_sem,
):
    count, nz, width, ny = part_ref.shape
    me = lax.axis_index("vol")
    view = lax.axis_index("view")
    has_lo = me > 0
    has_hi = me < lax.axis_size("vol") - 1
    barrier = pltpu.get_barrier_semaphore()

    @pl.when(has_lo)
    def _():
        pl.semaphore_signal(barrier, inc=1, device_id=(view, me - 1), device_id_type=pl.DeviceIdType.MESH)

    @pl.when(has_hi)
    def _():
        pl.semaphore_signal(barrier, inc=1, device_id=(view, me + 1), device_id_type=pl.DeviceIdType.MESH)

    pl.semaphore_wait(barrier, has_lo.astype(jnp.int32) + has_hi.astype(jnp.int32))

    @pl.when(jnp.logical_not(has_lo))
    def _():
        recv_ref[:, 0] = jnp.zeros(recv_ref.shape[:1] + recv_ref.shape[2:], jnp.float32)

    @pl.when(jnp.logical_not(has_hi))
    def _():
        recv_ref[:, 1] = jnp.zeros(recv_ref.shape[:1] + recv_ref.shape[2:], jnp.float32)

    def copies(v):
        up = pltpu.make_async_remote_copy(
            src_ref=send_ref.at[v, 1], dst_ref=recv_ref.at[v, 0],
            send_sem=send_sem.at[v, 1], recv_sem=recv_sem.at[v, 0],
            device_id=(view, me + 1), device_id_type=pl.DeviceIdType.MESH,
        )
        down = pltpu.make_async_remote_copy(
            src_ref=send_ref.at[v, 0], dst_ref=recv_ref.at[v, 1],
            send_sem=send_sem.at[v, 0], recv_sem=recv_sem.at[v, 1],
            device_id=(view, me - 1), device_id_type=pl.DeviceIdType.MESH,
        )
        return up, down

    tb = [[taps_ref[v * 27 + 9 + t] for t in range(9)] for v in range(count)]

    def finish(v):
        up, down = copies(v)

        @pl.when(has_hi)
        def _():
            up.wait_send()
            down.wait_recv()

        @pl.when(has_lo)
        def _():
            down.wait_send()
            up.wait_recv()

        def back(c, carry):
            z0 = pl.multiple_of(c * CZ, CZ)
            p0 = pl.multiple_of(c * (CZ // 2), CZ // 2)
            ext_ref[:, 0:4, :] = _unpack(recv_ref.at[v, 0], p0)[:, 0:4, :]
            ext_ref[:, 4 : 4 + width, :] = part_ref[v, pl.ds(z0, CZ)]
            ext_ref[:, 4 + width :, :] = _unpack(recv_ref.at[v, 1], p0)[:, 0:4, :]
            acc = tb[v][8] * ext_ref[:, pl.ds(0, 8), :]
            for t in range(1, 9):
                acc = acc + tb[v][8 - t] * ext_ref[:, pl.ds(t, 8), :]
            term = jnp.log(acc)
            if v == 0:
                logs_ref[pl.ds(z0, CZ)] = term
            else:
                logs_ref[pl.ds(z0, CZ)] = logs_ref[pl.ds(z0, CZ)] + term
            return carry

        lax.fori_loop(0, nz // CZ, back, 0)

    zeros = jnp.zeros((4, width, ny), jnp.float32)
    a_ref[0:4] = zeros
    a_ref[nz + 4 : nz + 8] = zeros
    c_ref[0:4] = zeros
    c_ref[nz + 4 : nz + 8] = zeros
    for v in range(count):
        tx = [taps_ref[v * 27 + 9 + t] for t in range(9)]
        tz = [taps_ref[v * 27 + t] for t in range(9)]
        ty = [taps_ref[v * 27 + 18 + t] for t in range(9)]

        def along_x(c, carry):
            z0 = pl.multiple_of(c * CZ, CZ)
            _fill_wide(ext_ref, before_ref, mid_ref, after_ref, z0)
            acc = tx[0] * ext_ref[:, pl.ds(0, 8), :]
            for t in range(1, 9):
                acc = acc + tx[t] * ext_ref[:, pl.ds(t, 8), :]
            a_ref[pl.ds(z0 + 4, CZ)] = acc
            return carry

        lax.fori_loop(0, nz // CZ, along_x, 0)
        wy = _lane_weights(ty, ny, False)
        wy_rev = _lane_weights(ty, ny, True)

        def middle(c, carry):
            z0 = pl.multiple_of(c * CZ, CZ)
            acc = tz[0] * a_ref[pl.ds(z0, CZ)]
            for t in range(1, 9):
                acc = acc + tz[t] * a_ref[pl.ds(z0 + t, CZ)]
            blurred = _lane_correlate(acc, wy)
            ratio = brick_ref[v, pl.ds(z0, CZ)].astype(jnp.float32) / blurred
            c_ref[pl.ds(z0 + 4, CZ)] = _lane_correlate(ratio, wy_rev)
            return carry

        lax.fori_loop(0, nz // CZ, middle, 0)

        def along_z_back(c, carry):
            z0 = pl.multiple_of(c * CZ, CZ)
            acc = tz[8] * c_ref[pl.ds(z0, CZ)]
            for t in range(1, 9):
                acc = acc + tz[8 - t] * c_ref[pl.ds(z0 + t, CZ)]
            part_ref[v, pl.ds(z0, CZ)] = acc
            _pack(acc, send_ref.at[v, 0], send_ref.at[v, 1], pl.multiple_of(c * (CZ // 2), CZ // 2))
            return carry

        lax.fori_loop(0, nz // CZ, along_z_back, 0)
        up, down = copies(v)

        @pl.when(has_hi)
        def _():
            up.start()

        @pl.when(has_lo)
        def _():
            down.start()

        if v >= 1:
            finish(v - 1)
    finish(count - 1)


def iteration_logs(taps_flat, before, mid, after, bricks):
    count, nz, width, ny = bricks.shape
    return pl.pallas_call(
        _iteration_kernel,
        in_specs=[pl.BlockSpec(memory_space=pltpu.SMEM)] + [pl.BlockSpec(memory_space=pltpu.VMEM)] * 4,
        out_specs=pl.BlockSpec(memory_space=pltpu.VMEM),
        out_shape=jax.ShapeDtypeStruct((nz, width, ny), jnp.float32),
        scratch_shapes=[
            pltpu.VMEM((nz + 8, width, ny), jnp.float32),
            pltpu.VMEM((nz + 8, width, ny), jnp.float32),
            pltpu.VMEM((CZ, width + 8, ny), jnp.float32),
            pltpu.VMEM((count, nz, width, ny), jnp.float32),
            pltpu.VMEM((count, 2, nz // 2, width, ny), jnp.float32),
            pltpu.VMEM((count, 2, nz // 2, width, ny), jnp.float32),
            pltpu.SemaphoreType.DMA((count, 2)),
            pltpu.SemaphoreType.DMA((count, 2)),
        ],
        compiler_params=pltpu.CompilerParams(
            collective_id=0, has_side_effects=True, vmem_limit_bytes=48 * 1024 * 1024
        ),
    )(taps_flat, before, mid, after, bricks)


def _by_core(core, mine, theirs):
    low = jnp.where(core == 0, mine, theirs)
    high = jnp.where(core == 0, theirs, mine)
    return jnp.concatenate([low, high], axis=0)


def view_sum_update(part, update, rim_width):
    count = lax.axis_size("view")
    core_swap = [(i, i ^ 1) for i in range(count)]
    chip_swap = [(i, i ^ 2) for i in range(count)]
    half = part.shape[0] // 2
    core = lax.axis_index("view") % 2
    own = lax.dynamic_slice_in_dim(part, core * half, half, axis=0)
    give = lax.dynamic_slice_in_dim(part, (1 - core) * half, half, axis=0)
    own = own + lax.ppermute(give, "view", core_swap)
    own = own + lax.ppermute(own, "view", chip_swap)
    fresh = update(own, core * half, half)
    whole = _by_core(core, fresh, lax.ppermute(fresh, "view", core_swap))
    if rim_width is None:
        return whole
    before, after = halos(fresh, "vol", 1, rim_width)
    before = _by_core(core, before, lax.ppermute(before, "view", core_swap))
    after = _by_core(core, after, lax.ppermute(after, "view", core_swap))
    return whole, before, after


def per_device(raw_views, weights, offsets, psf_taps):
    count = raw_views.shape[0]
    total_views = count * lax.axis_size("view")
    rim_width = (psf_taps.shape[2] - 1) // 2
    weight_norm = weights / jnp.sum(weights, axis=-1, keepdims=True)
    taps_norm = psf_taps / jnp.sum(psf_taps, axis=-1, keepdims=True)
    taps_flat = taps_norm.reshape(-1)
    local_views = resample_views(raw_views, weight_norm, offsets)
    bricks = lax.all_to_all(local_views, "vol", split_axis=2, concat_axis=1, tiled=True)
    local_sum = bricks[0].astype(jnp.float32)
    for index in range(1, count):
        local_sum = local_sum + bricks[index].astype(jnp.float32)
    joined_volume, before, after = view_sum_update(
        local_sum, lambda own, at, size: own / total_views, rim_width
    )
    for turn in range(ITERS):
        logs = iteration_logs(taps_flat, before, joined_volume, after, bricks)

        def update(own, at, size, previous=joined_volume):
            return lax.dynamic_slice_in_dim(previous, at, size, axis=0) * jnp.exp(own / total_views)

        result = view_sum_update(logs, update, rim_width if turn < ITERS - 1 else None)
        if turn < ITERS - 1:
            joined_volume, before, after = result
        else:
            joined_volume = result
    return joined_volume


def solution(mesh):
    placed = (
        P("view", "vol", None, None),
        P("view", None, None),
        P("view", None),
        P("view", None, None),
    )
    return jax.shard_map(
        per_device, mesh=mesh, in_specs=placed, out_specs=P(None, "vol", None), check_vma=False
    )
```

```python
import functools

import jax
import jax.numpy as jnp
from jax import lax
from jax.experimental import pallas as pl
from jax.experimental.pallas import tpu as pltpu
from jax.sharding import PartitionSpec as P

ITERS = 2
CZ = 32


def halos(shard, axis, dim, width):
    length = shard.shape[dim]
    last = lax.slice_in_dim(shard, length - width, length, axis=dim)
    first = lax.slice_in_dim(shard, 0, width, axis=dim)
    return swap_rims(first, last, axis)


def swap_rims(first, last, axis):
    devices = lax.axis_size(axis)
    up = [(i, (i + 1) % devices) for i in range(devices - 1)]
    down = [(j, i) for i, j in up]
    before = lax.ppermute(last, axis, up)
    after = lax.ppermute(first, axis, down)
    return before, after


def _fill_wide(wide_ref, before_ref, mid_ref, after_ref, z0):
    rim = before_ref.shape[1]
    width = mid_ref.shape[1]
    wide_ref[:, 0:rim, :] = before_ref[pl.ds(z0, CZ)]
    wide_ref[:, rim : rim + width, :] = mid_ref[pl.ds(z0, CZ)]
    wide_ref[:, rim + width :, :] = after_ref[pl.ds(z0, CZ)]


def resample_views(raw_views, weight_norm, offsets):
    rows = raw_views.shape[2]
    band = weight_norm.shape[2]
    lag = jnp.arange(rows, dtype=jnp.int32)[None, None, :] - offsets[:, :, None]
    matrix = jnp.zeros(lag.shape, jnp.float32)
    for k in range(band):
        matrix = matrix + jnp.where(lag == k, weight_norm[:, :, k : k + 1], 0.0)
    result = jnp.einsum(
        "vxr,vzry->vzxy",
        matrix,
        raw_views.astype(jnp.float32),
        precision=lax.Precision.HIGHEST,
        preferred_element_type=jnp.float32,
    )
    return result.astype(jnp.bfloat16)


def _lane_weights(taps, ny, reverse):
    lane = lax.broadcasted_iota(jnp.int32, (8, ny), 1)
    out = []
    for t in range(9):
        d = t - 4
        tap = taps[8 - t] if reverse else taps[t]
        valid = (lane + d >= 0) & (lane + d < ny)
        out.append(((-d) % ny, jnp.where(valid, tap, 0.0)))
    return out


def _lane_correlate(f, weights):
    acc = None
    for shift, w in weights:
        rolled = f if shift == 0 else pltpu.roll(f, shift, 2)
        term = rolled * w[None]
        acc = term if acc is None else acc + term
    return acc


def _forward_kernel(
    v, taps_ref, before_ref, mid_ref, after_ref, brick_ref, out_ref, first_ref, last_ref, a_ref, c_ref, est_ref
):
    nz, width, ny = out_ref.shape
    rim = first_ref.shape[1]
    tx = [taps_ref[v * 27 + 9 + t] for t in range(9)]
    tz = [taps_ref[v * 27 + t] for t in range(9)]
    ty = [taps_ref[v * 27 + 18 + t] for t in range(9)]
    zeros = jnp.zeros((4,) + a_ref.shape[1:], jnp.float32)
    a_ref[0:4] = zeros
    a_ref[nz + 4 : nz + 8] = zeros
    c_ref[0:4] = zeros
    c_ref[nz + 4 : nz + 8] = zeros

    def along_x(c, carry):
        z0 = pl.multiple_of(c * CZ, CZ)
        _fill_wide(est_ref, before_ref, mid_ref, after_ref, z0)
        acc = tx[0] * est_ref[:, pl.ds(0, 8), :]
        for t in range(1, 9):
            acc = acc + tx[t] * est_ref[:, pl.ds(t, 8), :]
        a_ref[pl.ds(z0 + 4, CZ)] = acc
        return carry

    lax.fori_loop(0, nz // CZ, along_x, 0)
    wy = _lane_weights(ty, ny, False)
    wy_rev = _lane_weights(ty, ny, True)

    def middle(c, carry):
        z0 = pl.multiple_of(c * CZ, CZ)
        acc = tz[0] * a_ref[pl.ds(z0, CZ)]
        for t in range(1, 9):
            acc = acc + tz[t] * a_ref[pl.ds(z0 + t, CZ)]
        blurred = _lane_correlate(acc, wy)
        ratio = brick_ref[pl.ds(z0, CZ)].astype(jnp.float32) / blurred
        c_ref[pl.ds(z0 + 4, CZ)] = _lane_correlate(ratio, wy_rev)
        return carry

    lax.fori_loop(0, nz // CZ, middle, 0)

    def along_z_back(c, carry):
        z0 = pl.multiple_of(c * CZ, CZ)
        acc = tz[8] * c_ref[pl.ds(z0, CZ)]
        for t in range(1, 9):
            acc = acc + tz[8 - t] * c_ref[pl.ds(z0 + t, CZ)]
        out_ref[pl.ds(z0, CZ)] = acc
        first_ref[pl.ds(z0, CZ)] = acc[:, :rim, :]
        last_ref[pl.ds(z0, CZ)] = acc[:, width - rim :, :]
        return carry

    lax.fori_loop(0, nz // CZ, along_z_back, 0)


def forward_partial(taps_flat, v, before, mid, after, brick):
    nz, width, ny = brick.shape
    return pl.pallas_call(
        functools.partial(_forward_kernel, v),
        in_specs=[pl.BlockSpec(memory_space=pltpu.SMEM)] + [pl.BlockSpec(memory_space=pltpu.VMEM)] * 4,
        out_specs=[pl.BlockSpec(memory_space=pltpu.VMEM)] * 3,
        out_shape=[
            jax.ShapeDtypeStruct((nz, width, ny), jnp.float32),
            jax.ShapeDtypeStruct((nz, 4, ny), jnp.float32),
            jax.ShapeDtypeStruct((nz, 4, ny), jnp.float32),
        ],
        scratch_shapes=[
            pltpu.VMEM((nz + 8, width, ny), jnp.float32),
            pltpu.VMEM((nz + 8, width, ny), jnp.float32),
            pltpu.VMEM((CZ, width + 8, ny), jnp.float32),
        ],
    )(taps_flat, before, mid, after, brick)


def _back_kernel(taps_ref, *refs):
    parts, out_ref, wide_ref = refs[:-2], refs[-2], refs[-1]
    count = len(parts) // 3
    nz = out_ref.shape[0]
    tx = [[taps_ref[v * 27 + 9 + t] for t in range(9)] for v in range(count)]

    def body(c, carry):
        z0 = pl.multiple_of(c * CZ, CZ)
        total = None
        for v in range(count):
            _fill_wide(wide_ref, *parts[3 * v : 3 * v + 3], z0)
            acc = tx[v][8] * wide_ref[:, pl.ds(0, 8), :]
            for t in range(1, 9):
                acc = acc + tx[v][8 - t] * wide_ref[:, pl.ds(t, 8), :]
            term = jnp.log(acc)
            total = term if total is None else total + term
        out_ref[pl.ds(z0, CZ)] = total
        return carry

    lax.fori_loop(0, nz // CZ, body, 0)


def back_logs(taps_flat, parts):
    nz, width, ny = parts[1].shape
    return pl.pallas_call(
        _back_kernel,
        in_specs=[pl.BlockSpec(memory_space=pltpu.SMEM)]
        + [pl.BlockSpec(memory_space=pltpu.VMEM)] * len(parts),
        out_specs=pl.BlockSpec(memory_space=pltpu.VMEM),
        out_shape=jax.ShapeDtypeStruct((nz, width, ny), jnp.float32),
        scratch_shapes=[pltpu.VMEM((CZ, width + 8, ny), jnp.float32)],
    )(taps_flat, *parts)


def _pack(acc, first_ref, last_ref, p0):
    half = acc.shape[0] // 2
    upper, lower = acc[:half], acc[half:]
    row = lax.broadcasted_iota(jnp.int32, upper.shape, 1)
    first_ref[pl.ds(p0, half)] = jnp.where(row < 4, upper, pltpu.roll(lower, 4, 1))
    last_ref[pl.ds(p0, half)] = jnp.where(row < 4, pltpu.roll(upper, 4, 1), lower)


def _unpack(packed_ref, p0):
    packed = packed_ref[pl.ds(p0, CZ // 2)]
    return jnp.concatenate([packed, pltpu.roll(packed, 4, 1)], axis=0)


def _iteration_kernel(
    taps_ref, before_ref, mid_ref, after_ref, brick_ref, logs_ref,
    a_ref, c_ref, ext_ref, part_ref, send_ref, recv_ref, send_sem, recv_sem,
):
    count, nz, width, ny = part_ref.shape
    me = lax.axis_index("vol")
    view = lax.axis_index("view")
    has_lo = me > 0
    has_hi = me < lax.axis_size("vol") - 1
    barrier = pltpu.get_barrier_semaphore()

    @pl.when(has_lo)
    def _():
        pl.semaphore_signal(barrier, inc=1, device_id=(view, me - 1), device_id_type=pl.DeviceIdType.MESH)

    @pl.when(has_hi)
    def _():
        pl.semaphore_signal(barrier, inc=1, device_id=(view, me + 1), device_id_type=pl.DeviceIdType.MESH)

    pl.semaphore_wait(barrier, has_lo.astype(jnp.int32) + has_hi.astype(jnp.int32))

    @pl.when(jnp.logical_not(has_lo))
    def _():
        recv_ref[:, 0] = jnp.zeros(recv_ref.shape[:1] + recv_ref.shape[2:], jnp.float32)

    @pl.when(jnp.logical_not(has_hi))
    def _():
        recv_ref[:, 1] = jnp.zeros(recv_ref.shape[:1] + recv_ref.shape[2:], jnp.float32)

    def copies(v):
        up = pltpu.make_async_remote_copy(
            src_ref=send_ref.at[v, 1], dst_ref=recv_ref.at[v, 0],
            send_sem=send_sem.at[v, 1], recv_sem=recv_sem.at[v, 0],
            device_id=(view, me + 1), device_id_type=pl.DeviceIdType.MESH,
        )
        down = pltpu.make_async_remote_copy(
            src_ref=send_ref.at[v, 0], dst_ref=recv_ref.at[v, 1],
            send_sem=send_sem.at[v, 0], recv_sem=recv_sem.at[v, 1],
            device_id=(view, me - 1), device_id_type=pl.DeviceIdType.MESH,
        )
        return up, down

    tb = [[taps_ref[v * 27 + 9 + t] for t in range(9)] for v in range(count)]

    def finish(v):
        up, down = copies(v)

        @pl.when(has_hi)
        def _():
            up.wait_send()
            down.wait_recv()

        @pl.when(has_lo)
        def _():
            down.wait_send()
            up.wait_recv()

        def back(c, carry):
            z0 = pl.multiple_of(c * CZ, CZ)
            p0 = pl.multiple_of(c * (CZ // 2), CZ // 2)
            ext_ref[:, 0:4, :] = _unpack(recv_ref.at[v, 0], p0)[:, 0:4, :]
            ext_ref[:, 4 : 4 + width, :] = part_ref[v, pl.ds(z0, CZ)]
            ext_ref[:, 4 + width :, :] = _unpack(recv_ref.at[v, 1], p0)[:, 0:4, :]
            acc = tb[v][8] * ext_ref[:, pl.ds(0, 8), :]
            for t in range(1, 9):
                acc = acc + tb[v][8 - t] * ext_ref[:, pl.ds(t, 8), :]
            term = jnp.log(acc)
            if v == 0:
                logs_ref[pl.ds(z0, CZ)] = term
            else:
                logs_ref[pl.ds(z0, CZ)] = logs_ref[pl.ds(z0, CZ)] + term
            return carry

        lax.fori_loop(0, nz // CZ, back, 0)

    zeros = jnp.zeros((4, width, ny), jnp.float32)
    c_ref[0:4] = zeros
    c_ref[nz + 4 : nz + 8] = zeros
    tx_all = [[taps_ref[v * 27 + 9 + t] for t in range(9)] for v in range(count)]
    for v in range(count):
        a_ref[v, 0:4] = zeros
        a_ref[v, nz + 4 : nz + 8] = zeros

    def along_x(c, carry):
        z0 = pl.multiple_of(c * CZ, CZ)
        _fill_wide(ext_ref, before_ref, mid_ref, after_ref, z0)
        for sub in range(0, CZ, 8):
            accs = [None] * count
            for t in range(9):
                shifted = ext_ref[pl.ds(sub, 8), pl.ds(t, 8), :]
                for v in range(count):
                    term = tx_all[v][t] * shifted
                    accs[v] = term if accs[v] is None else accs[v] + term
            for v in range(count):
                a_ref[v, pl.ds(z0 + 4 + sub, 8)] = accs[v]
        return carry

    lax.fori_loop(0, nz // CZ, along_x, 0)
    for v in range(count):
        tz = [taps_ref[v * 27 + t] for t in range(9)]
        ty = [taps_ref[v * 27 + 18 + t] for t in range(9)]

        wy = _lane_weights(ty, ny, False)
        wy_rev = _lane_weights(ty, ny, True)

        def middle(c, carry):
            z0 = pl.multiple_of(c * CZ, CZ)
            acc = tz[0] * a_ref[v, pl.ds(z0, CZ)]
            for t in range(1, 9):
                acc = acc + tz[t] * a_ref[v, pl.ds(z0 + t, CZ)]
            blurred = _lane_correlate(acc, wy)
            ratio = brick_ref[v, pl.ds(z0, CZ)].astype(jnp.float32) / blurred
            c_ref[pl.ds(z0 + 4, CZ)] = _lane_correlate(ratio, wy_rev)
            return carry

        lax.fori_loop(0, nz // CZ, middle, 0)

        def along_z_back(c, carry):
            z0 = pl.multiple_of(c * CZ, CZ)
            acc = tz[8] * c_ref[pl.ds(z0, CZ)]
            for t in range(1, 9):
                acc = acc + tz[8 - t] * c_ref[pl.ds(z0 + t, CZ)]
            part_ref[v, pl.ds(z0, CZ)] = acc
            _pack(acc, send_ref.at[v, 0], send_ref.at[v, 1], pl.multiple_of(c * (CZ // 2), CZ // 2))
            return carry

        lax.fori_loop(0, nz // CZ, along_z_back, 0)
        up, down = copies(v)

        @pl.when(has_hi)
        def _():
            up.start()

        @pl.when(has_lo)
        def _():
            down.start()

    for v in range(count):
        finish(v)


def iteration_logs(taps_flat, before, mid, after, bricks):
    count, nz, width, ny = bricks.shape
    return pl.pallas_call(
        _iteration_kernel,
        in_specs=[pl.BlockSpec(memory_space=pltpu.SMEM)] + [pl.BlockSpec(memory_space=pltpu.VMEM)] * 4,
        out_specs=pl.BlockSpec(memory_space=pltpu.VMEM),
        out_shape=jax.ShapeDtypeStruct((nz, width, ny), jnp.float32),
        scratch_shapes=[
            pltpu.VMEM((count, nz + 8, width, ny), jnp.float32),
            pltpu.VMEM((nz + 8, width, ny), jnp.float32),
            pltpu.VMEM((CZ, width + 8, ny), jnp.float32),
            pltpu.VMEM((count, nz, width, ny), jnp.float32),
            pltpu.VMEM((count, 2, nz // 2, width, ny), jnp.float32),
            pltpu.VMEM((count, 2, nz // 2, width, ny), jnp.float32),
            pltpu.SemaphoreType.DMA((count, 2)),
            pltpu.SemaphoreType.DMA((count, 2)),
        ],
        compiler_params=pltpu.CompilerParams(
            collective_id=0, has_side_effects=True, vmem_limit_bytes=48 * 1024 * 1024
        ),
    )(taps_flat, before, mid, after, bricks)


def _by_core(core, mine, theirs):
    low = jnp.where(core == 0, mine, theirs)
    high = jnp.where(core == 0, theirs, mine)
    return jnp.concatenate([low, high], axis=0)


def view_sum_update(part, update, rim_width):
    count = lax.axis_size("view")
    core_swap = [(i, i ^ 1) for i in range(count)]
    chip_swap = [(i, i ^ 2) for i in range(count)]
    half = part.shape[0] // 2
    core = lax.axis_index("view") % 2
    own = lax.dynamic_slice_in_dim(part, core * half, half, axis=0)
    give = lax.dynamic_slice_in_dim(part, (1 - core) * half, half, axis=0)
    own = own + lax.ppermute(give, "view", core_swap)
    own = own + lax.ppermute(own, "view", chip_swap)
    fresh = update(own, core * half, half)
    whole = _by_core(core, fresh, lax.ppermute(fresh, "view", core_swap))
    if rim_width is None:
        return whole
    before, after = halos(fresh, "vol", 1, rim_width)
    before = _by_core(core, before, lax.ppermute(before, "view", core_swap))
    after = _by_core(core, after, lax.ppermute(after, "view", core_swap))
    return whole, before, after


def per_device(raw_views, weights, offsets, psf_taps):
    count = raw_views.shape[0]
    total_views = count * lax.axis_size("view")
    rim_width = (psf_taps.shape[2] - 1) // 2
    weight_norm = weights / jnp.sum(weights, axis=-1, keepdims=True)
    taps_norm = psf_taps / jnp.sum(psf_taps, axis=-1, keepdims=True)
    taps_flat = taps_norm.reshape(-1)
    local_views = resample_views(raw_views, weight_norm, offsets)
    bricks = lax.all_to_all(local_views, "vol", split_axis=2, concat_axis=1, tiled=True)
    local_sum = bricks[0].astype(jnp.float32)
    for index in range(1, count):
        local_sum = local_sum + bricks[index].astype(jnp.float32)
    joined_volume, before, after = view_sum_update(
        local_sum, lambda own, at, size: own / total_views, rim_width
    )
    for turn in range(ITERS):
        logs = iteration_logs(taps_flat, before, joined_volume, after, bricks)

        def update(own, at, size, previous=joined_volume):
            return lax.dynamic_slice_in_dim(previous, at, size, axis=0) * jnp.exp(own / total_views)

        result = view_sum_update(logs, update, rim_width if turn < ITERS - 1 else None)
        if turn < ITERS - 1:
            joined_volume, before, after = result
        else:
            joined_volume = result
    return joined_volume


def solution(mesh):
    placed = (
        P("view", "vol", None, None),
        P("view", None, None),
        P("view", None),
        P("view", None, None),
    )
    return jax.shard_map(
        per_device, mesh=mesh, in_specs=placed, out_specs=P(None, "vol", None), check_vma=False
    )
```

```python
import functools

import jax
import jax.numpy as jnp
from jax import lax
from jax.experimental import pallas as pl
from jax.experimental.pallas import tpu as pltpu
from jax.sharding import PartitionSpec as P

ITERS = 2
CZ = 32


def halos(shard, axis, dim, width):
    length = shard.shape[dim]
    last = lax.slice_in_dim(shard, length - width, length, axis=dim)
    first = lax.slice_in_dim(shard, 0, width, axis=dim)
    return swap_rims(first, last, axis)


def swap_rims(first, last, axis):
    devices = lax.axis_size(axis)
    up = [(i, (i + 1) % devices) for i in range(devices - 1)]
    down = [(j, i) for i, j in up]
    before = lax.ppermute(last, axis, up)
    after = lax.ppermute(first, axis, down)
    return before, after


def _fill_wide(wide_ref, before_ref, mid_ref, after_ref, z0):
    rim = before_ref.shape[1]
    width = mid_ref.shape[1]
    wide_ref[:, 0:rim, :] = before_ref[pl.ds(z0, CZ)]
    wide_ref[:, rim : rim + width, :] = mid_ref[pl.ds(z0, CZ)]
    wide_ref[:, rim + width :, :] = after_ref[pl.ds(z0, CZ)]


def resample_views(raw_views, weight_norm, offsets):
    rows = raw_views.shape[2]
    band = weight_norm.shape[2]
    lag = jnp.arange(rows, dtype=jnp.int32)[None, None, :] - offsets[:, :, None]
    matrix = jnp.zeros(lag.shape, jnp.float32)
    for k in range(band):
        matrix = matrix + jnp.where(lag == k, weight_norm[:, :, k : k + 1], 0.0)
    result = jnp.einsum(
        "vxr,vzry->vzxy",
        matrix,
        raw_views.astype(jnp.float32),
        precision=lax.Precision.HIGHEST,
        preferred_element_type=jnp.float32,
    )
    return result.astype(jnp.bfloat16)


def _lane_weights(taps, ny, reverse):
    lane = lax.broadcasted_iota(jnp.int32, (8, ny), 1)
    out = []
    for t in range(9):
        d = t - 4
        tap = taps[8 - t] if reverse else taps[t]
        valid = (lane + d >= 0) & (lane + d < ny)
        out.append(((-d) % ny, jnp.where(valid, tap, 0.0)))
    return out


def _lane_correlate(f, weights):
    acc = None
    for shift, w in weights:
        rolled = f if shift == 0 else pltpu.roll(f, shift, 2)
        term = rolled * w[None]
        acc = term if acc is None else acc + term
    return acc


def _pack(acc, first_ref, last_ref, p0):
    half = acc.shape[0] // 2
    upper, lower = acc[:half], acc[half:]
    row = lax.broadcasted_iota(jnp.int32, upper.shape, 1)
    first_ref[pl.ds(p0, half)] = jnp.where(row < 4, upper, pltpu.roll(lower, 4, 1))
    last_ref[pl.ds(p0, half)] = jnp.where(row < 4, pltpu.roll(upper, 4, 1), lower)


def _unpack(packed_ref, p0):
    packed = packed_ref[pl.ds(p0, CZ // 2)]
    return jnp.concatenate([packed, pltpu.roll(packed, 4, 1)], axis=0)


def _iteration_kernel(
    taps_ref, before_ref, mid_ref, after_ref, brick_ref, logs_ref,
    a_ref, c_ref, ext_ref, part_ref, send_ref, recv_ref, send_sem, recv_sem,
):
    count, nz, width, ny = part_ref.shape
    me = lax.axis_index("vol")
    view = lax.axis_index("view")
    has_lo = me > 0
    has_hi = me < lax.axis_size("vol") - 1
    barrier = pltpu.get_barrier_semaphore()

    @pl.when(has_lo)
    def _():
        pl.semaphore_signal(barrier, inc=1, device_id=(view, me - 1), device_id_type=pl.DeviceIdType.MESH)

    @pl.when(has_hi)
    def _():
        pl.semaphore_signal(barrier, inc=1, device_id=(view, me + 1), device_id_type=pl.DeviceIdType.MESH)

    pl.semaphore_wait(barrier, has_lo.astype(jnp.int32) + has_hi.astype(jnp.int32))

    @pl.when(jnp.logical_not(has_lo))
    def _():
        recv_ref[:, 0] = jnp.zeros(recv_ref.shape[:1] + recv_ref.shape[2:], jnp.float32)

    @pl.when(jnp.logical_not(has_hi))
    def _():
        recv_ref[:, 1] = jnp.zeros(recv_ref.shape[:1] + recv_ref.shape[2:], jnp.float32)

    rows = nz // 4

    def copies(v, h):
        rows_h = pl.ds(h * rows, rows)
        up = pltpu.make_async_remote_copy(
            src_ref=send_ref.at[v, 1, rows_h], dst_ref=recv_ref.at[v, 0, rows_h],
            send_sem=send_sem.at[v, 1, h], recv_sem=recv_sem.at[v, 0, h],
            device_id=(view, me + 1), device_id_type=pl.DeviceIdType.MESH,
        )
        down = pltpu.make_async_remote_copy(
            src_ref=send_ref.at[v, 0, rows_h], dst_ref=recv_ref.at[v, 1, rows_h],
            send_sem=send_sem.at[v, 0, h], recv_sem=recv_sem.at[v, 1, h],
            device_id=(view, me - 1), device_id_type=pl.DeviceIdType.MESH,
        )
        return up, down

    def launch(v, h):
        up, down = copies(v, h)

        @pl.when(has_hi)
        def _():
            up.start()

        @pl.when(has_lo)
        def _():
            down.start()

    tb = [[taps_ref[v * 27 + 9 + t] for t in range(9)] for v in range(count)]

    def finish(v):
        for h in range(2):
            up, down = copies(v, h)

            @pl.when(has_hi)
            def _():
                up.wait_send()
                down.wait_recv()

            @pl.when(has_lo)
            def _():
                down.wait_send()
                up.wait_recv()

        def back(c, carry):
            z0 = pl.multiple_of(c * CZ, CZ)
            p0 = pl.multiple_of(c * (CZ // 2), CZ // 2)
            ext_ref[:, 0:4, :] = _unpack(recv_ref.at[v, 0], p0)[:, 0:4, :]
            ext_ref[:, 4 : 4 + width, :] = part_ref[v, pl.ds(z0, CZ)]
            ext_ref[:, 4 + width :, :] = _unpack(recv_ref.at[v, 1], p0)[:, 0:4, :]
            acc = tb[v][8] * ext_ref[:, pl.ds(0, 8), :]
            for t in range(1, 9):
                acc = acc + tb[v][8 - t] * ext_ref[:, pl.ds(t, 8), :]
            term = jnp.log(acc)
            if v == 0:
                logs_ref[pl.ds(z0, CZ)] = term
            else:
                logs_ref[pl.ds(z0, CZ)] = logs_ref[pl.ds(z0, CZ)] + term
            return carry

        lax.fori_loop(0, nz // CZ, back, 0)

    zeros = jnp.zeros((4, width, ny), jnp.float32)
    c_ref[0:4] = zeros
    c_ref[nz + 4 : nz + 8] = zeros
    tx_all = [[taps_ref[v * 27 + 9 + t] for t in range(9)] for v in range(count)]
    for v in range(count):
        a_ref[v, 0:4] = zeros
        a_ref[v, nz + 4 : nz + 8] = zeros

    def along_x(c, carry):
        z0 = pl.multiple_of(c * CZ, CZ)
        _fill_wide(ext_ref, before_ref, mid_ref, after_ref, z0)
        for sub in range(0, CZ, 8):
            accs = [None] * count
            for t in range(9):
                shifted = ext_ref[pl.ds(sub, 8), pl.ds(t, 8), :]
                for v in range(count):
                    term = tx_all[v][t] * shifted
                    accs[v] = term if accs[v] is None else accs[v] + term
            for v in range(count):
                a_ref[v, pl.ds(z0 + 4 + sub, 8)] = accs[v]
        return carry

    lax.fori_loop(0, nz // CZ, along_x, 0)
    for v in range(count):
        tz = [taps_ref[v * 27 + t] for t in range(9)]
        ty = [taps_ref[v * 27 + 18 + t] for t in range(9)]

        wy = _lane_weights(ty, ny, False)
        wy_rev = _lane_weights(ty, ny, True)

        def middle(c, carry):
            z0 = pl.multiple_of(c * CZ, CZ)
            acc = tz[0] * a_ref[v, pl.ds(z0, CZ)]
            for t in range(1, 9):
                acc = acc + tz[t] * a_ref[v, pl.ds(z0 + t, CZ)]
            blurred = _lane_correlate(acc, wy)
            ratio = brick_ref[v, pl.ds(z0, CZ)].astype(jnp.float32) / blurred
            c_ref[pl.ds(z0 + 4, CZ)] = _lane_correlate(ratio, wy_rev)
            return carry


        def along_z_back(c, carry):
            z0 = pl.multiple_of(c * CZ, CZ)
            acc = tz[8] * c_ref[pl.ds(z0, CZ)]
            for t in range(1, 9):
                acc = acc + tz[8 - t] * c_ref[pl.ds(z0 + t, CZ)]
            part_ref[v, pl.ds(z0, CZ)] = acc
            _pack(acc, send_ref.at[v, 0], send_ref.at[v, 1], pl.multiple_of(c * (CZ // 2), CZ // 2))
            return carry

        chunks = nz // CZ
        lax.fori_loop(0, chunks // 2 + 1, middle, 0)
        lax.fori_loop(0, chunks // 2, along_z_back, 0)
        launch(v, 0)
        lax.fori_loop(chunks // 2 + 1, chunks, middle, 0)
        lax.fori_loop(chunks // 2, chunks, along_z_back, 0)
        launch(v, 1)

    for v in range(count):
        finish(v)


def iteration_logs(taps_flat, before, mid, after, bricks):
    count, nz, width, ny = bricks.shape
    return pl.pallas_call(
        _iteration_kernel,
        in_specs=[pl.BlockSpec(memory_space=pltpu.SMEM)] + [pl.BlockSpec(memory_space=pltpu.VMEM)] * 4,
        out_specs=pl.BlockSpec(memory_space=pltpu.VMEM),
        out_shape=jax.ShapeDtypeStruct((nz, width, ny), jnp.float32),
        scratch_shapes=[
            pltpu.VMEM((count, nz + 8, width, ny), jnp.float32),
            pltpu.VMEM((nz + 8, width, ny), jnp.float32),
            pltpu.VMEM((CZ, width + 8, ny), jnp.float32),
            pltpu.VMEM((count, nz, width, ny), jnp.float32),
            pltpu.VMEM((count, 2, nz // 2, width, ny), jnp.float32),
            pltpu.VMEM((count, 2, nz // 2, width, ny), jnp.float32),
            pltpu.SemaphoreType.DMA((count, 2, 2)),
            pltpu.SemaphoreType.DMA((count, 2, 2)),
        ],
        compiler_params=pltpu.CompilerParams(
            collective_id=0, has_side_effects=True, vmem_limit_bytes=48 * 1024 * 1024
        ),
    )(taps_flat, before, mid, after, bricks)


def _by_core(core, mine, theirs):
    low = jnp.where(core == 0, mine, theirs)
    high = jnp.where(core == 0, theirs, mine)
    return jnp.concatenate([low, high], axis=0)


def view_sum_update(part, update, rim_width):
    count = lax.axis_size("view")
    core_swap = [(i, i ^ 1) for i in range(count)]
    chip_swap = [(i, i ^ 2) for i in range(count)]
    half = part.shape[0] // 2
    core = lax.axis_index("view") % 2
    own = lax.dynamic_slice_in_dim(part, core * half, half, axis=0)
    give = lax.dynamic_slice_in_dim(part, (1 - core) * half, half, axis=0)
    own = own + lax.ppermute(give, "view", core_swap)
    own = own + lax.ppermute(own, "view", chip_swap)
    fresh = update(own, core * half, half)
    whole = _by_core(core, fresh, lax.ppermute(fresh, "view", core_swap))
    if rim_width is None:
        return whole
    before, after = halos(fresh, "vol", 1, rim_width)
    before = _by_core(core, before, lax.ppermute(before, "view", core_swap))
    after = _by_core(core, after, lax.ppermute(after, "view", core_swap))
    return whole, before, after


def per_device(raw_views, weights, offsets, psf_taps):
    count = raw_views.shape[0]
    total_views = count * lax.axis_size("view")
    rim_width = (psf_taps.shape[2] - 1) // 2
    weight_norm = weights / jnp.sum(weights, axis=-1, keepdims=True)
    taps_norm = psf_taps / jnp.sum(psf_taps, axis=-1, keepdims=True)
    taps_flat = taps_norm.reshape(-1)
    local_views = resample_views(raw_views, weight_norm, offsets)
    bricks = lax.all_to_all(local_views, "vol", split_axis=2, concat_axis=1, tiled=True)
    local_sum = bricks[0].astype(jnp.float32)
    for index in range(1, count):
        local_sum = local_sum + bricks[index].astype(jnp.float32)
    joined_volume, before, after = view_sum_update(
        local_sum, lambda own, at, size: own / total_views, rim_width
    )
    for turn in range(ITERS):
        logs = iteration_logs(taps_flat, before, joined_volume, after, bricks)

        def update(own, at, size, previous=joined_volume):
            return lax.dynamic_slice_in_dim(previous, at, size, axis=0) * jnp.exp(own / total_views)

        result = view_sum_update(logs, update, rim_width if turn < ITERS - 1 else None)
        if turn < ITERS - 1:
            joined_volume, before, after = result
        else:
            joined_volume = result
    return joined_volume


def solution(mesh):
    placed = (
        P("view", "vol", None, None),
        P("view", None, None),
        P("view", None),
        P("view", None, None),
    )
    return jax.shard_map(
        per_device, mesh=mesh, in_specs=placed, out_specs=P(None, "vol", None), check_vma=False
    )
```

```python
import functools

import jax
import jax.numpy as jnp
from jax import lax
from jax.experimental import pallas as pl
from jax.experimental.pallas import tpu as pltpu
from jax.sharding import PartitionSpec as P

ITERS = 2
CZ = 32


def halos(shard, axis, dim, width):
    length = shard.shape[dim]
    last = lax.slice_in_dim(shard, length - width, length, axis=dim)
    first = lax.slice_in_dim(shard, 0, width, axis=dim)
    return swap_rims(first, last, axis)


def swap_rims(first, last, axis):
    devices = lax.axis_size(axis)
    up = [(i, (i + 1) % devices) for i in range(devices - 1)]
    down = [(j, i) for i, j in up]
    before = lax.ppermute(last, axis, up)
    after = lax.ppermute(first, axis, down)
    return before, after


def _fill_wide(wide_ref, before_ref, mid_ref, after_ref, z0):
    rim = before_ref.shape[1]
    width = mid_ref.shape[1]
    wide_ref[:, 0:rim, :] = before_ref[pl.ds(z0, CZ)]
    wide_ref[:, rim : rim + width, :] = mid_ref[pl.ds(z0, CZ)]
    wide_ref[:, rim + width :, :] = after_ref[pl.ds(z0, CZ)]


def resample_views(raw_views, weight_norm, offsets):
    rows = raw_views.shape[2]
    band = weight_norm.shape[2]
    lag = jnp.arange(rows, dtype=jnp.int32)[None, None, :] - offsets[:, :, None]
    matrix = jnp.zeros(lag.shape, jnp.float32)
    for k in range(band):
        matrix = matrix + jnp.where(lag == k, weight_norm[:, :, k : k + 1], 0.0)
    result = jnp.einsum(
        "vxr,vzry->vzxy",
        matrix,
        raw_views.astype(jnp.float32),
        precision=lax.Precision.HIGHEST,
        preferred_element_type=jnp.float32,
    )
    return result.astype(jnp.bfloat16)


def _lane_weights(taps, ny, reverse):
    lane = lax.broadcasted_iota(jnp.int32, (8, ny), 1)
    out = []
    for t in range(9):
        d = t - 4
        tap = taps[8 - t] if reverse else taps[t]
        valid = (lane + d >= 0) & (lane + d < ny)
        out.append(((-d) % ny, jnp.where(valid, tap, 0.0)))
    return out


def _lane_correlate(f, weights):
    acc = None
    for shift, w in weights:
        rolled = f if shift == 0 else pltpu.roll(f, shift, 2)
        term = rolled * w[None]
        acc = term if acc is None else acc + term
    return acc


def _pack(acc, first_ref, last_ref, p0):
    half = acc.shape[0] // 2
    upper, lower = acc[:half], acc[half:]
    row = lax.broadcasted_iota(jnp.int32, upper.shape, 1)
    first_ref[pl.ds(p0, half)] = jnp.where(row < 4, upper, pltpu.roll(lower, 4, 1))
    last_ref[pl.ds(p0, half)] = jnp.where(row < 4, pltpu.roll(upper, 4, 1), lower)


def _unpack(packed_ref, p0):
    packed = packed_ref[pl.ds(p0, CZ // 2)]
    return jnp.concatenate([packed, pltpu.roll(packed, 4, 1)], axis=0)


def _iteration_kernel(
    taps_ref, before_ref, mid_ref, after_ref, brick_ref, logs_ref,
    a_ref, c_ref, ext_ref, part_ref, send_ref, recv_ref, send_sem, recv_sem,
):
    count, nz, width, ny = part_ref.shape
    me = lax.axis_index("vol")
    view = lax.axis_index("view")
    has_lo = me > 0
    has_hi = me < lax.axis_size("vol") - 1
    barrier = pltpu.get_barrier_semaphore()

    @pl.when(has_lo)
    def _():
        pl.semaphore_signal(barrier, inc=1, device_id=(view, me - 1), device_id_type=pl.DeviceIdType.MESH)

    @pl.when(has_hi)
    def _():
        pl.semaphore_signal(barrier, inc=1, device_id=(view, me + 1), device_id_type=pl.DeviceIdType.MESH)

    pl.semaphore_wait(barrier, has_lo.astype(jnp.int32) + has_hi.astype(jnp.int32))

    @pl.when(jnp.logical_not(has_lo))
    def _():
        recv_ref[:, 0] = jnp.zeros(recv_ref.shape[:1] + recv_ref.shape[2:], jnp.float32)

    @pl.when(jnp.logical_not(has_hi))
    def _():
        recv_ref[:, 1] = jnp.zeros(recv_ref.shape[:1] + recv_ref.shape[2:], jnp.float32)

    pieces = 4
    rows = nz // 2 // pieces

    def copies(v, h):
        rows_h = pl.ds(h * rows, rows)
        up = pltpu.make_async_remote_copy(
            src_ref=send_ref.at[v, 1, rows_h], dst_ref=recv_ref.at[v, 0, rows_h],
            send_sem=send_sem.at[v, 1, h], recv_sem=recv_sem.at[v, 0, h],
            device_id=(view, me + 1), device_id_type=pl.DeviceIdType.MESH,
        )
        down = pltpu.make_async_remote_copy(
            src_ref=send_ref.at[v, 0, rows_h], dst_ref=recv_ref.at[v, 1, rows_h],
            send_sem=send_sem.at[v, 0, h], recv_sem=recv_sem.at[v, 1, h],
            device_id=(view, me - 1), device_id_type=pl.DeviceIdType.MESH,
        )
        return up, down

    def launch(v, h):
        up, down = copies(v, h)

        @pl.when(has_hi)
        def _():
            up.start()

        @pl.when(has_lo)
        def _():
            down.start()

    tb = [[taps_ref[v * 27 + 9 + t] for t in range(9)] for v in range(count)]

    def finish(v):
        for h in range(pieces):
            up, down = copies(v, h)

            @pl.when(has_hi)
            def _():
                up.wait_send()
                down.wait_recv()

            @pl.when(has_lo)
            def _():
                down.wait_send()
                up.wait_recv()

        def back(c, carry):
            z0 = pl.multiple_of(c * CZ, CZ)
            p0 = pl.multiple_of(c * (CZ // 2), CZ // 2)
            ext_ref[:, 0:4, :] = _unpack(recv_ref.at[v, 0], p0)[:, 0:4, :]
            ext_ref[:, 4 : 4 + width, :] = part_ref[v, pl.ds(z0, CZ)]
            ext_ref[:, 4 + width :, :] = _unpack(recv_ref.at[v, 1], p0)[:, 0:4, :]
            acc = tb[v][8] * ext_ref[:, pl.ds(0, 8), :]
            for t in range(1, 9):
                acc = acc + tb[v][8 - t] * ext_ref[:, pl.ds(t, 8), :]
            term = jnp.log(acc)
            if v == 0:
                logs_ref[pl.ds(z0, CZ)] = term
            else:
                logs_ref[pl.ds(z0, CZ)] = logs_ref[pl.ds(z0, CZ)] + term
            return carry

        lax.fori_loop(0, nz // CZ, back, 0)

    zeros = jnp.zeros((4, width, ny), jnp.float32)
    c_ref[0:4] = zeros
    c_ref[nz + 4 : nz + 8] = zeros
    tx_all = [[taps_ref[v * 27 + 9 + t] for t in range(9)] for v in range(count)]
    for v in range(count):
        a_ref[v, 0:4] = zeros
        a_ref[v, nz + 4 : nz + 8] = zeros

    def along_x(c, carry):
        z0 = pl.multiple_of(c * CZ, CZ)
        _fill_wide(ext_ref, before_ref, mid_ref, after_ref, z0)
        for sub in range(0, CZ, 8):
            accs = [None] * count
            for t in range(9):
                shifted = ext_ref[pl.ds(sub, 8), pl.ds(t, 8), :]
                for v in range(count):
                    term = tx_all[v][t] * shifted
                    accs[v] = term if accs[v] is None else accs[v] + term
            for v in range(count):
                a_ref[v, pl.ds(z0 + 4 + sub, 8)] = accs[v]
        return carry

    lax.fori_loop(0, nz // CZ, along_x, 0)
    for v in range(count):
        tz = [taps_ref[v * 27 + t] for t in range(9)]
        ty = [taps_ref[v * 27 + 18 + t] for t in range(9)]

        wy = _lane_weights(ty, ny, False)
        wy_rev = _lane_weights(ty, ny, True)

        def middle(c, carry):
            z0 = pl.multiple_of(c * CZ, CZ)
            acc = tz[0] * a_ref[v, pl.ds(z0, CZ)]
            for t in range(1, 9):
                acc = acc + tz[t] * a_ref[v, pl.ds(z0 + t, CZ)]
            blurred = _lane_correlate(acc, wy)
            ratio = brick_ref[v, pl.ds(z0, CZ)].astype(jnp.float32) / blurred
            c_ref[pl.ds(z0 + 4, CZ)] = _lane_correlate(ratio, wy_rev)
            return carry


        def along_z_back(c, carry):
            z0 = pl.multiple_of(c * CZ, CZ)
            acc = tz[8] * c_ref[pl.ds(z0, CZ)]
            for t in range(1, 9):
                acc = acc + tz[8 - t] * c_ref[pl.ds(z0 + t, CZ)]
            part_ref[v, pl.ds(z0, CZ)] = acc
            _pack(acc, send_ref.at[v, 0], send_ref.at[v, 1], pl.multiple_of(c * (CZ // 2), CZ // 2))
            return carry

        chunks = nz // CZ
        step = chunks // pieces
        for h in range(pieces):
            lax.fori_loop(0 if h == 0 else h * step + 1, min((h + 1) * step + 1, chunks), middle, 0)
            lax.fori_loop(h * step, (h + 1) * step, along_z_back, 0)
            launch(v, h)

    for v in range(count):
        finish(v)


def iteration_logs(taps_flat, before, mid, after, bricks):
    count, nz, width, ny = bricks.shape
    return pl.pallas_call(
        _iteration_kernel,
        in_specs=[pl.BlockSpec(memory_space=pltpu.SMEM)] + [pl.BlockSpec(memory_space=pltpu.VMEM)] * 4,
        out_specs=pl.BlockSpec(memory_space=pltpu.VMEM),
        out_shape=jax.ShapeDtypeStruct((nz, width, ny), jnp.float32),
        scratch_shapes=[
            pltpu.VMEM((count, nz + 8, width, ny), jnp.float32),
            pltpu.VMEM((nz + 8, width, ny), jnp.float32),
            pltpu.VMEM((CZ, width + 8, ny), jnp.float32),
            pltpu.VMEM((count, nz, width, ny), jnp.float32),
            pltpu.VMEM((count, 2, nz // 2, width, ny), jnp.float32),
            pltpu.VMEM((count, 2, nz // 2, width, ny), jnp.float32),
            pltpu.SemaphoreType.DMA((count, 2, 4)),
            pltpu.SemaphoreType.DMA((count, 2, 4)),
        ],
        compiler_params=pltpu.CompilerParams(
            collective_id=0, has_side_effects=True, vmem_limit_bytes=48 * 1024 * 1024
        ),
    )(taps_flat, before, mid, after, bricks)


def _by_core(core, mine, theirs):
    low = jnp.where(core == 0, mine, theirs)
    high = jnp.where(core == 0, theirs, mine)
    return jnp.concatenate([low, high], axis=0)


def view_sum_update(part, update, rim_width):
    count = lax.axis_size("view")
    core_swap = [(i, i ^ 1) for i in range(count)]
    chip_swap = [(i, i ^ 2) for i in range(count)]
    half = part.shape[0] // 2
    core = lax.axis_index("view") % 2
    own = lax.dynamic_slice_in_dim(part, core * half, half, axis=0)
    give = lax.dynamic_slice_in_dim(part, (1 - core) * half, half, axis=0)
    own = own + lax.ppermute(give, "view", core_swap)
    own = own + lax.ppermute(own, "view", chip_swap)
    fresh = update(own, core * half, half)
    whole = _by_core(core, fresh, lax.ppermute(fresh, "view", core_swap))
    if rim_width is None:
        return whole
    before, after = halos(fresh, "vol", 1, rim_width)
    before = _by_core(core, before, lax.ppermute(before, "view", core_swap))
    after = _by_core(core, after, lax.ppermute(after, "view", core_swap))
    return whole, before, after


def per_device(raw_views, weights, offsets, psf_taps):
    count = raw_views.shape[0]
    total_views = count * lax.axis_size("view")
    rim_width = (psf_taps.shape[2] - 1) // 2
    weight_norm = weights / jnp.sum(weights, axis=-1, keepdims=True)
    taps_norm = psf_taps / jnp.sum(psf_taps, axis=-1, keepdims=True)
    taps_flat = taps_norm.reshape(-1)
    local_views = resample_views(raw_views, weight_norm, offsets)
    bricks = lax.all_to_all(local_views, "vol", split_axis=2, concat_axis=1, tiled=True)
    local_sum = bricks[0].astype(jnp.float32)
    for index in range(1, count):
        local_sum = local_sum + bricks[index].astype(jnp.float32)
    joined_volume, before, after = view_sum_update(
        local_sum, lambda own, at, size: own / total_views, rim_width
    )
    for turn in range(ITERS):
        logs = iteration_logs(taps_flat, before, joined_volume, after, bricks)

        def update(own, at, size, previous=joined_volume):
            return lax.dynamic_slice_in_dim(previous, at, size, axis=0) * jnp.exp(own / total_views)

        result = view_sum_update(logs, update, rim_width if turn < ITERS - 1 else None)
        if turn < ITERS - 1:
            joined_volume, before, after = result
        else:
            joined_volume = result
    return joined_volume


def solution(mesh):
    placed = (
        P("view", "vol", None, None),
        P("view", None, None),
        P("view", None),
        P("view", None, None),
    )
    return jax.shard_map(
        per_device, mesh=mesh, in_specs=placed, out_specs=P(None, "vol", None), check_vma=False
    )
```

```python
import functools

import jax
import jax.numpy as jnp
from jax import lax
from jax.experimental import pallas as pl
from jax.experimental.pallas import tpu as pltpu
from jax.sharding import PartitionSpec as P

ITERS = 2
CZ = 32


def halos(shard, axis, dim, width):
    length = shard.shape[dim]
    last = lax.slice_in_dim(shard, length - width, length, axis=dim)
    first = lax.slice_in_dim(shard, 0, width, axis=dim)
    return swap_rims(first, last, axis)


def swap_rims(first, last, axis):
    devices = lax.axis_size(axis)
    up = [(i, (i + 1) % devices) for i in range(devices - 1)]
    down = [(j, i) for i, j in up]
    before = lax.ppermute(last, axis, up)
    after = lax.ppermute(first, axis, down)
    return before, after


def _fill_wide(wide_ref, before_ref, mid_ref, after_ref, z0):
    rim = before_ref.shape[1]
    width = mid_ref.shape[1]
    wide_ref[:, 0:rim, :] = before_ref[pl.ds(z0, CZ)]
    wide_ref[:, rim : rim + width, :] = mid_ref[pl.ds(z0, CZ)]
    wide_ref[:, rim + width :, :] = after_ref[pl.ds(z0, CZ)]


def resample_views(raw_views, weight_norm, offsets):
    rows = raw_views.shape[2]
    band = weight_norm.shape[2]
    lag = jnp.arange(rows, dtype=jnp.int32)[None, None, :] - offsets[:, :, None]
    matrix = jnp.zeros(lag.shape, jnp.float32)
    for k in range(band):
        matrix = matrix + jnp.where(lag == k, weight_norm[:, :, k : k + 1], 0.0)
    result = jnp.einsum(
        "vxr,vzry->vzxy",
        matrix,
        raw_views.astype(jnp.float32),
        precision=lax.Precision.HIGHEST,
        preferred_element_type=jnp.float32,
    )
    return result.astype(jnp.bfloat16)


def _lane_weights(taps, ny, reverse):
    lane = lax.broadcasted_iota(jnp.int32, (8, ny), 1)
    out = []
    for t in range(9):
        d = t - 4
        tap = taps[8 - t] if reverse else taps[t]
        valid = (lane + d >= 0) & (lane + d < ny)
        out.append(((-d) % ny, jnp.where(valid, tap, 0.0)))
    return out


def _lane_correlate(f, weights):
    acc = None
    for shift, w in weights:
        rolled = f if shift == 0 else pltpu.roll(f, shift, 2)
        term = rolled * w[None]
        acc = term if acc is None else acc + term
    return acc


def _pack(acc, first_ref, last_ref, p0):
    half = acc.shape[0] // 2
    upper, lower = acc[:half], acc[half:]
    row = lax.broadcasted_iota(jnp.int32, upper.shape, 1)
    first_ref[pl.ds(p0, half)] = jnp.where(row < 4, upper, pltpu.roll(lower, 4, 1))
    last_ref[pl.ds(p0, half)] = jnp.where(row < 4, pltpu.roll(upper, 4, 1), lower)


def _unpack(packed_ref, p0):
    packed = packed_ref[pl.ds(p0, CZ // 2)]
    return jnp.concatenate([packed, pltpu.roll(packed, 4, 1)], axis=0)


def _iteration_kernel(
    taps_ref, before_ref, mid_ref, after_ref, brick_ref, logs_ref,
    a_ref, c_ref, ext_ref, part_ref, send_ref, recv_ref, send_sem, recv_sem,
):
    count, nz, width, ny = part_ref.shape
    me = lax.axis_index("vol")
    view = lax.axis_index("view")
    has_lo = me > 0
    has_hi = me < lax.axis_size("vol") - 1
    barrier = pltpu.get_barrier_semaphore()

    @pl.when(has_lo)
    def _():
        pl.semaphore_signal(barrier, inc=1, device_id=(view, me - 1), device_id_type=pl.DeviceIdType.MESH)

    @pl.when(has_hi)
    def _():
        pl.semaphore_signal(barrier, inc=1, device_id=(view, me + 1), device_id_type=pl.DeviceIdType.MESH)

    pl.semaphore_wait(barrier, has_lo.astype(jnp.int32) + has_hi.astype(jnp.int32))

    @pl.when(jnp.logical_not(has_lo))
    def _():
        recv_ref[:, 0] = jnp.zeros(recv_ref.shape[:1] + recv_ref.shape[2:], jnp.float32)

    @pl.when(jnp.logical_not(has_hi))
    def _():
        recv_ref[:, 1] = jnp.zeros(recv_ref.shape[:1] + recv_ref.shape[2:], jnp.float32)

    pieces = 8
    rows = nz // 2 // pieces

    def copies(v, h):
        rows_h = pl.ds(h * rows, rows)
        up = pltpu.make_async_remote_copy(
            src_ref=send_ref.at[v, 1, rows_h], dst_ref=recv_ref.at[v, 0, rows_h],
            send_sem=send_sem.at[v, 1, h], recv_sem=recv_sem.at[v, 0, h],
            device_id=(view, me + 1), device_id_type=pl.DeviceIdType.MESH,
        )
        down = pltpu.make_async_remote_copy(
            src_ref=send_ref.at[v, 0, rows_h], dst_ref=recv_ref.at[v, 1, rows_h],
            send_sem=send_sem.at[v, 0, h], recv_sem=recv_sem.at[v, 1, h],
            device_id=(view, me - 1), device_id_type=pl.DeviceIdType.MESH,
        )
        return up, down

    def launch(v, h):
        up, down = copies(v, h)

        @pl.when(has_hi)
        def _():
            up.start()

        @pl.when(has_lo)
        def _():
            down.start()

    tb = [[taps_ref[v * 27 + 9 + t] for t in range(9)] for v in range(count)]

    def finish(v):
        for h in range(pieces):
            up, down = copies(v, h)

            @pl.when(has_hi)
            def _():
                up.wait_send()
                down.wait_recv()

            @pl.when(has_lo)
            def _():
                down.wait_send()
                up.wait_recv()

        def back(c, carry):
            z0 = pl.multiple_of(c * CZ, CZ)
            p0 = pl.multiple_of(c * (CZ // 2), CZ // 2)
            ext_ref[:, 0:4, :] = _unpack(recv_ref.at[v, 0], p0)[:, 0:4, :]
            ext_ref[:, 4 : 4 + width, :] = part_ref[v, pl.ds(z0, CZ)]
            ext_ref[:, 4 + width :, :] = _unpack(recv_ref.at[v, 1], p0)[:, 0:4, :]
            acc = tb[v][8] * ext_ref[:, pl.ds(0, 8), :]
            for t in range(1, 9):
                acc = acc + tb[v][8 - t] * ext_ref[:, pl.ds(t, 8), :]
            term = jnp.log(acc)
            if v == 0:
                logs_ref[pl.ds(z0, CZ)] = term
            else:
                logs_ref[pl.ds(z0, CZ)] = logs_ref[pl.ds(z0, CZ)] + term
            return carry

        lax.fori_loop(0, nz // CZ, back, 0)

    zeros = jnp.zeros((4, width, ny), jnp.float32)
    c_ref[0:4] = zeros
    c_ref[nz + 4 : nz + 8] = zeros
    tx_all = [[taps_ref[v * 27 + 9 + t] for t in range(9)] for v in range(count)]
    for v in range(count):
        a_ref[v, 0:4] = zeros
        a_ref[v, nz + 4 : nz + 8] = zeros

    def along_x(c, carry):
        z0 = pl.multiple_of(c * CZ, CZ)
        _fill_wide(ext_ref, before_ref, mid_ref, after_ref, z0)
        for sub in range(0, CZ, 8):
            accs = [None] * count
            for t in range(9):
                shifted = ext_ref[pl.ds(sub, 8), pl.ds(t, 8), :]
                for v in range(count):
                    term = tx_all[v][t] * shifted
                    accs[v] = term if accs[v] is None else accs[v] + term
            for v in range(count):
                a_ref[v, pl.ds(z0 + 4 + sub, 8)] = accs[v]
        return carry

    lax.fori_loop(0, nz // CZ, along_x, 0)
    for v in range(count):
        tz = [taps_ref[v * 27 + t] for t in range(9)]
        ty = [taps_ref[v * 27 + 18 + t] for t in range(9)]

        wy = _lane_weights(ty, ny, False)
        wy_rev = _lane_weights(ty, ny, True)

        def middle(c, carry):
            z0 = pl.multiple_of(c * CZ, CZ)
            acc = tz[0] * a_ref[v, pl.ds(z0, CZ)]
            for t in range(1, 9):
                acc = acc + tz[t] * a_ref[v, pl.ds(z0 + t, CZ)]
            blurred = _lane_correlate(acc, wy)
            ratio = brick_ref[v, pl.ds(z0, CZ)].astype(jnp.float32) / blurred
            c_ref[pl.ds(z0 + 4, CZ)] = _lane_correlate(ratio, wy_rev)
            return carry


        def along_z_back(c, carry):
            z0 = pl.multiple_of(c * CZ, CZ)
            acc = tz[8] * c_ref[pl.ds(z0, CZ)]
            for t in range(1, 9):
                acc = acc + tz[8 - t] * c_ref[pl.ds(z0 + t, CZ)]
            part_ref[v, pl.ds(z0, CZ)] = acc
            _pack(acc, send_ref.at[v, 0], send_ref.at[v, 1], pl.multiple_of(c * (CZ // 2), CZ // 2))
            return carry

        chunks = nz // CZ
        step = chunks // pieces
        for h in range(pieces):
            lax.fori_loop(0 if h == 0 else h * step + 1, min((h + 1) * step + 1, chunks), middle, 0)
            lax.fori_loop(h * step, (h + 1) * step, along_z_back, 0)
            launch(v, h)

    for v in range(count):
        finish(v)


def iteration_logs(taps_flat, before, mid, after, bricks):
    count, nz, width, ny = bricks.shape
    return pl.pallas_call(
        _iteration_kernel,
        in_specs=[pl.BlockSpec(memory_space=pltpu.SMEM)] + [pl.BlockSpec(memory_space=pltpu.VMEM)] * 4,
        out_specs=pl.BlockSpec(memory_space=pltpu.VMEM),
        out_shape=jax.ShapeDtypeStruct((nz, width, ny), jnp.float32),
        scratch_shapes=[
            pltpu.VMEM((count, nz + 8, width, ny), jnp.float32),
            pltpu.VMEM((nz + 8, width, ny), jnp.float32),
            pltpu.VMEM((CZ, width + 8, ny), jnp.float32),
            pltpu.VMEM((count, nz, width, ny), jnp.float32),
            pltpu.VMEM((count, 2, nz // 2, width, ny), jnp.float32),
            pltpu.VMEM((count, 2, nz // 2, width, ny), jnp.float32),
            pltpu.SemaphoreType.DMA((count, 2, 8)),
            pltpu.SemaphoreType.DMA((count, 2, 8)),
        ],
        compiler_params=pltpu.CompilerParams(
            collective_id=0, has_side_effects=True, vmem_limit_bytes=48 * 1024 * 1024
        ),
    )(taps_flat, before, mid, after, bricks)


def _by_core(core, mine, theirs):
    low = jnp.where(core == 0, mine, theirs)
    high = jnp.where(core == 0, theirs, mine)
    return jnp.concatenate([low, high], axis=0)


def view_sum_update(part, update, rim_width):
    count = lax.axis_size("view")
    core_swap = [(i, i ^ 1) for i in range(count)]
    chip_swap = [(i, i ^ 2) for i in range(count)]
    half = part.shape[0] // 2
    core = lax.axis_index("view") % 2
    own = lax.dynamic_slice_in_dim(part, core * half, half, axis=0)
    give = lax.dynamic_slice_in_dim(part, (1 - core) * half, half, axis=0)
    own = own + lax.ppermute(give, "view", core_swap)
    own = own + lax.ppermute(own, "view", chip_swap)
    fresh = update(own, core * half, half)
    whole = _by_core(core, fresh, lax.ppermute(fresh, "view", core_swap))
    if rim_width is None:
        return whole
    before, after = halos(fresh, "vol", 1, rim_width)
    before = _by_core(core, before, lax.ppermute(before, "view", core_swap))
    after = _by_core(core, after, lax.ppermute(after, "view", core_swap))
    return whole, before, after


def per_device(raw_views, weights, offsets, psf_taps):
    count = raw_views.shape[0]
    total_views = count * lax.axis_size("view")
    rim_width = (psf_taps.shape[2] - 1) // 2
    weight_norm = weights / jnp.sum(weights, axis=-1, keepdims=True)
    taps_norm = psf_taps / jnp.sum(psf_taps, axis=-1, keepdims=True)
    taps_flat = taps_norm.reshape(-1)
    local_views = resample_views(raw_views, weight_norm, offsets)
    bricks = lax.all_to_all(local_views, "vol", split_axis=2, concat_axis=1, tiled=True)
    local_sum = bricks[0].astype(jnp.float32)
    for index in range(1, count):
        local_sum = local_sum + bricks[index].astype(jnp.float32)
    joined_volume, before, after = view_sum_update(
        local_sum, lambda own, at, size: own / total_views, rim_width
    )
    for turn in range(ITERS):
        logs = iteration_logs(taps_flat, before, joined_volume, after, bricks)

        def update(own, at, size, previous=joined_volume):
            return lax.dynamic_slice_in_dim(previous, at, size, axis=0) * jnp.exp(own / total_views)

        result = view_sum_update(logs, update, rim_width if turn < ITERS - 1 else None)
        if turn < ITERS - 1:
            joined_volume, before, after = result
        else:
            joined_volume = result
    return joined_volume


def solution(mesh):
    placed = (
        P("view", "vol", None, None),
        P("view", None, None),
        P("view", None),
        P("view", None, None),
    )
    return jax.shard_map(
        per_device, mesh=mesh, in_specs=placed, out_specs=P(None, "vol", None), check_vma=False
    )
```

```python
import functools

import jax
import jax.numpy as jnp
from jax import lax
from jax.experimental import pallas as pl
from jax.experimental.pallas import tpu as pltpu
from jax.sharding import PartitionSpec as P

ITERS = 2
CZ = 32


def halos(shard, axis, dim, width):
    length = shard.shape[dim]
    last = lax.slice_in_dim(shard, length - width, length, axis=dim)
    first = lax.slice_in_dim(shard, 0, width, axis=dim)
    return swap_rims(first, last, axis)


def swap_rims(first, last, axis):
    devices = lax.axis_size(axis)
    up = [(i, (i + 1) % devices) for i in range(devices - 1)]
    down = [(j, i) for i, j in up]
    before = lax.ppermute(last, axis, up)
    after = lax.ppermute(first, axis, down)
    return before, after


def _fill_wide(wide_ref, before_ref, mid_ref, after_ref, z0):
    rim = before_ref.shape[1]
    width = mid_ref.shape[1]
    wide_ref[:, 0:rim, :] = before_ref[pl.ds(z0, CZ)]
    wide_ref[:, rim : rim + width, :] = mid_ref[pl.ds(z0, CZ)]
    wide_ref[:, rim + width :, :] = after_ref[pl.ds(z0, CZ)]


def resample_views(raw_views, weight_norm, offsets):
    rows = raw_views.shape[2]
    band = weight_norm.shape[2]
    lag = jnp.arange(rows, dtype=jnp.int32)[None, None, :] - offsets[:, :, None]
    matrix = jnp.zeros(lag.shape, jnp.float32)
    for k in range(band):
        matrix = matrix + jnp.where(lag == k, weight_norm[:, :, k : k + 1], 0.0)
    result = jnp.einsum(
        "vxr,vzry->vzxy",
        matrix,
        raw_views.astype(jnp.float32),
        precision=lax.Precision.HIGHEST,
        preferred_element_type=jnp.float32,
    )
    return result.astype(jnp.bfloat16)


def _lane_weights(taps, ny, reverse):
    lane = lax.broadcasted_iota(jnp.int32, (8, ny), 1)
    out = []
    for t in range(9):
        d = t - 4
        tap = taps[8 - t] if reverse else taps[t]
        valid = (lane + d >= 0) & (lane + d < ny)
        out.append(((-d) % ny, jnp.where(valid, tap, 0.0)))
    return out


def _lane_correlate(f, weights):
    acc = None
    for shift, w in weights:
        rolled = f if shift == 0 else pltpu.roll(f, shift, 2)
        term = rolled * w[None]
        acc = term if acc is None else acc + term
    return acc


def _pack(acc, first_ref, last_ref, p0):
    half = acc.shape[0] // 2
    upper, lower = acc[:half], acc[half:]
    row = lax.broadcasted_iota(jnp.int32, upper.shape, 1)
    first_ref[pl.ds(p0, half)] = jnp.where(row < 4, upper, pltpu.roll(lower, 4, 1))
    last_ref[pl.ds(p0, half)] = jnp.where(row < 4, pltpu.roll(upper, 4, 1), lower)


def _unpack(packed_ref, p0):
    packed = packed_ref[pl.ds(p0, CZ // 2)]
    return jnp.concatenate([packed, pltpu.roll(packed, 4, 1)], axis=0)


def _iteration_kernel(
    taps_ref, before_ref, mid_ref, after_ref, brick_ref, logs_ref,
    a_ref, c_ref, ext_ref, part_ref, send_ref, recv_ref, send_sem, recv_sem,
):
    count, nz, width, ny = part_ref.shape
    me = lax.axis_index("vol")
    view = lax.axis_index("view")
    has_lo = me > 0
    has_hi = me < lax.axis_size("vol") - 1
    barrier = pltpu.get_barrier_semaphore()

    @pl.when(has_lo)
    def _():
        pl.semaphore_signal(barrier, inc=1, device_id=(view, me - 1), device_id_type=pl.DeviceIdType.MESH)

    @pl.when(has_hi)
    def _():
        pl.semaphore_signal(barrier, inc=1, device_id=(view, me + 1), device_id_type=pl.DeviceIdType.MESH)

    pl.semaphore_wait(barrier, has_lo.astype(jnp.int32) + has_hi.astype(jnp.int32))

    @pl.when(jnp.logical_not(has_lo))
    def _():
        recv_ref[:, 0] = jnp.zeros(recv_ref.shape[:1] + recv_ref.shape[2:], jnp.float32)

    @pl.when(jnp.logical_not(has_hi))
    def _():
        recv_ref[:, 1] = jnp.zeros(recv_ref.shape[:1] + recv_ref.shape[2:], jnp.float32)

    pieces = 4
    rows = nz // 2 // pieces

    def copies(v, h):
        rows_h = pl.ds(h * rows, rows)
        up = pltpu.make_async_remote_copy(
            src_ref=send_ref.at[v, 1, rows_h], dst_ref=recv_ref.at[v, 0, rows_h],
            send_sem=send_sem.at[v, 1, h], recv_sem=recv_sem.at[v, 0, h],
            device_id=(view, me + 1), device_id_type=pl.DeviceIdType.MESH,
        )
        down = pltpu.make_async_remote_copy(
            src_ref=send_ref.at[v, 0, rows_h], dst_ref=recv_ref.at[v, 1, rows_h],
            send_sem=send_sem.at[v, 0, h], recv_sem=recv_sem.at[v, 1, h],
            device_id=(view, me - 1), device_id_type=pl.DeviceIdType.MESH,
        )
        return up, down

    def launch(v, h):
        up, down = copies(v, h)

        @pl.when(has_hi)
        def _():
            up.start()

        @pl.when(has_lo)
        def _():
            down.start()

    tb = [[taps_ref[v * 27 + 9 + t] for t in range(9)] for v in range(count)]

    def finish(v):
        for h in range(pieces):
            up, down = copies(v, h)

            @pl.when(has_hi)
            def _():
                up.wait_send()
                down.wait_recv()

            @pl.when(has_lo)
            def _():
                down.wait_send()
                up.wait_recv()

        def back(c, carry):
            z0 = pl.multiple_of(c * CZ, CZ)
            p0 = pl.multiple_of(c * (CZ // 2), CZ // 2)
            ext_ref[:, 0:4, :] = _unpack(recv_ref.at[v, 0], p0)[:, 0:4, :]
            ext_ref[:, 4 : 4 + width, :] = part_ref[v, pl.ds(z0, CZ)]
            ext_ref[:, 4 + width :, :] = _unpack(recv_ref.at[v, 1], p0)[:, 0:4, :]
            acc = tb[v][8] * ext_ref[:, pl.ds(0, 8), :]
            for t in range(1, 9):
                acc = acc + tb[v][8 - t] * ext_ref[:, pl.ds(t, 8), :]
            term = jnp.log(acc)
            if v == 0:
                logs_ref[pl.ds(z0, CZ)] = term
            else:
                logs_ref[pl.ds(z0, CZ)] = logs_ref[pl.ds(z0, CZ)] + term
            return carry

        lax.fori_loop(0, nz // CZ, back, 0)

    zeros = jnp.zeros((4, width, ny), jnp.float32)
    c_ref[0:4] = zeros
    c_ref[nz + 4 : nz + 8] = zeros
    tx_all = [[taps_ref[v * 27 + 9 + t] for t in range(9)] for v in range(count)]
    for v in range(count):
        a_ref[v, 0:4] = zeros
        a_ref[v, nz + 4 : nz + 8] = zeros

    def along_x(c, carry):
        z0 = pl.multiple_of(c * CZ, CZ)
        _fill_wide(ext_ref, before_ref, mid_ref, after_ref, z0)
        for sub in range(0, CZ, 8):
            accs = [None] * count
            for t in range(9):
                shifted = ext_ref[pl.ds(sub, 8), pl.ds(t, 8), :]
                for v in range(count):
                    term = tx_all[v][t] * shifted
                    accs[v] = term if accs[v] is None else accs[v] + term
            for v in range(count):
                a_ref[v, pl.ds(z0 + 4 + sub, 8)] = accs[v]
        return carry

    lax.fori_loop(0, nz // CZ, along_x, 0)
    for v in range(count):
        tz = [taps_ref[v * 27 + t] for t in range(9)]
        ty = [taps_ref[v * 27 + 18 + t] for t in range(9)]

        wy = _lane_weights(ty, ny, False)
        wy_rev = _lane_weights(ty, ny, True)

        def middle(c, carry):
            z0 = pl.multiple_of(c * CZ, CZ)
            acc = tz[0] * a_ref[v, pl.ds(z0, CZ)]
            for t in range(1, 9):
                acc = acc + tz[t] * a_ref[v, pl.ds(z0 + t, CZ)]
            blurred = _lane_correlate(acc, wy)
            ratio = brick_ref[v, pl.ds(z0, CZ)].astype(jnp.float32) / blurred
            c_ref[pl.ds(z0 + 4, CZ)] = _lane_correlate(ratio, wy_rev)
            return carry


        def along_z_back(c, carry):
            z0 = pl.multiple_of(c * CZ, CZ)
            acc = tz[8] * c_ref[pl.ds(z0, CZ)]
            for t in range(1, 9):
                acc = acc + tz[8 - t] * c_ref[pl.ds(z0 + t, CZ)]
            part_ref[v, pl.ds(z0, CZ)] = acc
            _pack(acc, send_ref.at[v, 0], send_ref.at[v, 1], pl.multiple_of(c * (CZ // 2), CZ // 2))
            return carry

        chunks = nz // CZ
        step = chunks // pieces
        for h in range(pieces):
            lax.fori_loop(0 if h == 0 else h * step + 1, min((h + 1) * step + 1, chunks), middle, 0)
            lax.fori_loop(h * step, (h + 1) * step, along_z_back, 0)
            launch(v, h)

    for v in range(count):
        finish(v)


def iteration_logs(taps_flat, before, mid, after, bricks):
    count, nz, width, ny = bricks.shape
    return pl.pallas_call(
        _iteration_kernel,
        in_specs=[pl.BlockSpec(memory_space=pltpu.SMEM)] + [pl.BlockSpec(memory_space=pltpu.VMEM)] * 4,
        out_specs=pl.BlockSpec(memory_space=pltpu.VMEM),
        out_shape=jax.ShapeDtypeStruct((nz, width, ny), jnp.float32),
        scratch_shapes=[
            pltpu.VMEM((count, nz + 8, width, ny), jnp.float32),
            pltpu.VMEM((nz + 8, width, ny), jnp.float32),
            pltpu.VMEM((CZ, width + 8, ny), jnp.float32),
            pltpu.VMEM((count, nz, width, ny), jnp.float32),
            pltpu.VMEM((count, 2, nz // 2, width, ny), jnp.float32),
            pltpu.VMEM((count, 2, nz // 2, width, ny), jnp.float32),
            pltpu.SemaphoreType.DMA((count, 2, 4)),
            pltpu.SemaphoreType.DMA((count, 2, 4)),
        ],
        compiler_params=pltpu.CompilerParams(
            collective_id=0, has_side_effects=True, vmem_limit_bytes=48 * 1024 * 1024
        ),
    )(taps_flat, before, mid, after, bricks)


def _by_core(core, mine, theirs):
    low = jnp.where(core == 0, mine, theirs)
    high = jnp.where(core == 0, theirs, mine)
    return jnp.concatenate([low, high], axis=0)


def view_sum_update(part, update, rim_width):
    count = lax.axis_size("view")
    core_swap = [(i, i ^ 1) for i in range(count)]
    chip_swap = [(i, i ^ 2) for i in range(count)]
    half = part.shape[0] // 2
    core = lax.axis_index("view") % 2
    own = lax.dynamic_slice_in_dim(part, core * half, half, axis=0)
    give = lax.dynamic_slice_in_dim(part, (1 - core) * half, half, axis=0)
    own = own + lax.ppermute(give, "view", core_swap)
    own = own + lax.ppermute(own, "view", chip_swap)
    fresh = update(own, core * half, half)
    whole = _by_core(core, fresh, lax.ppermute(fresh, "view", core_swap))
    if rim_width is None:
        return whole
    before, after = halos(fresh, "vol", 1, rim_width)
    before = _by_core(core, before, lax.ppermute(before, "view", core_swap))
    after = _by_core(core, after, lax.ppermute(after, "view", core_swap))
    return whole, before, after


def per_device(raw_views, weights, offsets, psf_taps):
    count = raw_views.shape[0]
    total_views = count * lax.axis_size("view")
    rim_width = (psf_taps.shape[2] - 1) // 2
    weight_norm = weights / jnp.sum(weights, axis=-1, keepdims=True)
    taps_norm = psf_taps / jnp.sum(psf_taps, axis=-1, keepdims=True)
    taps_flat = taps_norm.reshape(-1)
    moved = []
    for index in range(count):
        one_view = resample_views(
            raw_views[index : index + 1], weight_norm[index : index + 1], offsets[index : index + 1]
        )
        moved.append(lax.all_to_all(one_view, "vol", split_axis=2, concat_axis=1, tiled=True))
    bricks = jnp.concatenate(moved, axis=0)
    local_sum = bricks[0].astype(jnp.float32)
    for index in range(1, count):
        local_sum = local_sum + bricks[index].astype(jnp.float32)
    joined_volume, before, after = view_sum_update(
        local_sum, lambda own, at, size: own / total_views, rim_width
    )
    for turn in range(ITERS):
        logs = iteration_logs(taps_flat, before, joined_volume, after, bricks)

        def update(own, at, size, previous=joined_volume):
            return lax.dynamic_slice_in_dim(previous, at, size, axis=0) * jnp.exp(own / total_views)

        result = view_sum_update(logs, update, rim_width if turn < ITERS - 1 else None)
        if turn < ITERS - 1:
            joined_volume, before, after = result
        else:
            joined_volume = result
    return joined_volume


def solution(mesh):
    placed = (
        P("view", "vol", None, None),
        P("view", None, None),
        P("view", None),
        P("view", None, None),
    )
    return jax.shard_map(
        per_device, mesh=mesh, in_specs=placed, out_specs=P(None, "vol", None), check_vma=False
    )
```

```python
import functools

import jax
import jax.numpy as jnp
from jax import lax
from jax.experimental import pallas as pl
from jax.experimental.pallas import tpu as pltpu
from jax.sharding import PartitionSpec as P

ITERS = 2
CZ = 32
SUB = 16


def halos(shard, axis, dim, width):
    length = shard.shape[dim]
    last = lax.slice_in_dim(shard, length - width, length, axis=dim)
    first = lax.slice_in_dim(shard, 0, width, axis=dim)
    return swap_rims(first, last, axis)


def swap_rims(first, last, axis):
    devices = lax.axis_size(axis)
    up = [(i, (i + 1) % devices) for i in range(devices - 1)]
    down = [(j, i) for i, j in up]
    before = lax.ppermute(last, axis, up)
    after = lax.ppermute(first, axis, down)
    return before, after


def _fill_wide(wide_ref, before_ref, mid_ref, after_ref, z0):
    rim = before_ref.shape[1]
    width = mid_ref.shape[1]
    wide_ref[:, 0:rim, :] = before_ref[pl.ds(z0, CZ)]
    wide_ref[:, rim : rim + width, :] = mid_ref[pl.ds(z0, CZ)]
    wide_ref[:, rim + width :, :] = after_ref[pl.ds(z0, CZ)]


def resample_views(raw_views, weight_norm, offsets):
    rows = raw_views.shape[2]
    band = weight_norm.shape[2]
    lag = jnp.arange(rows, dtype=jnp.int32)[None, None, :] - offsets[:, :, None]
    matrix = jnp.zeros(lag.shape, jnp.float32)
    for k in range(band):
        matrix = matrix + jnp.where(lag == k, weight_norm[:, :, k : k + 1], 0.0)
    result = jnp.einsum(
        "vxr,vzry->vzxy",
        matrix,
        raw_views.astype(jnp.float32),
        precision=lax.Precision.HIGHEST,
        preferred_element_type=jnp.float32,
    )
    return result.astype(jnp.bfloat16)


def _lane_weights(taps, ny, reverse):
    lane = lax.broadcasted_iota(jnp.int32, (8, ny), 1)
    out = []
    for t in range(9):
        d = t - 4
        tap = taps[8 - t] if reverse else taps[t]
        valid = (lane + d >= 0) & (lane + d < ny)
        out.append(((-d) % ny, jnp.where(valid, tap, 0.0)))
    return out


def _lane_correlate(f, weights):
    acc = None
    for shift, w in weights:
        rolled = f if shift == 0 else pltpu.roll(f, shift, 2)
        term = rolled * w[None]
        acc = term if acc is None else acc + term
    return acc


def _pack(acc, first_ref, last_ref, p0):
    half = acc.shape[0] // 2
    upper, lower = acc[:half], acc[half:]
    row = lax.broadcasted_iota(jnp.int32, upper.shape, 1)
    first_ref[pl.ds(p0, half)] = jnp.where(row < 4, upper, pltpu.roll(lower, 4, 1))
    last_ref[pl.ds(p0, half)] = jnp.where(row < 4, pltpu.roll(upper, 4, 1), lower)


def _unpack(packed_ref, p0):
    packed = packed_ref[pl.ds(p0, CZ // 2)]
    return jnp.concatenate([packed, pltpu.roll(packed, 4, 1)], axis=0)


def _iteration_kernel(
    taps_ref, before_ref, mid_ref, after_ref, brick_ref, logs_ref,
    a_ref, c_ref, ext_ref, part_ref, send_ref, recv_ref, send_sem, recv_sem,
):
    count, nz, width, ny = part_ref.shape
    me = lax.axis_index("vol")
    view = lax.axis_index("view")
    has_lo = me > 0
    has_hi = me < lax.axis_size("vol") - 1
    barrier = pltpu.get_barrier_semaphore()

    @pl.when(has_lo)
    def _():
        pl.semaphore_signal(barrier, inc=1, device_id=(view, me - 1), device_id_type=pl.DeviceIdType.MESH)

    @pl.when(has_hi)
    def _():
        pl.semaphore_signal(barrier, inc=1, device_id=(view, me + 1), device_id_type=pl.DeviceIdType.MESH)

    pl.semaphore_wait(barrier, has_lo.astype(jnp.int32) + has_hi.astype(jnp.int32))

    @pl.when(jnp.logical_not(has_lo))
    def _():
        recv_ref[:, 0] = jnp.zeros(recv_ref.shape[:1] + recv_ref.shape[2:], jnp.float32)

    @pl.when(jnp.logical_not(has_hi))
    def _():
        recv_ref[:, 1] = jnp.zeros(recv_ref.shape[:1] + recv_ref.shape[2:], jnp.float32)

    pieces = 4
    rows = nz // 2 // pieces

    def copies(v, h):
        rows_h = pl.ds(h * rows, rows)
        up = pltpu.make_async_remote_copy(
            src_ref=send_ref.at[v, 1, rows_h], dst_ref=recv_ref.at[v, 0, rows_h],
            send_sem=send_sem.at[v, 1, h], recv_sem=recv_sem.at[v, 0, h],
            device_id=(view, me + 1), device_id_type=pl.DeviceIdType.MESH,
        )
        down = pltpu.make_async_remote_copy(
            src_ref=send_ref.at[v, 0, rows_h], dst_ref=recv_ref.at[v, 1, rows_h],
            send_sem=send_sem.at[v, 0, h], recv_sem=recv_sem.at[v, 1, h],
            device_id=(view, me - 1), device_id_type=pl.DeviceIdType.MESH,
        )
        return up, down

    def launch(v, h):
        up, down = copies(v, h)

        @pl.when(has_hi)
        def _():
            up.start()

        @pl.when(has_lo)
        def _():
            down.start()

    tb = [[taps_ref[v * 27 + 9 + t] for t in range(9)] for v in range(count)]

    def finish(v):
        for h in range(pieces):
            up, down = copies(v, h)

            @pl.when(has_hi)
            def _():
                up.wait_send()
                down.wait_recv()

            @pl.when(has_lo)
            def _():
                down.wait_send()
                up.wait_recv()

        def back(c, carry):
            z0 = pl.multiple_of(c * CZ, CZ)
            p0 = pl.multiple_of(c * (CZ // 2), CZ // 2)
            ext_ref[:, 0:4, :] = _unpack(recv_ref.at[v, 0], p0)[:, 0:4, :]
            ext_ref[:, 4 : 4 + width, :] = part_ref[v, pl.ds(z0, CZ)]
            ext_ref[:, 4 + width :, :] = _unpack(recv_ref.at[v, 1], p0)[:, 0:4, :]
            acc = tb[v][8] * ext_ref[:, pl.ds(0, 8), :]
            for t in range(1, 9):
                acc = acc + tb[v][8 - t] * ext_ref[:, pl.ds(t, 8), :]
            term = jnp.log(acc)
            if v == 0:
                logs_ref[pl.ds(z0, CZ)] = term
            else:
                logs_ref[pl.ds(z0, CZ)] = logs_ref[pl.ds(z0, CZ)] + term
            return carry

        lax.fori_loop(0, nz // CZ, back, 0)

    zeros = jnp.zeros((4, width, ny), jnp.float32)
    c_ref[0:4] = zeros
    c_ref[nz + 4 : nz + 8] = zeros
    tx_all = [[taps_ref[v * 27 + 9 + t] for t in range(9)] for v in range(count)]
    for v in range(count):
        a_ref[v, 0:4] = zeros
        a_ref[v, nz + 4 : nz + 8] = zeros

    def along_x(c, carry):
        z0 = pl.multiple_of(c * CZ, CZ)
        _fill_wide(ext_ref, before_ref, mid_ref, after_ref, z0)
        for sub in range(0, CZ, 8):
            accs = [None] * count
            for t in range(9):
                shifted = ext_ref[pl.ds(sub, 8), pl.ds(t, 8), :]
                for v in range(count):
                    term = tx_all[v][t] * shifted
                    accs[v] = term if accs[v] is None else accs[v] + term
            for v in range(count):
                a_ref[v, pl.ds(z0 + 4 + sub, 8)] = accs[v]
        return carry

    lax.fori_loop(0, nz // CZ, along_x, 0)
    for v in range(count):
        tz = [taps_ref[v * 27 + t] for t in range(9)]
        ty = [taps_ref[v * 27 + 18 + t] for t in range(9)]

        wy = _lane_weights(ty, ny, False)
        wy_rev = _lane_weights(ty, ny, True)

        def middle(c, carry):
            for sub in range(0, CZ, SUB):
                z0 = pl.multiple_of(c * CZ + sub, SUB)
                acc = tz[0] * a_ref[v, pl.ds(z0, SUB)]
                for t in range(1, 9):
                    acc = acc + tz[t] * a_ref[v, pl.ds(z0 + t, SUB)]
                blurred = _lane_correlate(acc, wy)
                ratio = brick_ref[v, pl.ds(z0, SUB)].astype(jnp.float32) / blurred
                c_ref[pl.ds(z0 + 4, SUB)] = _lane_correlate(ratio, wy_rev)
            return carry


        def along_z_back(c, carry):
            z0 = pl.multiple_of(c * CZ, CZ)
            acc = tz[8] * c_ref[pl.ds(z0, CZ)]
            for t in range(1, 9):
                acc = acc + tz[8 - t] * c_ref[pl.ds(z0 + t, CZ)]
            part_ref[v, pl.ds(z0, CZ)] = acc
            _pack(acc, send_ref.at[v, 0], send_ref.at[v, 1], pl.multiple_of(c * (CZ // 2), CZ // 2))
            return carry

        chunks = nz // CZ
        step = chunks // pieces
        for h in range(pieces):
            lax.fori_loop(0 if h == 0 else h * step + 1, min((h + 1) * step + 1, chunks), middle, 0)
            lax.fori_loop(h * step, (h + 1) * step, along_z_back, 0)
            launch(v, h)

    for v in range(count):
        finish(v)


def iteration_logs(taps_flat, before, mid, after, bricks):
    count, nz, width, ny = bricks.shape
    return pl.pallas_call(
        _iteration_kernel,
        in_specs=[pl.BlockSpec(memory_space=pltpu.SMEM)] + [pl.BlockSpec(memory_space=pltpu.VMEM)] * 4,
        out_specs=pl.BlockSpec(memory_space=pltpu.VMEM),
        out_shape=jax.ShapeDtypeStruct((nz, width, ny), jnp.float32),
        scratch_shapes=[
            pltpu.VMEM((count, nz + 8, width, ny), jnp.float32),
            pltpu.VMEM((nz + 8, width, ny), jnp.float32),
            pltpu.VMEM((CZ, width + 8, ny), jnp.float32),
            pltpu.VMEM((count, nz, width, ny), jnp.float32),
            pltpu.VMEM((count, 2, nz // 2, width, ny), jnp.float32),
            pltpu.VMEM((count, 2, nz // 2, width, ny), jnp.float32),
            pltpu.SemaphoreType.DMA((count, 2, 4)),
            pltpu.SemaphoreType.DMA((count, 2, 4)),
        ],
        compiler_params=pltpu.CompilerParams(
            collective_id=0, has_side_effects=True, vmem_limit_bytes=48 * 1024 * 1024
        ),
    )(taps_flat, before, mid, after, bricks)


def _by_core(core, mine, theirs):
    low = jnp.where(core == 0, mine, theirs)
    high = jnp.where(core == 0, theirs, mine)
    return jnp.concatenate([low, high], axis=0)


def view_sum_update(part, update, rim_width):
    count = lax.axis_size("view")
    core_swap = [(i, i ^ 1) for i in range(count)]
    chip_swap = [(i, i ^ 2) for i in range(count)]
    half = part.shape[0] // 2
    core = lax.axis_index("view") % 2
    own = lax.dynamic_slice_in_dim(part, core * half, half, axis=0)
    give = lax.dynamic_slice_in_dim(part, (1 - core) * half, half, axis=0)
    own = own + lax.ppermute(give, "view", core_swap)
    own = own + lax.ppermute(own, "view", chip_swap)
    fresh = update(own, core * half, half)
    whole = _by_core(core, fresh, lax.ppermute(fresh, "view", core_swap))
    if rim_width is None:
        return whole
    before, after = halos(fresh, "vol", 1, rim_width)
    before = _by_core(core, before, lax.ppermute(before, "view", core_swap))
    after = _by_core(core, after, lax.ppermute(after, "view", core_swap))
    return whole, before, after


def per_device(raw_views, weights, offsets, psf_taps):
    count = raw_views.shape[0]
    total_views = count * lax.axis_size("view")
    rim_width = (psf_taps.shape[2] - 1) // 2
    weight_norm = weights / jnp.sum(weights, axis=-1, keepdims=True)
    taps_norm = psf_taps / jnp.sum(psf_taps, axis=-1, keepdims=True)
    taps_flat = taps_norm.reshape(-1)
    local_views = resample_views(raw_views, weight_norm, offsets)
    bricks = lax.all_to_all(local_views, "vol", split_axis=2, concat_axis=1, tiled=True)
    local_sum = bricks[0].astype(jnp.float32)
    for index in range(1, count):
        local_sum = local_sum + bricks[index].astype(jnp.float32)
    joined_volume, before, after = view_sum_update(
        local_sum, lambda own, at, size: own / total_views, rim_width
    )
    for turn in range(ITERS):
        logs = iteration_logs(taps_flat, before, joined_volume, after, bricks)

        def update(own, at, size, previous=joined_volume):
            return lax.dynamic_slice_in_dim(previous, at, size, axis=0) * jnp.exp(own / total_views)

        result = view_sum_update(logs, update, rim_width if turn < ITERS - 1 else None)
        if turn < ITERS - 1:
            joined_volume, before, after = result
        else:
            joined_volume = result
    return joined_volume


def solution(mesh):
    placed = (
        P("view", "vol", None, None),
        P("view", None, None),
        P("view", None),
        P("view", None, None),
    )
    return jax.shard_map(
        per_device, mesh=mesh, in_specs=placed, out_specs=P(None, "vol", None), check_vma=False
    )
```

```python
import functools

import jax
import jax.numpy as jnp
from jax import lax
from jax.experimental import pallas as pl
from jax.experimental.pallas import tpu as pltpu
from jax.sharding import PartitionSpec as P

ITERS = 2
CZ = 32


def halos(shard, axis, dim, width):
    length = shard.shape[dim]
    last = lax.slice_in_dim(shard, length - width, length, axis=dim)
    first = lax.slice_in_dim(shard, 0, width, axis=dim)
    return swap_rims(first, last, axis)


def swap_rims(first, last, axis):
    devices = lax.axis_size(axis)
    up = [(i, (i + 1) % devices) for i in range(devices - 1)]
    down = [(j, i) for i, j in up]
    before = lax.ppermute(last, axis, up)
    after = lax.ppermute(first, axis, down)
    return before, after


def _fill_wide(wide_ref, before_ref, mid_ref, after_ref, z0):
    rim = before_ref.shape[1]
    width = mid_ref.shape[1]
    wide_ref[:, 0:rim, :] = before_ref[pl.ds(z0, CZ)]
    wide_ref[:, rim : rim + width, :] = mid_ref[pl.ds(z0, CZ)]
    wide_ref[:, rim + width :, :] = after_ref[pl.ds(z0, CZ)]


def resample_views(raw_views, weight_norm, offsets):
    rows = raw_views.shape[2]
    band = weight_norm.shape[2]
    lag = jnp.arange(rows, dtype=jnp.int32)[None, None, :] - offsets[:, :, None]
    matrix = jnp.zeros(lag.shape, jnp.float32)
    for k in range(band):
        matrix = matrix + jnp.where(lag == k, weight_norm[:, :, k : k + 1], 0.0)
    result = jnp.einsum(
        "vxr,vzry->vzxy",
        matrix,
        raw_views.astype(jnp.float32),
        precision=lax.Precision.HIGHEST,
        preferred_element_type=jnp.float32,
    )
    return result.astype(jnp.bfloat16)


def _lane_weights(taps, ny, reverse):
    lane = lax.broadcasted_iota(jnp.int32, (8, ny), 1)
    out = []
    for t in range(9):
        d = t - 4
        tap = taps[8 - t] if reverse else taps[t]
        valid = (lane + d >= 0) & (lane + d < ny)
        out.append(((-d) % ny, jnp.where(valid, tap, 0.0)))
    return out


def _lane_correlate(f, weights):
    acc = None
    for shift, w in weights:
        rolled = f if shift == 0 else pltpu.roll(f, shift, 2)
        term = rolled * w[None]
        acc = term if acc is None else acc + term
    return acc


def _pack(acc, first_ref, last_ref, p0):
    half = acc.shape[0] // 2
    upper, lower = acc[:half], acc[half:]
    row = lax.broadcasted_iota(jnp.int32, upper.shape, 1)
    first_ref[pl.ds(p0, half)] = jnp.where(row < 4, upper, pltpu.roll(lower, 4, 1))
    last_ref[pl.ds(p0, half)] = jnp.where(row < 4, pltpu.roll(upper, 4, 1), lower)


def _unpack(packed_ref, p0):
    packed = packed_ref[pl.ds(p0, CZ // 2)]
    return jnp.concatenate([packed, pltpu.roll(packed, 4, 1)], axis=0)


def _iteration_kernel(
    taps_ref, before_ref, mid_ref, after_ref, brick_ref, logs_ref,
    a_ref, c_ref, ext_ref, part_ref, send_ref, recv_ref, send_sem, recv_sem,
):
    count, nz, width, ny = part_ref.shape
    me = lax.axis_index("vol")
    view = lax.axis_index("view")
    has_lo = me > 0
    has_hi = me < lax.axis_size("vol") - 1
    barrier = pltpu.get_barrier_semaphore()

    @pl.when(has_lo)
    def _():
        pl.semaphore_signal(barrier, inc=1, device_id=(view, me - 1), device_id_type=pl.DeviceIdType.MESH)

    @pl.when(has_hi)
    def _():
        pl.semaphore_signal(barrier, inc=1, device_id=(view, me + 1), device_id_type=pl.DeviceIdType.MESH)

    pl.semaphore_wait(barrier, has_lo.astype(jnp.int32) + has_hi.astype(jnp.int32))

    @pl.when(jnp.logical_not(has_lo))
    def _():
        recv_ref[:, 0] = jnp.zeros(recv_ref.shape[:1] + recv_ref.shape[2:], jnp.float32)

    @pl.when(jnp.logical_not(has_hi))
    def _():
        recv_ref[:, 1] = jnp.zeros(recv_ref.shape[:1] + recv_ref.shape[2:], jnp.float32)

    pieces = 4
    rows = nz // 2 // pieces

    def copies(v, h):
        rows_h = pl.ds(h * rows, rows)
        up = pltpu.make_async_remote_copy(
            src_ref=send_ref.at[v, 1, rows_h], dst_ref=recv_ref.at[v, 0, rows_h],
            send_sem=send_sem.at[v, 1, h], recv_sem=recv_sem.at[v, 0, h],
            device_id=(view, me + 1), device_id_type=pl.DeviceIdType.MESH,
        )
        down = pltpu.make_async_remote_copy(
            src_ref=send_ref.at[v, 0, rows_h], dst_ref=recv_ref.at[v, 1, rows_h],
            send_sem=send_sem.at[v, 0, h], recv_sem=recv_sem.at[v, 1, h],
            device_id=(view, me - 1), device_id_type=pl.DeviceIdType.MESH,
        )
        return up, down

    def launch(v, h):
        up, down = copies(v, h)

        @pl.when(has_hi)
        def _():
            up.start()

        @pl.when(has_lo)
        def _():
            down.start()

    tb = [[taps_ref[v * 27 + 9 + t] for t in range(9)] for v in range(count)]

    def finish(v):
        for h in range(pieces):
            up, down = copies(v, h)

            @pl.when(has_hi)
            def _():
                up.wait_send()
                down.wait_recv()

            @pl.when(has_lo)
            def _():
                down.wait_send()
                up.wait_recv()

        def back(c, carry):
            z0 = pl.multiple_of(c * CZ, CZ)
            p0 = pl.multiple_of(c * (CZ // 2), CZ // 2)
            ext_ref[:, 0:4, :] = _unpack(recv_ref.at[v, 0], p0)[:, 0:4, :]
            ext_ref[:, 4 : 4 + width, :] = part_ref[v, pl.ds(z0, CZ)]
            ext_ref[:, 4 + width :, :] = _unpack(recv_ref.at[v, 1], p0)[:, 0:4, :]
            acc = tb[v][8] * ext_ref[:, pl.ds(0, 8), :]
            for t in range(1, 9):
                acc = acc + tb[v][8 - t] * ext_ref[:, pl.ds(t, 8), :]
            term = jnp.log(acc)
            if v == 0:
                logs_ref[pl.ds(z0, CZ)] = term
            else:
                logs_ref[pl.ds(z0, CZ)] = logs_ref[pl.ds(z0, CZ)] + term
            return carry

        lax.fori_loop(0, nz // CZ, back, 0)

    zeros = jnp.zeros((4, width, ny), jnp.float32)
    c_ref[0:4] = zeros
    c_ref[nz + 4 : nz + 8] = zeros
    tx_all = [[taps_ref[v * 27 + 9 + t] for t in range(9)] for v in range(count)]
    for v in range(count):
        a_ref[v, 0:4] = zeros
        a_ref[v, nz + 4 : nz + 8] = zeros

    def along_x(c, carry):
        z0 = pl.multiple_of(c * CZ, CZ)
        _fill_wide(ext_ref, before_ref, mid_ref, after_ref, z0)
        for sub in range(0, CZ, 8):
            accs = [None] * count
            for t in range(9):
                shifted = ext_ref[pl.ds(sub, 8), pl.ds(t, 8), :]
                for v in range(count):
                    term = tx_all[v][t] * shifted
                    accs[v] = term if accs[v] is None else accs[v] + term
            for v in range(count):
                a_ref[v, pl.ds(z0 + 4 + sub, 8)] = accs[v]
        return carry

    lax.fori_loop(0, nz // CZ, along_x, 0)
    for v in range(count):
        tz = [taps_ref[v * 27 + t] for t in range(9)]
        ty = [taps_ref[v * 27 + 18 + t] for t in range(9)]

        wy = _lane_weights(ty, ny, False)
        wy_rev = _lane_weights(ty, ny, True)

        def middle(c, carry):
            z0 = pl.multiple_of(c * CZ, CZ)
            acc = tz[0] * a_ref[v, pl.ds(z0, CZ)]
            for t in range(1, 9):
                acc = acc + tz[t] * a_ref[v, pl.ds(z0 + t, CZ)]
            blurred = _lane_correlate(acc, wy)
            ratio = brick_ref[v, pl.ds(z0, CZ)].astype(jnp.float32) / blurred
            c_ref[pl.ds(z0 + 4, CZ)] = _lane_correlate(ratio, wy_rev)
            return carry


        def along_z_back(c, carry):
            z0 = pl.multiple_of(c * CZ, CZ)
            acc = tz[8] * c_ref[pl.ds(z0, CZ)]
            for t in range(1, 9):
                acc = acc + tz[8 - t] * c_ref[pl.ds(z0 + t, CZ)]
            part_ref[v, pl.ds(z0, CZ)] = acc
            _pack(acc, send_ref.at[v, 0], send_ref.at[v, 1], pl.multiple_of(c * (CZ // 2), CZ // 2))
            return carry

        chunks = nz // CZ
        step = chunks // pieces
        for h in range(pieces):
            lax.fori_loop(0 if h == 0 else h * step + 1, min((h + 1) * step + 1, chunks), middle, 0)
            lax.fori_loop(h * step, (h + 1) * step, along_z_back, 0)
            launch(v, h)

    for v in range(count):
        finish(v)


def iteration_logs(taps_flat, before, mid, after, bricks):
    count, nz, width, ny = bricks.shape
    return pl.pallas_call(
        _iteration_kernel,
        in_specs=[pl.BlockSpec(memory_space=pltpu.SMEM)] + [pl.BlockSpec(memory_space=pltpu.VMEM)] * 4,
        out_specs=pl.BlockSpec(memory_space=pltpu.VMEM),
        out_shape=jax.ShapeDtypeStruct((nz, width, ny), jnp.float32),
        scratch_shapes=[
            pltpu.VMEM((count, nz + 8, width, ny), jnp.float32),
            pltpu.VMEM((nz + 8, width, ny), jnp.float32),
            pltpu.VMEM((CZ, width + 8, ny), jnp.float32),
            pltpu.VMEM((count, nz, width, ny), jnp.float32),
            pltpu.VMEM((count, 2, nz // 2, width, ny), jnp.float32),
            pltpu.VMEM((count, 2, nz // 2, width, ny), jnp.float32),
            pltpu.SemaphoreType.DMA((count, 2, 4)),
            pltpu.SemaphoreType.DMA((count, 2, 4)),
        ],
        compiler_params=pltpu.CompilerParams(
            collective_id=0, has_side_effects=True, vmem_limit_bytes=48 * 1024 * 1024
        ),
    )(taps_flat, before, mid, after, bricks)


def _by_core(core, mine, theirs):
    low = jnp.where(core == 0, mine, theirs)
    high = jnp.where(core == 0, theirs, mine)
    return jnp.concatenate([low, high], axis=0)


def view_sum_update(part, update, rim_width):
    count = lax.axis_size("view")
    core_swap = [(i, i ^ 1) for i in range(count)]
    chip_swap = [(i, i ^ 2) for i in range(count)]
    half = part.shape[0] // 2
    core = lax.axis_index("view") % 2
    own = lax.dynamic_slice_in_dim(part, core * half, half, axis=0)
    give = lax.dynamic_slice_in_dim(part, (1 - core) * half, half, axis=0)
    own = own + lax.ppermute(give, "view", core_swap)
    if rim_width is None:
        own = own + lax.ppermute(own, "view", chip_swap)
        fresh = update(own, core * half, half)
        return _by_core(core, fresh, lax.ppermute(fresh, "view", core_swap))
    splits = 2
    quarter = half // splits
    fresh_parts, before_parts, after_parts = [], [], []
    for index in range(splits):
        piece = own[index * quarter : (index + 1) * quarter]
        piece = piece + lax.ppermute(piece, "view", chip_swap)
        fresh_piece = update(piece, core * half + index * quarter, quarter)
        low, high = halos(fresh_piece, "vol", 1, rim_width)
        fresh_parts.append(fresh_piece)
        before_parts.append(low)
        after_parts.append(high)
    fresh = jnp.concatenate(fresh_parts, axis=0)
    whole = _by_core(core, fresh, lax.ppermute(fresh, "view", core_swap))
    before = jnp.concatenate(before_parts, axis=0)
    after = jnp.concatenate(after_parts, axis=0)
    before = _by_core(core, before, lax.ppermute(before, "view", core_swap))
    after = _by_core(core, after, lax.ppermute(after, "view", core_swap))
    return whole, before, after


def per_device(raw_views, weights, offsets, psf_taps):
    count = raw_views.shape[0]
    total_views = count * lax.axis_size("view")
    rim_width = (psf_taps.shape[2] - 1) // 2
    weight_norm = weights / jnp.sum(weights, axis=-1, keepdims=True)
    taps_norm = psf_taps / jnp.sum(psf_taps, axis=-1, keepdims=True)
    taps_flat = taps_norm.reshape(-1)
    local_views = resample_views(raw_views, weight_norm, offsets)
    bricks = lax.all_to_all(local_views, "vol", split_axis=2, concat_axis=1, tiled=True)
    local_sum = bricks[0].astype(jnp.float32)
    for index in range(1, count):
        local_sum = local_sum + bricks[index].astype(jnp.float32)
    joined_volume, before, after = view_sum_update(
        local_sum, lambda own, at, size: own / total_views, rim_width
    )
    for turn in range(ITERS):
        logs = iteration_logs(taps_flat, before, joined_volume, after, bricks)

        def update(own, at, size, previous=joined_volume):
            return lax.dynamic_slice_in_dim(previous, at, size, axis=0) * jnp.exp(own / total_views)

        result = view_sum_update(logs, update, rim_width if turn < ITERS - 1 else None)
        if turn < ITERS - 1:
            joined_volume, before, after = result
        else:
            joined_volume = result
    return joined_volume


def solution(mesh):
    placed = (
        P("view", "vol", None, None),
        P("view", None, None),
        P("view", None),
        P("view", None, None),
    )
    return jax.shard_map(
        per_device, mesh=mesh, in_specs=placed, out_specs=P(None, "vol", None), check_vma=False
    )
```

```python
import functools

import jax
import jax.numpy as jnp
from jax import lax
from jax.experimental import pallas as pl
from jax.experimental.pallas import tpu as pltpu
from jax.sharding import PartitionSpec as P

ITERS = 2
CZ = 32


def halos(shard, axis, dim, width):
    length = shard.shape[dim]
    last = lax.slice_in_dim(shard, length - width, length, axis=dim)
    first = lax.slice_in_dim(shard, 0, width, axis=dim)
    return swap_rims(first, last, axis)


def swap_rims(first, last, axis):
    devices = lax.axis_size(axis)
    up = [(i, (i + 1) % devices) for i in range(devices - 1)]
    down = [(j, i) for i, j in up]
    before = lax.ppermute(last, axis, up)
    after = lax.ppermute(first, axis, down)
    return before, after


def _fill_wide(wide_ref, before_ref, mid_ref, after_ref, z0):
    rim = before_ref.shape[1]
    width = mid_ref.shape[1]
    wide_ref[:, 0:rim, :] = before_ref[pl.ds(z0, CZ)]
    wide_ref[:, rim : rim + width, :] = mid_ref[pl.ds(z0, CZ)]
    wide_ref[:, rim + width :, :] = after_ref[pl.ds(z0, CZ)]


def resample_views(raw_views, band_weights, offsets):
    rows = raw_views.shape[2]
    band = band_weights.shape[2]
    lag = jnp.arange(rows, dtype=jnp.int32)[None, None, :] - offsets[:, :, None]
    matrix = jnp.zeros(lag.shape, jnp.float32)
    for k in range(band):
        matrix = matrix + jnp.where(lag == k, band_weights[:, :, k : k + 1], 0.0)
    matrix = matrix / jnp.sum(band_weights, axis=-1, keepdims=True)
    result = jnp.einsum(
        "vxr,vzry->vzxy",
        matrix,
        raw_views.astype(jnp.float32),
        precision=lax.Precision.HIGHEST,
        preferred_element_type=jnp.float32,
    )
    return result.astype(jnp.bfloat16)


def _lane_weights(taps, ny, reverse):
    lane = lax.broadcasted_iota(jnp.int32, (8, ny), 1)
    out = []
    for t in range(9):
        d = t - 4
        tap = taps[8 - t] if reverse else taps[t]
        valid = (lane + d >= 0) & (lane + d < ny)
        out.append(((-d) % ny, jnp.where(valid, tap, 0.0)))
    return out


def _lane_correlate(f, weights):
    acc = None
    for shift, w in weights:
        rolled = f if shift == 0 else pltpu.roll(f, shift, 2)
        term = rolled * w[None]
        acc = term if acc is None else acc + term
    return acc


def _pack(acc, first_ref, last_ref, p0):
    half = acc.shape[0] // 2
    upper, lower = acc[:half], acc[half:]
    row = lax.broadcasted_iota(jnp.int32, upper.shape, 1)
    first_ref[pl.ds(p0, half)] = jnp.where(row < 4, upper, pltpu.roll(lower, 4, 1))
    last_ref[pl.ds(p0, half)] = jnp.where(row < 4, pltpu.roll(upper, 4, 1), lower)


def _unpack(packed_ref, p0):
    packed = packed_ref[pl.ds(p0, CZ // 2)]
    return jnp.concatenate([packed, pltpu.roll(packed, 4, 1)], axis=0)


def _iteration_kernel(
    taps_ref, before_ref, mid_ref, after_ref, brick_ref, logs_ref,
    a_ref, c_ref, ext_ref, part_ref, send_ref, recv_ref, send_sem, recv_sem,
):
    count, nz, width, ny = part_ref.shape
    me = lax.axis_index("vol")
    view = lax.axis_index("view")
    has_lo = me > 0
    has_hi = me < lax.axis_size("vol") - 1
    barrier = pltpu.get_barrier_semaphore()

    @pl.when(has_lo)
    def _():
        pl.semaphore_signal(barrier, inc=1, device_id=(view, me - 1), device_id_type=pl.DeviceIdType.MESH)

    @pl.when(has_hi)
    def _():
        pl.semaphore_signal(barrier, inc=1, device_id=(view, me + 1), device_id_type=pl.DeviceIdType.MESH)

    pl.semaphore_wait(barrier, has_lo.astype(jnp.int32) + has_hi.astype(jnp.int32))

    @pl.when(jnp.logical_not(has_lo))
    def _():
        recv_ref[:, 0] = jnp.zeros(recv_ref.shape[:1] + recv_ref.shape[2:], jnp.float32)

    @pl.when(jnp.logical_not(has_hi))
    def _():
        recv_ref[:, 1] = jnp.zeros(recv_ref.shape[:1] + recv_ref.shape[2:], jnp.float32)

    pieces = 4
    rows = nz // 2 // pieces

    def copies(v, h):
        rows_h = pl.ds(h * rows, rows)
        up = pltpu.make_async_remote_copy(
            src_ref=send_ref.at[v, 1, rows_h], dst_ref=recv_ref.at[v, 0, rows_h],
            send_sem=send_sem.at[v, 1, h], recv_sem=recv_sem.at[v, 0, h],
            device_id=(view, me + 1), device_id_type=pl.DeviceIdType.MESH,
        )
        down = pltpu.make_async_remote_copy(
            src_ref=send_ref.at[v, 0, rows_h], dst_ref=recv_ref.at[v, 1, rows_h],
            send_sem=send_sem.at[v, 0, h], recv_sem=recv_sem.at[v, 1, h],
            device_id=(view, me - 1), device_id_type=pl.DeviceIdType.MESH,
        )
        return up, down

    def launch(v, h):
        up, down = copies(v, h)

        @pl.when(has_hi)
        def _():
            up.start()

        @pl.when(has_lo)
        def _():
            down.start()

    tb = [[taps_ref[v * 27 + 9 + t] for t in range(9)] for v in range(count)]

    def finish(v):
        for h in range(pieces):
            up, down = copies(v, h)

            @pl.when(has_hi)
            def _():
                up.wait_send()
                down.wait_recv()

            @pl.when(has_lo)
            def _():
                down.wait_send()
                up.wait_recv()

        def back(c, carry):
            z0 = pl.multiple_of(c * CZ, CZ)
            p0 = pl.multiple_of(c * (CZ // 2), CZ // 2)
            ext_ref[:, 0:4, :] = _unpack(recv_ref.at[v, 0], p0)[:, 0:4, :]
            ext_ref[:, 4 : 4 + width, :] = part_ref[v, pl.ds(z0, CZ)]
            ext_ref[:, 4 + width :, :] = _unpack(recv_ref.at[v, 1], p0)[:, 0:4, :]
            acc = tb[v][8] * ext_ref[:, pl.ds(0, 8), :]
            for t in range(1, 9):
                acc = acc + tb[v][8 - t] * ext_ref[:, pl.ds(t, 8), :]
            term = jnp.log(acc)
            if v == 0:
                logs_ref[pl.ds(z0, CZ)] = term
            else:
                logs_ref[pl.ds(z0, CZ)] = logs_ref[pl.ds(z0, CZ)] + term
            return carry

        lax.fori_loop(0, nz // CZ, back, 0)

    zeros = jnp.zeros((4, width, ny), jnp.float32)
    c_ref[0:4] = zeros
    c_ref[nz + 4 : nz + 8] = zeros
    tx_all = [[taps_ref[v * 27 + 9 + t] for t in range(9)] for v in range(count)]
    for v in range(count):
        a_ref[v, 0:4] = zeros
        a_ref[v, nz + 4 : nz + 8] = zeros

    def along_x(c, carry):
        z0 = pl.multiple_of(c * CZ, CZ)
        _fill_wide(ext_ref, before_ref, mid_ref, after_ref, z0)
        for sub in range(0, CZ, 8):
            accs = [None] * count
            for t in range(9):
                shifted = ext_ref[pl.ds(sub, 8), pl.ds(t, 8), :]
                for v in range(count):
                    term = tx_all[v][t] * shifted
                    accs[v] = term if accs[v] is None else accs[v] + term
            for v in range(count):
                a_ref[v, pl.ds(z0 + 4 + sub, 8)] = accs[v]
        return carry

    lax.fori_loop(0, nz // CZ, along_x, 0)
    for v in range(count):
        tz = [taps_ref[v * 27 + t] for t in range(9)]
        ty = [taps_ref[v * 27 + 18 + t] for t in range(9)]

        wy = _lane_weights(ty, ny, False)
        wy_rev = _lane_weights(ty, ny, True)

        def middle(c, carry):
            z0 = pl.multiple_of(c * CZ, CZ)
            acc = tz[0] * a_ref[v, pl.ds(z0, CZ)]
            for t in range(1, 9):
                acc = acc + tz[t] * a_ref[v, pl.ds(z0 + t, CZ)]
            blurred = _lane_correlate(acc, wy)
            ratio = brick_ref[v, pl.ds(z0, CZ)].astype(jnp.float32) / blurred
            c_ref[pl.ds(z0 + 4, CZ)] = _lane_correlate(ratio, wy_rev)
            return carry


        def along_z_back(c, carry):
            z0 = pl.multiple_of(c * CZ, CZ)
            acc = tz[8] * c_ref[pl.ds(z0, CZ)]
            for t in range(1, 9):
                acc = acc + tz[8 - t] * c_ref[pl.ds(z0 + t, CZ)]
            part_ref[v, pl.ds(z0, CZ)] = acc
            _pack(acc, send_ref.at[v, 0], send_ref.at[v, 1], pl.multiple_of(c * (CZ // 2), CZ // 2))
            return carry

        chunks = nz // CZ
        step = chunks // pieces
        for h in range(pieces):
            lax.fori_loop(0 if h == 0 else h * step + 1, min((h + 1) * step + 1, chunks), middle, 0)
            lax.fori_loop(h * step, (h + 1) * step, along_z_back, 0)
            launch(v, h)

    for v in range(count):
        finish(v)


def iteration_logs(taps_flat, before, mid, after, bricks):
    count, nz, width, ny = bricks.shape
    return pl.pallas_call(
        _iteration_kernel,
        in_specs=[pl.BlockSpec(memory_space=pltpu.SMEM)] + [pl.BlockSpec(memory_space=pltpu.VMEM)] * 4,
        out_specs=pl.BlockSpec(memory_space=pltpu.VMEM),
        out_shape=jax.ShapeDtypeStruct((nz, width, ny), jnp.float32),
        scratch_shapes=[
            pltpu.VMEM((count, nz + 8, width, ny), jnp.float32),
            pltpu.VMEM((nz + 8, width, ny), jnp.float32),
            pltpu.VMEM((CZ, width + 8, ny), jnp.float32),
            pltpu.VMEM((count, nz, width, ny), jnp.float32),
            pltpu.VMEM((count, 2, nz // 2, width, ny), jnp.float32),
            pltpu.VMEM((count, 2, nz // 2, width, ny), jnp.float32),
            pltpu.SemaphoreType.DMA((count, 2, 4)),
            pltpu.SemaphoreType.DMA((count, 2, 4)),
        ],
        compiler_params=pltpu.CompilerParams(
            collective_id=0, has_side_effects=True, vmem_limit_bytes=48 * 1024 * 1024
        ),
    )(taps_flat, before, mid, after, bricks)


def _by_core(core, mine, theirs):
    low = jnp.where(core == 0, mine, theirs)
    high = jnp.where(core == 0, theirs, mine)
    return jnp.concatenate([low, high], axis=0)


def view_sum_update(part, update, rim_width):
    count = lax.axis_size("view")
    core_swap = [(i, i ^ 1) for i in range(count)]
    chip_swap = [(i, i ^ 2) for i in range(count)]
    half = part.shape[0] // 2
    core = lax.axis_index("view") % 2
    own = lax.dynamic_slice_in_dim(part, core * half, half, axis=0)
    give = lax.dynamic_slice_in_dim(part, (1 - core) * half, half, axis=0)
    own = own + lax.ppermute(give, "view", core_swap)
    own = own + lax.ppermute(own, "view", chip_swap)
    fresh = update(own, core * half, half)
    whole = _by_core(core, fresh, lax.ppermute(fresh, "view", core_swap))
    if rim_width is None:
        return whole
    before, after = halos(fresh, "vol", 1, rim_width)
    before = _by_core(core, before, lax.ppermute(before, "view", core_swap))
    after = _by_core(core, after, lax.ppermute(after, "view", core_swap))
    return whole, before, after


def per_device(raw_views, weights, offsets, psf_taps):
    count = raw_views.shape[0]
    total_views = count * lax.axis_size("view")
    rim_width = (psf_taps.shape[2] - 1) // 2
    taps_norm = psf_taps / jnp.sum(psf_taps, axis=-1, keepdims=True)
    taps_flat = taps_norm.reshape(-1)
    local_views = resample_views(raw_views, weights, offsets)
    bricks = lax.all_to_all(local_views, "vol", split_axis=2, concat_axis=1, tiled=True)
    local_sum = bricks[0].astype(jnp.float32)
    for index in range(1, count):
        local_sum = local_sum + bricks[index].astype(jnp.float32)
    joined_volume, before, after = view_sum_update(
        local_sum, lambda own, at, size: own / total_views, rim_width
    )
    for turn in range(ITERS):
        logs = iteration_logs(taps_flat, before, joined_volume, after, bricks)

        def update(own, at, size, previous=joined_volume):
            return lax.dynamic_slice_in_dim(previous, at, size, axis=0) * jnp.exp(own / total_views)

        result = view_sum_update(logs, update, rim_width if turn < ITERS - 1 else None)
        if turn < ITERS - 1:
            joined_volume, before, after = result
        else:
            joined_volume = result
    return joined_volume


def solution(mesh):
    placed = (
        P("view", "vol", None, None),
        P("view", None, None),
        P("view", None),
        P("view", None, None),
    )
    return jax.shard_map(
        per_device, mesh=mesh, in_specs=placed, out_specs=P(None, "vol", None), check_vma=False
    )
```
